128 devices in a mesh: mp: 4 (over z_lo, core), fsdp: 32 (over x, z_hi, y).
Axes of the slice: x: 4, y: 4, z: 4 (z_hi: 2, z_lo: 2; z = z_hi * 2 + z_lo), core: 2. Of those that a mesh axis runs over, the one named last changes fastest.
Arguments:
- activations: bfloat16 [4, 4096, 8192], P('mp', 'fsdp'), may hold values from -6 to 6
- out_grads: bfloat16 [4, 4096, 7168], P('mp', 'fsdp'), may hold values from -0.29882812 to 0.29882812
- seq_ids: int32 [4, 4096], P('mp', 'fsdp'), may hold values from 0 to 1, as said below
- weights: bfloat16 [4, 32768, 1792], P('mp', 'fsdp'), may hold values from -6 to 6
Outputs:
- merged: bfloat16 [32768, 1792], P('fsdp')
The draws below stay inside these ranges and needn't reach their ends.
Inputs may be any that keep to these rules, and one draw needn't show every extreme that they name: `seq_ids`: sequence ids never fall along the tokens of a copy; in every copy one of the 2 sequences holds exactly 3072 neighbouring tokens and the other the remaining 4096 - 3072, in either order.
All inputs are finite; a program needn't handle non-finite values.
Results may differ from the reference program's by a relative error of at most 0.001.
Values may be sent and summed in bfloat16 or wider, within the bound.
A program may use at most 128 MiB of HBM per device.

```python
import jax
import jax.numpy as jnp
from jax import lax

D = 8192
F = 7168
FB = 4
SEQS = 2
TOKENS = 4096
MOST = 3072
COPIES = 4
N_MP = 4


def draw_seq_ids(key, part):
    order = jax.random.randint(jax.random.fold_in(key, 11), (COPIES,), 0, 2).astype(jnp.int32)
    first_len = jnp.where(order == 1, jnp.int32(MOST), jnp.int32(TOKENS - MOST)).astype(jnp.int32)
    position = jnp.arange(TOKENS, dtype=jnp.int32)
    return (position[None, :] >= first_len[:, None]).astype(jnp.int32)


def block_scale(stream_key, shape, cuts, least, largest):
    def one(dim, blocks):
        heights = jax.random.uniform(jax.random.fold_in(jax.random.fold_in(stream_key, 6), dim), (blocks,), jnp.float32, least / len(cuts), largest / len(cuts))
        return jnp.repeat(jnp.exp(heights), shape[dim] // blocks).reshape((-1,) + (1,) * (len(shape) - dim - 1))

    factor_of = one(*cuts[0])
    for cut in cuts[1:]:
        factor_of = factor_of * one(*cut)
    return factor_of


def centred(rng, shape, scale, most, cuts=(), kind=jnp.bfloat16):
    result = scale * jax.random.normal(rng, shape, jnp.float32)
    if cuts:
        result = result * block_scale(rng, shape, cuts, -0.22, 0.18)
    return jnp.clip(result, -most, most).astype(kind)


def setup_inputs(seed: int = 0) -> dict:
    keys = jax.random.split(jax.random.key(seed), 5)
    activations = centred(keys[0], (COPIES, TOKENS, D), 1.0, 6.0, ((0, 4), (1, 32)))
    out_grads = centred(keys[1], (COPIES, TOKENS, F), 0.05, 0.29882812, ((0, 4), (1, 32)))
    seq_ids = draw_seq_ids(jax.random.fold_in(keys[4], 71), 0)
    weights = centred(keys[3], (COPIES, FB * D, F // FB), 1.0, 6.0, ((0, 4), (1, 32)))
    return {"activations": activations, "out_grads": out_grads, "seq_ids": seq_ids, "weights": weights}


smoothing = 0.05


def restack(full):
    rows, cols = full.shape
    return full.reshape(rows, FB, cols // FB).transpose(1, 0, 2).reshape(FB * rows, cols // FB)


def fisher_of(acts, grads, owners):
    total = acts.shape[0]
    xs = acts.astype(jnp.float32)
    gs = grads.astype(jnp.float32)
    fisher = jnp.zeros((acts.shape[1], grads.shape[1]), jnp.float32)
    for seq in range(SEQS):
        first = jnp.sum((owners < seq).astype(jnp.int32)).astype(jnp.int32)
        first = jnp.minimum(first, jnp.int32(total - MOST)).astype(jnp.int32)
        xw = lax.dynamic_slice_in_dim(xs, first, MOST, 0)
        gw = lax.dynamic_slice_in_dim(gs, first, MOST, 0)
        iw = lax.dynamic_slice_in_dim(owners, first, MOST, 0)
        masked = jnp.where((iw == seq)[:, None], gw, jnp.zeros_like(gw))
        grad = jnp.dot(xw.T, masked, precision=lax.Precision.HIGHEST)
        fisher = fisher + grad * grad
    return fisher / SEQS


def reference(activations, out_grads, seq_ids, weights):
    numer = jnp.zeros(weights.shape[1:], jnp.float32)
    denom = jnp.zeros(weights.shape[1:], jnp.float32)
    for copy in range(N_MP):
        prior = restack(fisher_of(activations[copy], out_grads[copy], seq_ids[copy])) + smoothing
        numer = numer + prior * weights[copy].astype(jnp.float32)
        denom = denom + prior
    return (numer / denom).astype(jnp.bfloat16)
```

```python
import functools

import jax
import jax.numpy as jnp
from jax import lax
from jax.experimental import pallas as pl
from jax.experimental.pallas import tpu as pltpu
from jax.sharding import PartitionSpec as P

F = 7168
SEQS = 2
MESH = pl.DeviceIdType.MESH

smoothing = 0.05


def exchange_kernel(n, row_blocks, act_ref, grad_ref, act_out, grad_out,
                    send_a, recv_a, send_g, recv_g, local_sem):
    me = lax.axis_index("fsdp")
    tok = act_ref.shape[0]
    rw = act_out.shape[1]
    cw = grad_out.shape[1]

    barrier = pltpu.get_barrier_semaphore()

    def greet(s, c):
        k = lax.rem(me + s, n)
        pl.semaphore_signal(barrier, 1, device_id={"fsdp": k}, device_id_type=MESH)
        return c

    lax.fori_loop(1, n, greet, 0)
    pl.semaphore_wait(barrier, n - 1)

    def act_copy(src_dev, dst_dev):
        r = lax.rem(dst_dev, row_blocks)
        return pltpu.make_async_remote_copy(
            src_ref=act_ref.at[:, pl.ds(pl.multiple_of(r * rw, 128), rw)],
            dst_ref=act_out.at[pl.ds(pl.multiple_of(src_dev * tok, tok), tok), :],
            send_sem=send_a.at[dst_dev],
            recv_sem=recv_a.at[src_dev],
            device_id={"fsdp": dst_dev},
            device_id_type=MESH,
        )

    def grad_copy(src_dev, dst_dev):
        a = dst_dev // row_blocks
        return pltpu.make_async_remote_copy(
            src_ref=grad_ref.at[:, pl.ds(pl.multiple_of(a * cw, 128), cw)],
            dst_ref=grad_out.at[pl.ds(pl.multiple_of(src_dev * tok, tok), tok), :],
            send_sem=send_g.at[dst_dev],
            recv_sem=recv_g.at[src_dev],
            device_id={"fsdp": dst_dev},
            device_id_type=MESH,
        )

    r_me = lax.rem(me, row_blocks)
    a_me = me // row_blocks
    own_a = pltpu.make_async_copy(
        act_ref.at[:, pl.ds(pl.multiple_of(r_me * rw, 128), rw)],
        act_out.at[pl.ds(pl.multiple_of(me * tok, tok), tok), :],
        local_sem.at[0],
    )
    own_g = pltpu.make_async_copy(
        grad_ref.at[:, pl.ds(pl.multiple_of(a_me * cw, 128), cw)],
        grad_out.at[pl.ds(pl.multiple_of(me * tok, tok), tok), :],
        local_sem.at[1],
    )
    own_a.start()
    own_g.start()

    def send(s, c):
        k = lax.rem(me + s, n)
        grad_copy(me, k).start()
        act_copy(me, k).start()
        return c

    lax.fori_loop(1, n, send, 0)

    def finish(s, c):
        k = lax.rem(me + s, n)
        j = lax.rem(me + n - s, n)
        grad_copy(me, k).wait_send()
        act_copy(me, k).wait_send()
        grad_copy(j, me).wait_recv()
        act_copy(j, me).wait_recv()
        return c

    lax.fori_loop(1, n, finish, 0)
    own_a.wait()
    own_g.wait()


def exchange(act, grad, n, row_blocks, rw, cw):
    tok = act.shape[0]
    total = n * tok
    return pl.pallas_call(
        functools.partial(exchange_kernel, n, row_blocks),
        out_shape=(
            jax.ShapeDtypeStruct((total, rw), act.dtype),
            jax.ShapeDtypeStruct((total, cw), grad.dtype),
        ),
        in_specs=[pl.BlockSpec(memory_space=pl.ANY)] * 2,
        out_specs=(pl.BlockSpec(memory_space=pl.ANY), pl.BlockSpec(memory_space=pl.ANY)),
        scratch_shapes=[
            pltpu.SemaphoreType.DMA((n,)),
            pltpu.SemaphoreType.DMA((n,)),
            pltpu.SemaphoreType.DMA((n,)),
            pltpu.SemaphoreType.DMA((n,)),
            pltpu.SemaphoreType.DMA((2,)),
        ],
        compiler_params=pltpu.CompilerParams(collective_id=0, has_side_effects=True),
    )(act, grad)


def per_device(activations, out_grads, seq_ids, weights):
    n = lax.axis_size("fsdp")
    col_width = weights.shape[2]
    row_width = weights.shape[1]
    blocks = F // col_width
    row_blocks = n // blocks
    owners = lax.all_gather(seq_ids[0], "fsdp", axis=0, tiled=True)
    total = owners.shape[0]
    quarter = total // 4
    act_all, grad_all = exchange(activations[0], out_grads[0], n, row_blocks, row_width, col_width)

    def part(lo, hi):
        return lax.dot_general(
            act_all[lo:hi], grad_all[lo:hi], (((0,), (0,)), ((), ())),
            preferred_element_type=jnp.float32,
        )

    head = part(0, quarter)
    mid = part(quarter, 3 * quarter)
    tail = part(3 * quarter, total)
    first_long = jnp.sum((owners < 1).astype(jnp.int32)) > 2 * quarter
    g0 = jnp.where(first_long, head + mid, head)
    g1 = jnp.where(first_long, tail, mid + tail)
    fisher = g0 * g0 + g1 * g1
    prior = fisher / SEQS + smoothing
    numer = prior * weights[0].astype(jnp.float32)
    numer_q, denom_q = lax.psum_scatter((numer, prior), "mp", scatter_dimension=0, tiled=True)
    merged_q = (numer_q / denom_q).astype(jnp.bfloat16)
    return lax.all_gather(merged_q, "mp", axis=0, tiled=True)


def solution(mesh):
    placed = (P("mp", "fsdp", None), P("mp", "fsdp", None), P("mp", "fsdp"), P("mp", "fsdp", None))
    return jax.shard_map(
        per_device, mesh=mesh, in_specs=placed, out_specs=P("fsdp", None), check_vma=False
    )
```

```python
import functools

import jax
import jax.numpy as jnp
from jax import lax
from jax.experimental import pallas as pl
from jax.experimental.pallas import tpu as pltpu
from jax.sharding import PartitionSpec as P

F = 7168
SEQS = 2
MESH = pl.DeviceIdType.MESH

smoothing = 0.05


def exchange_kernel(n, row_blocks, act_ref, grad_ref, act_out, grad_out,
                    send_a, recv_a, send_g, recv_g, local_sem):
    me = lax.axis_index("fsdp")
    tok = act_ref.shape[0]
    rw = act_out.shape[1]
    cw = grad_out.shape[1]

    barrier = pltpu.get_barrier_semaphore()

    def greet(s, c):
        k = lax.rem(me + s, n)
        pl.semaphore_signal(barrier, 1, device_id={"fsdp": k}, device_id_type=MESH)
        return c

    lax.fori_loop(1, n, greet, 0)
    pl.semaphore_wait(barrier, n - 1)

    def act_copy(src_dev, dst_dev):
        r = lax.rem(dst_dev, row_blocks)
        return pltpu.make_async_remote_copy(
            src_ref=act_ref.at[:, pl.ds(pl.multiple_of(r * rw, 128), rw)],
            dst_ref=act_out.at[pl.ds(pl.multiple_of(src_dev * tok, tok), tok), :],
            send_sem=send_a.at[dst_dev],
            recv_sem=recv_a.at[src_dev],
            device_id={"fsdp": dst_dev},
            device_id_type=MESH,
        )

    def grad_copy(src_dev, dst_dev):
        a = dst_dev // row_blocks
        return pltpu.make_async_remote_copy(
            src_ref=grad_ref.at[:, pl.ds(pl.multiple_of(a * cw, 128), cw)],
            dst_ref=grad_out.at[pl.ds(pl.multiple_of(src_dev * tok, tok), tok), :],
            send_sem=send_g.at[dst_dev],
            recv_sem=recv_g.at[src_dev],
            device_id={"fsdp": dst_dev},
            device_id_type=MESH,
        )

    r_me = lax.rem(me, row_blocks)
    a_me = me // row_blocks
    own_a = pltpu.make_async_copy(
        act_ref.at[:, pl.ds(pl.multiple_of(r_me * rw, 128), rw)],
        act_out.at[pl.ds(pl.multiple_of(me * tok, tok), tok), :],
        local_sem.at[0],
    )
    own_g = pltpu.make_async_copy(
        grad_ref.at[:, pl.ds(pl.multiple_of(a_me * cw, 128), cw)],
        grad_out.at[pl.ds(pl.multiple_of(me * tok, tok), tok), :],
        local_sem.at[1],
    )
    own_a.start()
    own_g.start()

    def send(s, c):
        k = lax.rem(me + s, n)
        grad_copy(me, k).start()
        act_copy(me, k).start()
        return c

    lax.fori_loop(1, n, send, 0)

    def finish(s, c):
        k = lax.rem(me + s, n)
        j = lax.rem(me + n - s, n)
        grad_copy(me, k).wait_send()
        act_copy(me, k).wait_send()
        grad_copy(j, me).wait_recv()
        act_copy(j, me).wait_recv()
        return c

    lax.fori_loop(1, n, finish, 0)
    own_a.wait()
    own_g.wait()


def exchange(act, grad, n, row_blocks, rw, cw):
    tok = act.shape[0]
    total = n * tok
    return pl.pallas_call(
        functools.partial(exchange_kernel, n, row_blocks),
        out_shape=(
            jax.ShapeDtypeStruct((total, rw), act.dtype),
            jax.ShapeDtypeStruct((total, cw), grad.dtype),
        ),
        in_specs=[pl.BlockSpec(memory_space=pl.ANY)] * 2,
        out_specs=(pl.BlockSpec(memory_space=pl.ANY), pl.BlockSpec(memory_space=pl.ANY)),
        scratch_shapes=[
            pltpu.SemaphoreType.DMA((n,)),
            pltpu.SemaphoreType.DMA((n,)),
            pltpu.SemaphoreType.DMA((n,)),
            pltpu.SemaphoreType.DMA((n,)),
            pltpu.SemaphoreType.DMA((2,)),
        ],
        compiler_params=pltpu.CompilerParams(collective_id=0, has_side_effects=True),
    )(act, grad)


def per_device(activations, out_grads, seq_ids, weights):
    nx = lax.axis_size("x")
    nj = lax.axis_size(("zh", "y"))
    tok = activations.shape[1]
    col_width = weights.shape[2]
    row_width = weights.shape[1]
    owners = lax.all_gather(seq_ids[0], ("x", "zh", "y"), axis=0, tiled=True)
    total = owners.shape[0]
    act_blocks = activations[0].reshape(tok, nj, row_width).transpose(1, 0, 2)
    act_mine = lax.all_to_all(act_blocks, ("zh", "y"), 0, 0, tiled=True)
    act_all = lax.all_gather(act_mine.reshape(nj * tok, row_width), "x", axis=0, tiled=True)
    grad_blocks = out_grads[0].reshape(tok, nx, col_width).transpose(1, 0, 2)
    grad_mine = lax.all_to_all(grad_blocks, "x", 0, 0, tiled=True)
    grad_all = lax.all_gather(grad_mine, ("zh", "y"), axis=0, tiled=False)
    act_x = act_all.reshape(nx, nj * tok, row_width)

    def part(x):
        g = grad_all[:, x].reshape(nj * tok, col_width)
        return lax.dot_general(
            act_x[x], g, (((0,), (0,)), ((), ())), preferred_element_type=jnp.float32
        )

    head = part(0)
    mid = part(1) + part(2)
    tail = part(3)
    first_long = jnp.sum((owners < 1).astype(jnp.int32)) > total // 2
    g0 = jnp.where(first_long, head + mid, head)
    g1 = jnp.where(first_long, tail, mid + tail)
    fisher = g0 * g0 + g1 * g1
    prior = fisher / SEQS + smoothing
    numer = prior * weights[0].astype(jnp.float32)
    numer_q, denom_q = lax.psum_scatter((numer, prior), ("zl", "c"), scatter_dimension=0, tiled=True)
    merged_q = (numer_q / denom_q).astype(jnp.bfloat16)
    return lax.all_gather(merged_q, ("zl", "c"), axis=0, tiled=True)


def solution(mesh):
    assert mesh.shape["mp"] == 4 and mesh.shape["fsdp"] == 32
    fine = jax.sharding.Mesh(
        mesh.devices.reshape(2, 2, 4, 2, 4), ("zl", "c", "x", "zh", "y")
    )
    mp, fs = ("zl", "c"), ("x", "zh", "y")
    placed = (P(mp, fs, None), P(mp, fs, None), P(mp, fs), P(mp, fs, None))
    return jax.shard_map(
        per_device, mesh=fine, in_specs=placed, out_specs=P(fs, None), check_vma=False
    )
```

```python
import functools

import jax
import jax.numpy as jnp
from jax import lax
from jax.experimental import pallas as pl
from jax.experimental.pallas import tpu as pltpu
from jax.sharding import PartitionSpec as P

F = 7168
SEQS = 2
MESH = pl.DeviceIdType.MESH

smoothing = 0.05


def exchange_kernel(n, row_blocks, act_ref, grad_ref, act_out, grad_out,
                    send_a, recv_a, send_g, recv_g, local_sem):
    me = lax.axis_index("fsdp")
    tok = act_ref.shape[0]
    rw = act_out.shape[1]
    cw = grad_out.shape[1]

    barrier = pltpu.get_barrier_semaphore()

    def greet(s, c):
        k = lax.rem(me + s, n)
        pl.semaphore_signal(barrier, 1, device_id={"fsdp": k}, device_id_type=MESH)
        return c

    lax.fori_loop(1, n, greet, 0)
    pl.semaphore_wait(barrier, n - 1)

    def act_copy(src_dev, dst_dev):
        r = lax.rem(dst_dev, row_blocks)
        return pltpu.make_async_remote_copy(
            src_ref=act_ref.at[:, pl.ds(pl.multiple_of(r * rw, 128), rw)],
            dst_ref=act_out.at[pl.ds(pl.multiple_of(src_dev * tok, tok), tok), :],
            send_sem=send_a.at[dst_dev],
            recv_sem=recv_a.at[src_dev],
            device_id={"fsdp": dst_dev},
            device_id_type=MESH,
        )

    def grad_copy(src_dev, dst_dev):
        a = dst_dev // row_blocks
        return pltpu.make_async_remote_copy(
            src_ref=grad_ref.at[:, pl.ds(pl.multiple_of(a * cw, 128), cw)],
            dst_ref=grad_out.at[pl.ds(pl.multiple_of(src_dev * tok, tok), tok), :],
            send_sem=send_g.at[dst_dev],
            recv_sem=recv_g.at[src_dev],
            device_id={"fsdp": dst_dev},
            device_id_type=MESH,
        )

    r_me = lax.rem(me, row_blocks)
    a_me = me // row_blocks
    own_a = pltpu.make_async_copy(
        act_ref.at[:, pl.ds(pl.multiple_of(r_me * rw, 128), rw)],
        act_out.at[pl.ds(pl.multiple_of(me * tok, tok), tok), :],
        local_sem.at[0],
    )
    own_g = pltpu.make_async_copy(
        grad_ref.at[:, pl.ds(pl.multiple_of(a_me * cw, 128), cw)],
        grad_out.at[pl.ds(pl.multiple_of(me * tok, tok), tok), :],
        local_sem.at[1],
    )
    own_a.start()
    own_g.start()

    def send(s, c):
        k = lax.rem(me + s, n)
        grad_copy(me, k).start()
        act_copy(me, k).start()
        return c

    lax.fori_loop(1, n, send, 0)

    def finish(s, c):
        k = lax.rem(me + s, n)
        j = lax.rem(me + n - s, n)
        grad_copy(me, k).wait_send()
        act_copy(me, k).wait_send()
        grad_copy(j, me).wait_recv()
        act_copy(j, me).wait_recv()
        return c

    lax.fori_loop(1, n, finish, 0)
    own_a.wait()
    own_g.wait()


def exchange(act, grad, n, row_blocks, rw, cw):
    tok = act.shape[0]
    total = n * tok
    return pl.pallas_call(
        functools.partial(exchange_kernel, n, row_blocks),
        out_shape=(
            jax.ShapeDtypeStruct((total, rw), act.dtype),
            jax.ShapeDtypeStruct((total, cw), grad.dtype),
        ),
        in_specs=[pl.BlockSpec(memory_space=pl.ANY)] * 2,
        out_specs=(pl.BlockSpec(memory_space=pl.ANY), pl.BlockSpec(memory_space=pl.ANY)),
        scratch_shapes=[
            pltpu.SemaphoreType.DMA((n,)),
            pltpu.SemaphoreType.DMA((n,)),
            pltpu.SemaphoreType.DMA((n,)),
            pltpu.SemaphoreType.DMA((n,)),
            pltpu.SemaphoreType.DMA((2,)),
        ],
        compiler_params=pltpu.CompilerParams(collective_id=0, has_side_effects=True),
    )(act, grad)


def per_device(activations, out_grads, seq_ids, weights):
    nx = lax.axis_size("x")
    nj = lax.axis_size(("zh", "y"))
    tok = activations.shape[1]
    col_width = weights.shape[2]
    row_width = weights.shape[1]
    owners = lax.all_gather(seq_ids[0], ("x", "zh", "y"), axis=0, tiled=True)
    total = owners.shape[0]
    act_blocks = activations[0].reshape(tok, nj, row_width).transpose(1, 0, 2)
    act_mine = lax.all_to_all(act_blocks, ("zh", "y"), 0, 0, tiled=True)
    act_all = lax.all_gather(act_mine.reshape(nj * tok, row_width), "x", axis=0, tiled=True)
    grad_blocks = out_grads[0].reshape(tok, nx, col_width).transpose(1, 0, 2)
    grad_mine = lax.all_to_all(grad_blocks, "x", 0, 0, tiled=True)
    grad_all = lax.all_gather(grad_mine, ("zh", "y"), axis=0, tiled=False)
    act_x = act_all.reshape(nx, nj * tok, row_width)

    def part(x):
        g = grad_all[:, x].reshape(nj * tok, col_width)
        return lax.dot_general(
            act_x[x], g, (((0,), (0,)), ((), ())), preferred_element_type=jnp.float32
        )

    head = part(0)
    mid = part(1) + part(2)
    tail = part(3)
    first_long = jnp.sum((owners < 1).astype(jnp.int32)) > total // 2
    g0 = jnp.where(first_long, head + mid, head)
    g1 = jnp.where(first_long, tail, mid + tail)
    fisher = g0 * g0 + g1 * g1
    prior = fisher / SEQS + smoothing
    numer = prior * weights[0].astype(jnp.float32)
    both = jnp.stack([numer, prior], axis=0)
    both = lax.psum_scatter(both, "c", scatter_dimension=1, tiled=True)
    both = lax.psum_scatter(both, "zl", scatter_dimension=1, tiled=True)
    merged_q = (both[0] / both[1]).astype(jnp.bfloat16)
    merged_h = lax.all_gather(merged_q, "zl", axis=0, tiled=True)
    return lax.all_gather(merged_h, "c", axis=0, tiled=True)


def solution(mesh):
    assert mesh.shape["mp"] == 4 and mesh.shape["fsdp"] == 32
    fine = jax.sharding.Mesh(
        mesh.devices.reshape(2, 2, 4, 2, 4), ("zl", "c", "x", "zh", "y")
    )
    mp, fs = ("zl", "c"), ("x", "zh", "y")
    placed = (P(mp, fs, None), P(mp, fs, None), P(mp, fs), P(mp, fs, None))
    return jax.shard_map(
        per_device, mesh=fine, in_specs=placed, out_specs=P(fs, None), check_vma=False
    )
```

```python
import functools

import jax
import jax.numpy as jnp
from jax import lax
from jax.experimental import pallas as pl
from jax.experimental.pallas import tpu as pltpu
from jax.sharding import PartitionSpec as P

F = 7168
SEQS = 2
MESH = pl.DeviceIdType.MESH

smoothing = 0.05


def exchange_kernel(n, row_blocks, act_ref, grad_ref, act_out, grad_out,
                    send_a, recv_a, send_g, recv_g, local_sem):
    me = lax.axis_index("fsdp")
    tok = act_ref.shape[0]
    rw = act_out.shape[1]
    cw = grad_out.shape[1]

    barrier = pltpu.get_barrier_semaphore()

    def greet(s, c):
        k = lax.rem(me + s, n)
        pl.semaphore_signal(barrier, 1, device_id={"fsdp": k}, device_id_type=MESH)
        return c

    lax.fori_loop(1, n, greet, 0)
    pl.semaphore_wait(barrier, n - 1)

    def act_copy(src_dev, dst_dev):
        r = lax.rem(dst_dev, row_blocks)
        return pltpu.make_async_remote_copy(
            src_ref=act_ref.at[:, pl.ds(pl.multiple_of(r * rw, 128), rw)],
            dst_ref=act_out.at[pl.ds(pl.multiple_of(src_dev * tok, tok), tok), :],
            send_sem=send_a.at[dst_dev],
            recv_sem=recv_a.at[src_dev],
            device_id={"fsdp": dst_dev},
            device_id_type=MESH,
        )

    def grad_copy(src_dev, dst_dev):
        a = dst_dev // row_blocks
        return pltpu.make_async_remote_copy(
            src_ref=grad_ref.at[:, pl.ds(pl.multiple_of(a * cw, 128), cw)],
            dst_ref=grad_out.at[pl.ds(pl.multiple_of(src_dev * tok, tok), tok), :],
            send_sem=send_g.at[dst_dev],
            recv_sem=recv_g.at[src_dev],
            device_id={"fsdp": dst_dev},
            device_id_type=MESH,
        )

    r_me = lax.rem(me, row_blocks)
    a_me = me // row_blocks
    own_a = pltpu.make_async_copy(
        act_ref.at[:, pl.ds(pl.multiple_of(r_me * rw, 128), rw)],
        act_out.at[pl.ds(pl.multiple_of(me * tok, tok), tok), :],
        local_sem.at[0],
    )
    own_g = pltpu.make_async_copy(
        grad_ref.at[:, pl.ds(pl.multiple_of(a_me * cw, 128), cw)],
        grad_out.at[pl.ds(pl.multiple_of(me * tok, tok), tok), :],
        local_sem.at[1],
    )
    own_a.start()
    own_g.start()

    def send(s, c):
        k = lax.rem(me + s, n)
        grad_copy(me, k).start()
        act_copy(me, k).start()
        return c

    lax.fori_loop(1, n, send, 0)

    def finish(s, c):
        k = lax.rem(me + s, n)
        j = lax.rem(me + n - s, n)
        grad_copy(me, k).wait_send()
        act_copy(me, k).wait_send()
        grad_copy(j, me).wait_recv()
        act_copy(j, me).wait_recv()
        return c

    lax.fori_loop(1, n, finish, 0)
    own_a.wait()
    own_g.wait()


def exchange(act, grad, n, row_blocks, rw, cw):
    tok = act.shape[0]
    total = n * tok
    return pl.pallas_call(
        functools.partial(exchange_kernel, n, row_blocks),
        out_shape=(
            jax.ShapeDtypeStruct((total, rw), act.dtype),
            jax.ShapeDtypeStruct((total, cw), grad.dtype),
        ),
        in_specs=[pl.BlockSpec(memory_space=pl.ANY)] * 2,
        out_specs=(pl.BlockSpec(memory_space=pl.ANY), pl.BlockSpec(memory_space=pl.ANY)),
        scratch_shapes=[
            pltpu.SemaphoreType.DMA((n,)),
            pltpu.SemaphoreType.DMA((n,)),
            pltpu.SemaphoreType.DMA((n,)),
            pltpu.SemaphoreType.DMA((n,)),
            pltpu.SemaphoreType.DMA((2,)),
        ],
        compiler_params=pltpu.CompilerParams(collective_id=0, has_side_effects=True),
    )(act, grad)


def xgather_kernel(act_ref, act_out, send_sem, recv_sem, local_sem):
    n = lax.axis_size("x")
    me = lax.axis_index("x")
    right, left = lax.rem(me + 1, n), lax.rem(me + n - 1, n)
    far = lax.rem(me + 2, n)
    rows = act_ref.shape[0]
    half = rows // 2

    barrier = pltpu.get_barrier_semaphore()
    for nb in (left, right):
        pl.semaphore_signal(barrier, 1, device_id={"x": nb}, device_id_type=MESH)
    pl.semaphore_wait(barrier, 2)

    own = pltpu.make_async_copy(act_ref, act_out.at[me], local_sem.at[0])
    own.start()
    to_right = pltpu.make_async_remote_copy(
        src_ref=act_ref, dst_ref=act_out.at[me], send_sem=send_sem.at[0],
        recv_sem=recv_sem.at[0], device_id={"x": right}, device_id_type=MESH)
    to_left = pltpu.make_async_remote_copy(
        src_ref=act_ref, dst_ref=act_out.at[me], send_sem=send_sem.at[1],
        recv_sem=recv_sem.at[1], device_id={"x": left}, device_id_type=MESH)
    to_right.start()
    to_left.start()
    from_left = pltpu.make_async_remote_copy(
        src_ref=act_ref, dst_ref=act_out.at[left], send_sem=send_sem.at[0],
        recv_sem=recv_sem.at[0], device_id={"x": left}, device_id_type=MESH)
    from_right = pltpu.make_async_remote_copy(
        src_ref=act_ref, dst_ref=act_out.at[right], send_sem=send_sem.at[1],
        recv_sem=recv_sem.at[1], device_id={"x": right}, device_id_type=MESH)
    from_left.wait_recv()
    from_right.wait_recv()
    relay_left = pltpu.make_async_remote_copy(
        src_ref=act_out.at[right, pl.ds(0, half)], dst_ref=act_out.at[right, pl.ds(0, half)],
        send_sem=send_sem.at[2], recv_sem=recv_sem.at[2], device_id={"x": left},
        device_id_type=MESH)
    relay_right = pltpu.make_async_remote_copy(
        src_ref=act_out.at[left, pl.ds(half, half)], dst_ref=act_out.at[left, pl.ds(half, half)],
        send_sem=send_sem.at[3], recv_sem=recv_sem.at[3], device_id={"x": right},
        device_id_type=MESH)
    relay_left.start()
    relay_right.start()
    far_first = pltpu.make_async_remote_copy(
        src_ref=act_out.at[far, pl.ds(0, half)], dst_ref=act_out.at[far, pl.ds(0, half)],
        send_sem=send_sem.at[2], recv_sem=recv_sem.at[2], device_id={"x": right},
        device_id_type=MESH)
    far_second = pltpu.make_async_remote_copy(
        src_ref=act_out.at[far, pl.ds(half, half)], dst_ref=act_out.at[far, pl.ds(half, half)],
        send_sem=send_sem.at[3], recv_sem=recv_sem.at[3], device_id={"x": left},
        device_id_type=MESH)
    far_first.wait_recv()
    far_second.wait_recv()
    to_right.wait_send()
    to_left.wait_send()
    relay_left.wait_send()
    relay_right.wait_send()
    own.wait()


def xgather(act):
    n = 4
    rows, cols = act.shape
    return pl.pallas_call(
        xgather_kernel,
        out_shape=jax.ShapeDtypeStruct((n, rows, cols), act.dtype),
        in_specs=[pl.BlockSpec(memory_space=pl.ANY)],
        out_specs=pl.BlockSpec(memory_space=pl.ANY),
        scratch_shapes=[
            pltpu.SemaphoreType.DMA((4,)),
            pltpu.SemaphoreType.DMA((4,)),
            pltpu.SemaphoreType.DMA((1,)),
        ],
        compiler_params=pltpu.CompilerParams(collective_id=1, has_side_effects=True),
        cost_estimate=pl.CostEstimate(flops=0, bytes_accessed=8 * rows * cols * 2, transcendentals=0),
    )(act)


def per_device(activations, out_grads, seq_ids, weights):
    nx = lax.axis_size("x")
    nj = lax.axis_size(("zh", "y"))
    tok = activations.shape[1]
    col_width = weights.shape[2]
    row_width = weights.shape[1]
    owners = lax.all_gather(seq_ids[0], ("x", "zh", "y"), axis=0, tiled=True)
    total = owners.shape[0]
    act_blocks = activations[0].reshape(tok, nj, row_width).transpose(1, 0, 2)
    act_mine = lax.all_to_all(act_blocks, ("zh", "y"), 0, 0, tiled=True)
    act_all = xgather(act_mine.reshape(nj * tok, row_width))
    grad_blocks = out_grads[0].reshape(tok, nx, col_width).transpose(1, 0, 2)
    grad_mine = lax.all_to_all(grad_blocks, "x", 0, 0, tiled=True)
    grad_all = lax.all_gather(grad_mine, ("zh", "y"), axis=0, tiled=False)
    act_x = act_all

    def part(x):
        g = grad_all[:, x].reshape(nj * tok, col_width)
        return lax.dot_general(
            act_x[x], g, (((0,), (0,)), ((), ())), preferred_element_type=jnp.float32
        )

    head = part(0)
    mid = part(1) + part(2)
    tail = part(3)
    first_long = jnp.sum((owners < 1).astype(jnp.int32)) > total // 2
    g0 = jnp.where(first_long, head + mid, head)
    g1 = jnp.where(first_long, tail, mid + tail)
    fisher = g0 * g0 + g1 * g1
    prior = fisher / SEQS + smoothing
    numer = prior * weights[0].astype(jnp.float32)
    both = jnp.stack([numer, prior], axis=0)
    both = lax.psum_scatter(both, "c", scatter_dimension=1, tiled=True)
    both = lax.psum_scatter(both, "zl", scatter_dimension=1, tiled=True)
    merged_q = (both[0] / both[1]).astype(jnp.bfloat16)
    merged_h = lax.all_gather(merged_q, "zl", axis=0, tiled=True)
    return lax.all_gather(merged_h, "c", axis=0, tiled=True)


def solution(mesh):
    assert mesh.shape["mp"] == 4 and mesh.shape["fsdp"] == 32
    fine = jax.sharding.Mesh(
        mesh.devices.reshape(2, 2, 4, 2, 4), ("zl", "c", "x", "zh", "y")
    )
    mp, fs = ("zl", "c"), ("x", "zh", "y")
    placed = (P(mp, fs, None), P(mp, fs, None), P(mp, fs), P(mp, fs, None))
    return jax.shard_map(
        per_device, mesh=fine, in_specs=placed, out_specs=P(fs, None), check_vma=False
    )
```

```python
import functools

import jax
import jax.numpy as jnp
from jax import lax
from jax.experimental import pallas as pl
from jax.experimental.pallas import tpu as pltpu
from jax.sharding import PartitionSpec as P

F = 7168
SEQS = 2
MESH = pl.DeviceIdType.MESH

smoothing = 0.05


def exchange_kernel(n, row_blocks, act_ref, grad_ref, act_out, grad_out,
                    send_a, recv_a, send_g, recv_g, local_sem):
    me = lax.axis_index("fsdp")
    tok = act_ref.shape[0]
    rw = act_out.shape[1]
    cw = grad_out.shape[1]

    barrier = pltpu.get_barrier_semaphore()

    def greet(s, c):
        k = lax.rem(me + s, n)
        pl.semaphore_signal(barrier, 1, device_id={"fsdp": k}, device_id_type=MESH)
        return c

    lax.fori_loop(1, n, greet, 0)
    pl.semaphore_wait(barrier, n - 1)

    def act_copy(src_dev, dst_dev):
        r = lax.rem(dst_dev, row_blocks)
        return pltpu.make_async_remote_copy(
            src_ref=act_ref.at[:, pl.ds(pl.multiple_of(r * rw, 128), rw)],
            dst_ref=act_out.at[pl.ds(pl.multiple_of(src_dev * tok, tok), tok), :],
            send_sem=send_a.at[dst_dev],
            recv_sem=recv_a.at[src_dev],
            device_id={"fsdp": dst_dev},
            device_id_type=MESH,
        )

    def grad_copy(src_dev, dst_dev):
        a = dst_dev // row_blocks
        return pltpu.make_async_remote_copy(
            src_ref=grad_ref.at[:, pl.ds(pl.multiple_of(a * cw, 128), cw)],
            dst_ref=grad_out.at[pl.ds(pl.multiple_of(src_dev * tok, tok), tok), :],
            send_sem=send_g.at[dst_dev],
            recv_sem=recv_g.at[src_dev],
            device_id={"fsdp": dst_dev},
            device_id_type=MESH,
        )

    r_me = lax.rem(me, row_blocks)
    a_me = me // row_blocks
    own_a = pltpu.make_async_copy(
        act_ref.at[:, pl.ds(pl.multiple_of(r_me * rw, 128), rw)],
        act_out.at[pl.ds(pl.multiple_of(me * tok, tok), tok), :],
        local_sem.at[0],
    )
    own_g = pltpu.make_async_copy(
        grad_ref.at[:, pl.ds(pl.multiple_of(a_me * cw, 128), cw)],
        grad_out.at[pl.ds(pl.multiple_of(me * tok, tok), tok), :],
        local_sem.at[1],
    )
    own_a.start()
    own_g.start()

    def send(s, c):
        k = lax.rem(me + s, n)
        grad_copy(me, k).start()
        act_copy(me, k).start()
        return c

    lax.fori_loop(1, n, send, 0)

    def finish(s, c):
        k = lax.rem(me + s, n)
        j = lax.rem(me + n - s, n)
        grad_copy(me, k).wait_send()
        act_copy(me, k).wait_send()
        grad_copy(j, me).wait_recv()
        act_copy(j, me).wait_recv()
        return c

    lax.fori_loop(1, n, finish, 0)
    own_a.wait()
    own_g.wait()


def exchange(act, grad, n, row_blocks, rw, cw):
    tok = act.shape[0]
    total = n * tok
    return pl.pallas_call(
        functools.partial(exchange_kernel, n, row_blocks),
        out_shape=(
            jax.ShapeDtypeStruct((total, rw), act.dtype),
            jax.ShapeDtypeStruct((total, cw), grad.dtype),
        ),
        in_specs=[pl.BlockSpec(memory_space=pl.ANY)] * 2,
        out_specs=(pl.BlockSpec(memory_space=pl.ANY), pl.BlockSpec(memory_space=pl.ANY)),
        scratch_shapes=[
            pltpu.SemaphoreType.DMA((n,)),
            pltpu.SemaphoreType.DMA((n,)),
            pltpu.SemaphoreType.DMA((n,)),
            pltpu.SemaphoreType.DMA((n,)),
            pltpu.SemaphoreType.DMA((2,)),
        ],
        compiler_params=pltpu.CompilerParams(collective_id=0, has_side_effects=True),
    )(act, grad)


def xgather_kernel(act_ref, seq_ref, act_out, seq_out, send_sem, recv_sem, local_sem,
                   seq_send, seq_recv):
    n = lax.axis_size("x")
    me = lax.axis_index("x")
    right, left = lax.rem(me + 1, n), lax.rem(me + n - 1, n)
    far = lax.rem(me + 2, n)
    rows = act_ref.shape[0]
    half = rows // 2

    barrier = pltpu.get_barrier_semaphore()
    for nb in (left, right):
        pl.semaphore_signal(barrier, 1, device_id={"x": nb}, device_id_type=MESH)
    pl.semaphore_wait(barrier, 2)

    own = pltpu.make_async_copy(act_ref, act_out.at[me], local_sem.at[0])
    own.start()
    own_seq = pltpu.make_async_copy(seq_ref, seq_out.at[me], local_sem.at[1])
    own_seq.start()

    def seq_copy(src, dst, slot, dev):
        return pltpu.make_async_remote_copy(
            src_ref=src, dst_ref=dst, send_sem=seq_send.at[slot], recv_sem=seq_recv.at[slot],
            device_id={"x": dev}, device_id_type=MESH)

    seq_r = seq_copy(seq_ref, seq_out.at[me], 0, right)
    seq_l = seq_copy(seq_ref, seq_out.at[me], 1, left)
    seq_r.start()
    seq_l.start()
    to_right = pltpu.make_async_remote_copy(
        src_ref=act_ref, dst_ref=act_out.at[me], send_sem=send_sem.at[0],
        recv_sem=recv_sem.at[0], device_id={"x": right}, device_id_type=MESH)
    to_left = pltpu.make_async_remote_copy(
        src_ref=act_ref, dst_ref=act_out.at[me], send_sem=send_sem.at[1],
        recv_sem=recv_sem.at[1], device_id={"x": left}, device_id_type=MESH)
    to_right.start()
    to_left.start()
    from_left = pltpu.make_async_remote_copy(
        src_ref=act_ref, dst_ref=act_out.at[left], send_sem=send_sem.at[0],
        recv_sem=recv_sem.at[0], device_id={"x": left}, device_id_type=MESH)
    from_right = pltpu.make_async_remote_copy(
        src_ref=act_ref, dst_ref=act_out.at[right], send_sem=send_sem.at[1],
        recv_sem=recv_sem.at[1], device_id={"x": right}, device_id_type=MESH)
    from_left.wait_recv()
    from_right.wait_recv()
    seq_copy(seq_ref, seq_out.at[left], 0, left).wait_recv()
    seq_copy(seq_ref, seq_out.at[right], 1, right).wait_recv()
    seq_relay = seq_copy(seq_out.at[right], seq_out.at[right], 2, left)
    seq_relay.start()
    relay_left = pltpu.make_async_remote_copy(
        src_ref=act_out.at[right, pl.ds(0, half)], dst_ref=act_out.at[right, pl.ds(0, half)],
        send_sem=send_sem.at[2], recv_sem=recv_sem.at[2], device_id={"x": left},
        device_id_type=MESH)
    relay_right = pltpu.make_async_remote_copy(
        src_ref=act_out.at[left, pl.ds(half, half)], dst_ref=act_out.at[left, pl.ds(half, half)],
        send_sem=send_sem.at[3], recv_sem=recv_sem.at[3], device_id={"x": right},
        device_id_type=MESH)
    relay_left.start()
    relay_right.start()
    far_first = pltpu.make_async_remote_copy(
        src_ref=act_out.at[far, pl.ds(0, half)], dst_ref=act_out.at[far, pl.ds(0, half)],
        send_sem=send_sem.at[2], recv_sem=recv_sem.at[2], device_id={"x": right},
        device_id_type=MESH)
    far_second = pltpu.make_async_remote_copy(
        src_ref=act_out.at[far, pl.ds(half, half)], dst_ref=act_out.at[far, pl.ds(half, half)],
        send_sem=send_sem.at[3], recv_sem=recv_sem.at[3], device_id={"x": left},
        device_id_type=MESH)
    far_first.wait_recv()
    far_second.wait_recv()
    seq_copy(seq_out.at[far], seq_out.at[far], 2, right).wait_recv()
    seq_r.wait_send()
    seq_l.wait_send()
    seq_relay.wait_send()
    own_seq.wait()
    to_right.wait_send()
    to_left.wait_send()
    relay_left.wait_send()
    relay_right.wait_send()
    own.wait()


def xgather(act, seq):
    n = 4
    rows, cols = act.shape
    return pl.pallas_call(
        xgather_kernel,
        out_shape=(
            jax.ShapeDtypeStruct((n, rows, cols), act.dtype),
            jax.ShapeDtypeStruct((n,) + seq.shape, seq.dtype),
        ),
        in_specs=[pl.BlockSpec(memory_space=pl.ANY)] * 2,
        out_specs=(pl.BlockSpec(memory_space=pl.ANY), pl.BlockSpec(memory_space=pl.ANY)),
        scratch_shapes=[
            pltpu.SemaphoreType.DMA((4,)),
            pltpu.SemaphoreType.DMA((4,)),
            pltpu.SemaphoreType.DMA((2,)),
            pltpu.SemaphoreType.DMA((3,)),
            pltpu.SemaphoreType.DMA((3,)),
        ],
        compiler_params=pltpu.CompilerParams(collective_id=1, has_side_effects=True),
        cost_estimate=pl.CostEstimate(flops=0, bytes_accessed=8 * rows * cols * 2, transcendentals=0),
    )(act, seq)


def per_device(activations, out_grads, seq_ids, weights):
    nx = lax.axis_size("x")
    nj = lax.axis_size(("zh", "y"))
    tok = activations.shape[1]
    col_width = weights.shape[2]
    row_width = weights.shape[1]
    total = nx * nj * tok
    act_blocks = activations[0].reshape(tok, nj, row_width).transpose(1, 0, 2)
    act_mine = lax.all_to_all(act_blocks, ("zh", "y"), 0, 0, tiled=True)
    act_all, owners = xgather(act_mine.reshape(nj * tok, row_width), seq_ids)
    grad_blocks = out_grads[0].reshape(tok, nx, col_width).transpose(1, 0, 2)
    grad_mine = lax.all_to_all(grad_blocks, "x", 0, 0, tiled=True)
    grad_all = lax.all_gather(grad_mine, ("zh", "y"), axis=0, tiled=False)
    act_x = act_all

    def part(x):
        g = grad_all[:, x].reshape(nj * tok, col_width)
        return lax.dot_general(
            act_x[x], g, (((0,), (0,)), ((), ())), preferred_element_type=jnp.float32
        )

    head = part(0)
    mid = part(1) + part(2)
    tail = part(3)
    first_long = jnp.sum((owners < 1).astype(jnp.int32)) * (total // owners.size) > total // 2
    g0 = jnp.where(first_long, head + mid, head)
    g1 = jnp.where(first_long, tail, mid + tail)
    fisher = g0 * g0 + g1 * g1
    prior = fisher / SEQS + smoothing
    w = weights[0].astype(jnp.float32)
    both = prior[None] * jnp.stack([w, jnp.ones_like(w)], axis=0)
    both = lax.psum_scatter(both, "c", scatter_dimension=1, tiled=True)
    both = lax.psum_scatter(both, "zl", scatter_dimension=1, tiled=True)
    merged_q = (both[0] / both[1]).astype(jnp.bfloat16)
    merged_h = lax.all_gather(merged_q, "zl", axis=0, tiled=True)
    return lax.all_gather(merged_h, "c", axis=0, tiled=True)


def solution(mesh):
    assert mesh.shape["mp"] == 4 and mesh.shape["fsdp"] == 32
    fine = jax.sharding.Mesh(
        mesh.devices.reshape(2, 2, 4, 2, 4), ("zl", "c", "x", "zh", "y")
    )
    mp, fs = ("zl", "c"), ("x", "zh", "y")
    placed = (P(mp, fs, None), P(mp, fs, None), P(mp, fs), P(mp, fs, None))
    return jax.shard_map(
        per_device, mesh=fine, in_specs=placed, out_specs=P(fs, None), check_vma=False
    )
```

```python
import functools

import jax
import jax.numpy as jnp
from jax import lax
from jax.experimental import pallas as pl
from jax.experimental.pallas import tpu as pltpu
from jax.sharding import PartitionSpec as P

F = 7168
SEQS = 2
MESH = pl.DeviceIdType.MESH

smoothing = 0.05


def exchange_kernel(n, row_blocks, act_ref, grad_ref, act_out, grad_out,
                    send_a, recv_a, send_g, recv_g, local_sem):
    me = lax.axis_index("fsdp")
    tok = act_ref.shape[0]
    rw = act_out.shape[1]
    cw = grad_out.shape[1]

    barrier = pltpu.get_barrier_semaphore()

    def greet(s, c):
        k = lax.rem(me + s, n)
        pl.semaphore_signal(barrier, 1, device_id={"fsdp": k}, device_id_type=MESH)
        return c

    lax.fori_loop(1, n, greet, 0)
    pl.semaphore_wait(barrier, n - 1)

    def act_copy(src_dev, dst_dev):
        r = lax.rem(dst_dev, row_blocks)
        return pltpu.make_async_remote_copy(
            src_ref=act_ref.at[:, pl.ds(pl.multiple_of(r * rw, 128), rw)],
            dst_ref=act_out.at[pl.ds(pl.multiple_of(src_dev * tok, tok), tok), :],
            send_sem=send_a.at[dst_dev],
            recv_sem=recv_a.at[src_dev],
            device_id={"fsdp": dst_dev},
            device_id_type=MESH,
        )

    def grad_copy(src_dev, dst_dev):
        a = dst_dev // row_blocks
        return pltpu.make_async_remote_copy(
            src_ref=grad_ref.at[:, pl.ds(pl.multiple_of(a * cw, 128), cw)],
            dst_ref=grad_out.at[pl.ds(pl.multiple_of(src_dev * tok, tok), tok), :],
            send_sem=send_g.at[dst_dev],
            recv_sem=recv_g.at[src_dev],
            device_id={"fsdp": dst_dev},
            device_id_type=MESH,
        )

    r_me = lax.rem(me, row_blocks)
    a_me = me // row_blocks
    own_a = pltpu.make_async_copy(
        act_ref.at[:, pl.ds(pl.multiple_of(r_me * rw, 128), rw)],
        act_out.at[pl.ds(pl.multiple_of(me * tok, tok), tok), :],
        local_sem.at[0],
    )
    own_g = pltpu.make_async_copy(
        grad_ref.at[:, pl.ds(pl.multiple_of(a_me * cw, 128), cw)],
        grad_out.at[pl.ds(pl.multiple_of(me * tok, tok), tok), :],
        local_sem.at[1],
    )
    own_a.start()
    own_g.start()

    def send(s, c):
        k = lax.rem(me + s, n)
        grad_copy(me, k).start()
        act_copy(me, k).start()
        return c

    lax.fori_loop(1, n, send, 0)

    def finish(s, c):
        k = lax.rem(me + s, n)
        j = lax.rem(me + n - s, n)
        grad_copy(me, k).wait_send()
        act_copy(me, k).wait_send()
        grad_copy(j, me).wait_recv()
        act_copy(j, me).wait_recv()
        return c

    lax.fori_loop(1, n, finish, 0)
    own_a.wait()
    own_g.wait()


def exchange(act, grad, n, row_blocks, rw, cw):
    tok = act.shape[0]
    total = n * tok
    return pl.pallas_call(
        functools.partial(exchange_kernel, n, row_blocks),
        out_shape=(
            jax.ShapeDtypeStruct((total, rw), act.dtype),
            jax.ShapeDtypeStruct((total, cw), grad.dtype),
        ),
        in_specs=[pl.BlockSpec(memory_space=pl.ANY)] * 2,
        out_specs=(pl.BlockSpec(memory_space=pl.ANY), pl.BlockSpec(memory_space=pl.ANY)),
        scratch_shapes=[
            pltpu.SemaphoreType.DMA((n,)),
            pltpu.SemaphoreType.DMA((n,)),
            pltpu.SemaphoreType.DMA((n,)),
            pltpu.SemaphoreType.DMA((n,)),
            pltpu.SemaphoreType.DMA((2,)),
        ],
        compiler_params=pltpu.CompilerParams(collective_id=0, has_side_effects=True),
    )(act, grad)


def xgather_kernel(act_ref, seq_ref, act_out, seq_out, send_sem, recv_sem, local_sem,
                   seq_send, seq_recv):
    n = lax.axis_size("x")
    me = lax.axis_index("x")
    right, left = lax.rem(me + 1, n), lax.rem(me + n - 1, n)
    far = lax.rem(me + 2, n)
    rows = act_ref.shape[0]
    half = rows // 2

    barrier = pltpu.get_barrier_semaphore()
    for nb in (left, right):
        pl.semaphore_signal(barrier, 1, device_id={"x": nb}, device_id_type=MESH)
    pl.semaphore_wait(barrier, 2)

    own = pltpu.make_async_copy(act_ref, act_out.at[me], local_sem.at[0])
    own.start()
    own_seq = pltpu.make_async_copy(seq_ref, seq_out.at[me], local_sem.at[1])
    own_seq.start()

    def seq_copy(src, dst, slot, dev):
        return pltpu.make_async_remote_copy(
            src_ref=src, dst_ref=dst, send_sem=seq_send.at[slot], recv_sem=seq_recv.at[slot],
            device_id={"x": dev}, device_id_type=MESH)

    seq_r = seq_copy(seq_ref, seq_out.at[me], 0, right)
    seq_l = seq_copy(seq_ref, seq_out.at[me], 1, left)
    seq_r.start()
    seq_l.start()
    to_right = pltpu.make_async_remote_copy(
        src_ref=act_ref, dst_ref=act_out.at[me], send_sem=send_sem.at[0],
        recv_sem=recv_sem.at[0], device_id={"x": right}, device_id_type=MESH)
    to_left = pltpu.make_async_remote_copy(
        src_ref=act_ref, dst_ref=act_out.at[me], send_sem=send_sem.at[1],
        recv_sem=recv_sem.at[1], device_id={"x": left}, device_id_type=MESH)
    to_right.start()
    to_left.start()
    from_left = pltpu.make_async_remote_copy(
        src_ref=act_ref, dst_ref=act_out.at[left], send_sem=send_sem.at[0],
        recv_sem=recv_sem.at[0], device_id={"x": left}, device_id_type=MESH)
    from_right = pltpu.make_async_remote_copy(
        src_ref=act_ref, dst_ref=act_out.at[right], send_sem=send_sem.at[1],
        recv_sem=recv_sem.at[1], device_id={"x": right}, device_id_type=MESH)
    from_left.wait_recv()
    from_right.wait_recv()
    seq_copy(seq_ref, seq_out.at[left], 0, left).wait_recv()
    seq_copy(seq_ref, seq_out.at[right], 1, right).wait_recv()
    seq_relay = seq_copy(seq_out.at[right], seq_out.at[right], 2, left)
    seq_relay.start()
    relay_left = pltpu.make_async_remote_copy(
        src_ref=act_out.at[right, pl.ds(0, half)], dst_ref=act_out.at[right, pl.ds(0, half)],
        send_sem=send_sem.at[2], recv_sem=recv_sem.at[2], device_id={"x": left},
        device_id_type=MESH)
    relay_right = pltpu.make_async_remote_copy(
        src_ref=act_out.at[left, pl.ds(half, half)], dst_ref=act_out.at[left, pl.ds(half, half)],
        send_sem=send_sem.at[3], recv_sem=recv_sem.at[3], device_id={"x": right},
        device_id_type=MESH)
    relay_left.start()
    relay_right.start()
    far_first = pltpu.make_async_remote_copy(
        src_ref=act_out.at[far, pl.ds(0, half)], dst_ref=act_out.at[far, pl.ds(0, half)],
        send_sem=send_sem.at[2], recv_sem=recv_sem.at[2], device_id={"x": right},
        device_id_type=MESH)
    far_second = pltpu.make_async_remote_copy(
        src_ref=act_out.at[far, pl.ds(half, half)], dst_ref=act_out.at[far, pl.ds(half, half)],
        send_sem=send_sem.at[3], recv_sem=recv_sem.at[3], device_id={"x": left},
        device_id_type=MESH)
    far_first.wait_recv()
    far_second.wait_recv()
    seq_copy(seq_out.at[far], seq_out.at[far], 2, right).wait_recv()
    seq_r.wait_send()
    seq_l.wait_send()
    seq_relay.wait_send()
    own_seq.wait()
    to_right.wait_send()
    to_left.wait_send()
    relay_left.wait_send()
    relay_right.wait_send()
    own.wait()


def xgather(act, seq):
    n = 4
    rows, cols = act.shape
    return pl.pallas_call(
        xgather_kernel,
        out_shape=(
            jax.ShapeDtypeStruct((n, rows, cols), act.dtype),
            jax.ShapeDtypeStruct((n,) + seq.shape, seq.dtype),
        ),
        in_specs=[pl.BlockSpec(memory_space=pl.ANY)] * 2,
        out_specs=(pl.BlockSpec(memory_space=pl.ANY), pl.BlockSpec(memory_space=pl.ANY)),
        scratch_shapes=[
            pltpu.SemaphoreType.DMA((4,)),
            pltpu.SemaphoreType.DMA((4,)),
            pltpu.SemaphoreType.DMA((2,)),
            pltpu.SemaphoreType.DMA((3,)),
            pltpu.SemaphoreType.DMA((3,)),
        ],
        compiler_params=pltpu.CompilerParams(collective_id=1, has_side_effects=True),
        cost_estimate=pl.CostEstimate(flops=0, bytes_accessed=8 * rows * cols * 2, transcendentals=0),
    )(act, seq)


def mp_merge_kernel(both_ref, out_ref, recv1, recv2, send_sem, recv_sem):
    c = lax.axis_index("c")
    z = lax.axis_index("zl")
    rows = both_ref.shape[1]
    half, quarter = rows // 2, rows // 4
    step = 32
    core = {"c": 1 - c}
    chip = {"zl": 1 - z}

    barrier = pltpu.get_barrier_semaphore()
    pl.semaphore_signal(barrier, 1, device_id=core, device_id_type=MESH)
    pl.semaphore_signal(barrier, 1, device_id=chip, device_id_type=MESH)
    pl.semaphore_wait(barrier, 2)

    mine = pl.multiple_of(c * half, half)
    other = pl.multiple_of((1 - c) * half, half)
    first = pltpu.make_async_remote_copy(
        src_ref=both_ref.at[:, pl.ds(other, half)], dst_ref=recv1,
        send_sem=send_sem.at[0], recv_sem=recv_sem.at[0], device_id=core, device_id_type=MESH)
    first.start()
    first.wait_recv()

    def add_half(i, carry):
        r = pl.multiple_of(i * step, step)
        recv1[:, pl.ds(r, step)] = recv1[:, pl.ds(r, step)] + both_ref[:, pl.ds(mine + r, step)]
        return carry

    lax.fori_loop(0, half // step, add_half, 0)

    my_q = pl.multiple_of(z * quarter, quarter)
    far_q = pl.multiple_of((1 - z) * quarter, quarter)
    second = pltpu.make_async_remote_copy(
        src_ref=recv1.at[:, pl.ds(far_q, quarter)], dst_ref=recv2,
        send_sem=send_sem.at[1], recv_sem=recv_sem.at[1], device_id=chip, device_id_type=MESH)
    second.start()
    second.wait_recv()

    def merge(i, carry):
        r = pl.multiple_of(i * step, step)
        n = recv1[0, pl.ds(my_q + r, step)] + recv2[0, pl.ds(r, step)]
        d = recv1[1, pl.ds(my_q + r, step)] + recv2[1, pl.ds(r, step)]
        out_ref[pl.ds(mine + my_q + r, step)] = (n / d).astype(out_ref.dtype)
        return carry

    lax.fori_loop(0, quarter // step, merge, 0)

    third = pltpu.make_async_remote_copy(
        src_ref=out_ref.at[pl.ds(mine + my_q, quarter)], dst_ref=out_ref.at[pl.ds(mine + my_q, quarter)],
        send_sem=send_sem.at[2], recv_sem=recv_sem.at[2], device_id=chip, device_id_type=MESH)
    third.start()
    pltpu.make_async_remote_copy(
        src_ref=out_ref.at[pl.ds(mine + far_q, quarter)], dst_ref=out_ref.at[pl.ds(mine + far_q, quarter)],
        send_sem=send_sem.at[2], recv_sem=recv_sem.at[2], device_id=chip, device_id_type=MESH).wait_recv()
    fourth = pltpu.make_async_remote_copy(
        src_ref=out_ref.at[pl.ds(mine, half)], dst_ref=out_ref.at[pl.ds(mine, half)],
        send_sem=send_sem.at[3], recv_sem=recv_sem.at[3], device_id=core, device_id_type=MESH)
    fourth.start()
    pltpu.make_async_remote_copy(
        src_ref=out_ref.at[pl.ds(other, half)], dst_ref=out_ref.at[pl.ds(other, half)],
        send_sem=send_sem.at[3], recv_sem=recv_sem.at[3], device_id=core, device_id_type=MESH).wait_recv()
    first.wait_send()
    second.wait_send()
    third.wait_send()
    fourth.wait_send()


def mp_merge(both):
    _, rows, cols = both.shape
    vmem = pltpu.MemorySpace.VMEM
    return pl.pallas_call(
        mp_merge_kernel,
        out_shape=jax.ShapeDtypeStruct((rows, cols), jnp.bfloat16),
        in_specs=[pl.BlockSpec(memory_space=vmem)],
        out_specs=pl.BlockSpec(memory_space=vmem),
        scratch_shapes=[
            pltpu.VMEM((2, rows // 2, cols), jnp.float32),
            pltpu.VMEM((2, rows // 4, cols), jnp.float32),
            pltpu.SemaphoreType.DMA((4,)),
            pltpu.SemaphoreType.DMA((4,)),
        ],
        compiler_params=pltpu.CompilerParams(
            collective_id=2, has_side_effects=True, vmem_limit_bytes=60 * 1024 * 1024),
        cost_estimate=pl.CostEstimate(flops=rows * cols * 4, bytes_accessed=rows * cols * 16, transcendentals=0),
    )(both)


def per_device(activations, out_grads, seq_ids, weights):
    nx = lax.axis_size("x")
    nj = lax.axis_size(("zh", "y"))
    tok = activations.shape[1]
    col_width = weights.shape[2]
    row_width = weights.shape[1]
    total = nx * nj * tok
    act_blocks = activations[0].reshape(tok, nj, row_width).transpose(1, 0, 2)
    act_mine = lax.all_to_all(act_blocks, ("zh", "y"), 0, 0, tiled=True)
    act_all, owners = xgather(act_mine.reshape(nj * tok, row_width), seq_ids)
    grad_blocks = out_grads[0].reshape(tok, nx, col_width).transpose(1, 0, 2)
    grad_mine = lax.all_to_all(grad_blocks, "x", 0, 0, tiled=True)
    grad_all = lax.all_gather(grad_mine, ("zh", "y"), axis=0, tiled=False)
    act_x = act_all

    def part(x):
        g = grad_all[:, x].reshape(nj * tok, col_width)
        return lax.dot_general(
            act_x[x], g, (((0,), (0,)), ((), ())), preferred_element_type=jnp.float32
        )

    head = part(0)
    mid = part(1) + part(2)
    tail = part(3)
    first_long = jnp.sum((owners < 1).astype(jnp.int32)) * (total // owners.size) > total // 2
    g0 = jnp.where(first_long, head + mid, head)
    g1 = jnp.where(first_long, tail, mid + tail)
    fisher = g0 * g0 + g1 * g1
    prior = fisher / SEQS + smoothing
    w = weights[0].astype(jnp.float32)
    both = prior[None] * jnp.stack([w, jnp.ones_like(w)], axis=0)
    return mp_merge(both)


def solution(mesh):
    assert mesh.shape["mp"] == 4 and mesh.shape["fsdp"] == 32
    fine = jax.sharding.Mesh(
        mesh.devices.reshape(2, 2, 4, 2, 4), ("zl", "c", "x", "zh", "y")
    )
    mp, fs = ("zl", "c"), ("x", "zh", "y")
    placed = (P(mp, fs, None), P(mp, fs, None), P(mp, fs), P(mp, fs, None))
    return jax.shard_map(
        per_device, mesh=fine, in_specs=placed, out_specs=P(fs, None), check_vma=False
    )
```

```python
import functools

import jax
import jax.numpy as jnp
from jax import lax
from jax.experimental import pallas as pl
from jax.experimental.pallas import tpu as pltpu
from jax.sharding import PartitionSpec as P

F = 7168
SEQS = 2
MESH = pl.DeviceIdType.MESH

smoothing = 0.05


def exchange_kernel(n, row_blocks, act_ref, grad_ref, act_out, grad_out,
                    send_a, recv_a, send_g, recv_g, local_sem):
    me = lax.axis_index("fsdp")
    tok = act_ref.shape[0]
    rw = act_out.shape[1]
    cw = grad_out.shape[1]

    barrier = pltpu.get_barrier_semaphore()

    def greet(s, c):
        k = lax.rem(me + s, n)
        pl.semaphore_signal(barrier, 1, device_id={"fsdp": k}, device_id_type=MESH)
        return c

    lax.fori_loop(1, n, greet, 0)
    pl.semaphore_wait(barrier, n - 1)

    def act_copy(src_dev, dst_dev):
        r = lax.rem(dst_dev, row_blocks)
        return pltpu.make_async_remote_copy(
            src_ref=act_ref.at[:, pl.ds(pl.multiple_of(r * rw, 128), rw)],
            dst_ref=act_out.at[pl.ds(pl.multiple_of(src_dev * tok, tok), tok), :],
            send_sem=send_a.at[dst_dev],
            recv_sem=recv_a.at[src_dev],
            device_id={"fsdp": dst_dev},
            device_id_type=MESH,
        )

    def grad_copy(src_dev, dst_dev):
        a = dst_dev // row_blocks
        return pltpu.make_async_remote_copy(
            src_ref=grad_ref.at[:, pl.ds(pl.multiple_of(a * cw, 128), cw)],
            dst_ref=grad_out.at[pl.ds(pl.multiple_of(src_dev * tok, tok), tok), :],
            send_sem=send_g.at[dst_dev],
            recv_sem=recv_g.at[src_dev],
            device_id={"fsdp": dst_dev},
            device_id_type=MESH,
        )

    r_me = lax.rem(me, row_blocks)
    a_me = me // row_blocks
    own_a = pltpu.make_async_copy(
        act_ref.at[:, pl.ds(pl.multiple_of(r_me * rw, 128), rw)],
        act_out.at[pl.ds(pl.multiple_of(me * tok, tok), tok), :],
        local_sem.at[0],
    )
    own_g = pltpu.make_async_copy(
        grad_ref.at[:, pl.ds(pl.multiple_of(a_me * cw, 128), cw)],
        grad_out.at[pl.ds(pl.multiple_of(me * tok, tok), tok), :],
        local_sem.at[1],
    )
    own_a.start()
    own_g.start()

    def send(s, c):
        k = lax.rem(me + s, n)
        grad_copy(me, k).start()
        act_copy(me, k).start()
        return c

    lax.fori_loop(1, n, send, 0)

    def finish(s, c):
        k = lax.rem(me + s, n)
        j = lax.rem(me + n - s, n)
        grad_copy(me, k).wait_send()
        act_copy(me, k).wait_send()
        grad_copy(j, me).wait_recv()
        act_copy(j, me).wait_recv()
        return c

    lax.fori_loop(1, n, finish, 0)
    own_a.wait()
    own_g.wait()


def exchange(act, grad, n, row_blocks, rw, cw):
    tok = act.shape[0]
    total = n * tok
    return pl.pallas_call(
        functools.partial(exchange_kernel, n, row_blocks),
        out_shape=(
            jax.ShapeDtypeStruct((total, rw), act.dtype),
            jax.ShapeDtypeStruct((total, cw), grad.dtype),
        ),
        in_specs=[pl.BlockSpec(memory_space=pl.ANY)] * 2,
        out_specs=(pl.BlockSpec(memory_space=pl.ANY), pl.BlockSpec(memory_space=pl.ANY)),
        scratch_shapes=[
            pltpu.SemaphoreType.DMA((n,)),
            pltpu.SemaphoreType.DMA((n,)),
            pltpu.SemaphoreType.DMA((n,)),
            pltpu.SemaphoreType.DMA((n,)),
            pltpu.SemaphoreType.DMA((2,)),
        ],
        compiler_params=pltpu.CompilerParams(collective_id=0, has_side_effects=True),
    )(act, grad)


def xgather_kernel(act_ref, seq_ref, act_out, seq_out, send_sem, recv_sem, local_sem,
                   seq_send, seq_recv):
    n = lax.axis_size("x")
    me = lax.axis_index("x")
    right, left = lax.rem(me + 1, n), lax.rem(me + n - 1, n)
    far = lax.rem(me + 2, n)
    rows = act_ref.shape[0]
    half = rows // 2

    barrier = pltpu.get_barrier_semaphore()
    for nb in (left, right):
        pl.semaphore_signal(barrier, 1, device_id={"x": nb}, device_id_type=MESH)
    pl.semaphore_wait(barrier, 2)

    own = pltpu.make_async_copy(act_ref, act_out.at[me], local_sem.at[0])
    own.start()
    own_seq = pltpu.make_async_copy(seq_ref, seq_out.at[me], local_sem.at[1])
    own_seq.start()

    def seq_copy(src, dst, slot, dev):
        return pltpu.make_async_remote_copy(
            src_ref=src, dst_ref=dst, send_sem=seq_send.at[slot], recv_sem=seq_recv.at[slot],
            device_id={"x": dev}, device_id_type=MESH)

    seq_r = seq_copy(seq_ref, seq_out.at[me], 0, right)
    seq_l = seq_copy(seq_ref, seq_out.at[me], 1, left)
    seq_r.start()
    seq_l.start()
    to_right = pltpu.make_async_remote_copy(
        src_ref=act_ref, dst_ref=act_out.at[me], send_sem=send_sem.at[0],
        recv_sem=recv_sem.at[0], device_id={"x": right}, device_id_type=MESH)
    to_left = pltpu.make_async_remote_copy(
        src_ref=act_ref, dst_ref=act_out.at[me], send_sem=send_sem.at[1],
        recv_sem=recv_sem.at[1], device_id={"x": left}, device_id_type=MESH)
    to_right.start()
    to_left.start()
    from_left = pltpu.make_async_remote_copy(
        src_ref=act_ref, dst_ref=act_out.at[left], send_sem=send_sem.at[0],
        recv_sem=recv_sem.at[0], device_id={"x": left}, device_id_type=MESH)
    from_right = pltpu.make_async_remote_copy(
        src_ref=act_ref, dst_ref=act_out.at[right], send_sem=send_sem.at[1],
        recv_sem=recv_sem.at[1], device_id={"x": right}, device_id_type=MESH)
    from_left.wait_recv()
    from_right.wait_recv()
    seq_copy(seq_ref, seq_out.at[left], 0, left).wait_recv()
    seq_copy(seq_ref, seq_out.at[right], 1, right).wait_recv()
    seq_relay = seq_copy(seq_out.at[right], seq_out.at[right], 2, left)
    seq_relay.start()
    relay_left = pltpu.make_async_remote_copy(
        src_ref=act_out.at[right, pl.ds(0, half)], dst_ref=act_out.at[right, pl.ds(0, half)],
        send_sem=send_sem.at[2], recv_sem=recv_sem.at[2], device_id={"x": left},
        device_id_type=MESH)
    relay_right = pltpu.make_async_remote_copy(
        src_ref=act_out.at[left, pl.ds(half, half)], dst_ref=act_out.at[left, pl.ds(half, half)],
        send_sem=send_sem.at[3], recv_sem=recv_sem.at[3], device_id={"x": right},
        device_id_type=MESH)
    relay_left.start()
    relay_right.start()
    far_first = pltpu.make_async_remote_copy(
        src_ref=act_out.at[far, pl.ds(0, half)], dst_ref=act_out.at[far, pl.ds(0, half)],
        send_sem=send_sem.at[2], recv_sem=recv_sem.at[2], device_id={"x": right},
        device_id_type=MESH)
    far_second = pltpu.make_async_remote_copy(
        src_ref=act_out.at[far, pl.ds(half, half)], dst_ref=act_out.at[far, pl.ds(half, half)],
        send_sem=send_sem.at[3], recv_sem=recv_sem.at[3], device_id={"x": left},
        device_id_type=MESH)
    far_first.wait_recv()
    far_second.wait_recv()
    seq_copy(seq_out.at[far], seq_out.at[far], 2, right).wait_recv()
    seq_r.wait_send()
    seq_l.wait_send()
    seq_relay.wait_send()
    own_seq.wait()
    to_right.wait_send()
    to_left.wait_send()
    relay_left.wait_send()
    relay_right.wait_send()
    own.wait()


def xgather(act, seq):
    n = 4
    rows, cols = act.shape
    return pl.pallas_call(
        xgather_kernel,
        out_shape=(
            jax.ShapeDtypeStruct((n, rows, cols), act.dtype),
            jax.ShapeDtypeStruct((n,) + seq.shape, seq.dtype),
        ),
        in_specs=[pl.BlockSpec(memory_space=pl.ANY)] * 2,
        out_specs=(pl.BlockSpec(memory_space=pl.ANY), pl.BlockSpec(memory_space=pl.ANY)),
        scratch_shapes=[
            pltpu.SemaphoreType.DMA((4,)),
            pltpu.SemaphoreType.DMA((4,)),
            pltpu.SemaphoreType.DMA((2,)),
            pltpu.SemaphoreType.DMA((3,)),
            pltpu.SemaphoreType.DMA((3,)),
        ],
        compiler_params=pltpu.CompilerParams(collective_id=1, has_side_effects=True),
        cost_estimate=pl.CostEstimate(flops=0, bytes_accessed=8 * rows * cols * 2, transcendentals=0),
    )(act, seq)


def mp_merge_kernel(both_ref, out_ref, recv1, recv2, send_sem, recv_sem):
    c = lax.axis_index("c")
    z = lax.axis_index("zl")
    rows = both_ref.shape[1]
    half, quarter = rows // 2, rows // 4
    step = 32
    core = {"c": 1 - c}
    chip = {"zl": 1 - z}

    barrier = pltpu.get_barrier_semaphore()
    pl.semaphore_signal(barrier, 1, device_id=core, device_id_type=MESH)
    pl.semaphore_signal(barrier, 1, device_id=chip, device_id_type=MESH)
    pl.semaphore_wait(barrier, 2)

    mine = pl.multiple_of(c * half, half)
    other = pl.multiple_of((1 - c) * half, half)
    first = pltpu.make_async_remote_copy(
        src_ref=both_ref.at[:, pl.ds(other, half)], dst_ref=recv1,
        send_sem=send_sem.at[0], recv_sem=recv_sem.at[0], device_id=core, device_id_type=MESH)
    first.start()
    first.wait_recv()

    def add_half(i, carry):
        r = pl.multiple_of(i * step, step)
        recv1[:, pl.ds(r, step)] = recv1[:, pl.ds(r, step)] + both_ref[:, pl.ds(mine + r, step)]
        return carry

    lax.fori_loop(0, half // step, add_half, 0)

    my_q = pl.multiple_of(z * quarter, quarter)
    far_q = pl.multiple_of((1 - z) * quarter, quarter)
    second = pltpu.make_async_remote_copy(
        src_ref=recv1.at[:, pl.ds(far_q, quarter)], dst_ref=recv2,
        send_sem=send_sem.at[1], recv_sem=recv_sem.at[1], device_id=chip, device_id_type=MESH)
    second.start()
    second.wait_recv()

    def merge(i, carry):
        r = pl.multiple_of(i * step, step)
        n = recv1[0, pl.ds(my_q + r, step)] + recv2[0, pl.ds(r, step)]
        d = recv1[1, pl.ds(my_q + r, step)] + recv2[1, pl.ds(r, step)]
        out_ref[pl.ds(mine + my_q + r, step)] = (n / d).astype(out_ref.dtype)
        return carry

    lax.fori_loop(0, quarter // step, merge, 0)

    third = pltpu.make_async_remote_copy(
        src_ref=out_ref.at[pl.ds(mine + my_q, quarter)], dst_ref=out_ref.at[pl.ds(mine + my_q, quarter)],
        send_sem=send_sem.at[2], recv_sem=recv_sem.at[2], device_id=chip, device_id_type=MESH)
    third.start()
    pltpu.make_async_remote_copy(
        src_ref=out_ref.at[pl.ds(mine + far_q, quarter)], dst_ref=out_ref.at[pl.ds(mine + far_q, quarter)],
        send_sem=send_sem.at[2], recv_sem=recv_sem.at[2], device_id=chip, device_id_type=MESH).wait_recv()
    fourth = pltpu.make_async_remote_copy(
        src_ref=out_ref.at[pl.ds(mine, half)], dst_ref=out_ref.at[pl.ds(mine, half)],
        send_sem=send_sem.at[3], recv_sem=recv_sem.at[3], device_id=core, device_id_type=MESH)
    fourth.start()
    pltpu.make_async_remote_copy(
        src_ref=out_ref.at[pl.ds(other, half)], dst_ref=out_ref.at[pl.ds(other, half)],
        send_sem=send_sem.at[3], recv_sem=recv_sem.at[3], device_id=core, device_id_type=MESH).wait_recv()
    first.wait_send()
    second.wait_send()
    third.wait_send()
    fourth.wait_send()


def mp_merge(both, cid):
    _, rows, cols = both.shape
    vmem = pltpu.MemorySpace.VMEM
    return pl.pallas_call(
        mp_merge_kernel,
        out_shape=jax.ShapeDtypeStruct((rows, cols), jnp.bfloat16),
        in_specs=[pl.BlockSpec(memory_space=vmem)],
        out_specs=pl.BlockSpec(memory_space=vmem),
        scratch_shapes=[
            pltpu.VMEM((2, rows // 2, cols), jnp.float32),
            pltpu.VMEM((2, rows // 4, cols), jnp.float32),
            pltpu.SemaphoreType.DMA((4,)),
            pltpu.SemaphoreType.DMA((4,)),
        ],
        compiler_params=pltpu.CompilerParams(
            collective_id=cid, has_side_effects=True, vmem_limit_bytes=60 * 1024 * 1024),
        cost_estimate=pl.CostEstimate(flops=rows * cols * 4, bytes_accessed=rows * cols * 16, transcendentals=0),
    )(both)


def per_device(activations, out_grads, seq_ids, weights):
    nx = lax.axis_size("x")
    nj = lax.axis_size(("zh", "y"))
    tok = activations.shape[1]
    col_width = weights.shape[2]
    row_width = weights.shape[1]
    total = nx * nj * tok
    act_blocks = activations[0].reshape(tok, nj, row_width).transpose(1, 0, 2)
    act_mine = lax.all_to_all(act_blocks, ("zh", "y"), 0, 0, tiled=True)
    grad_blocks = out_grads[0].reshape(tok, nx, col_width).transpose(1, 0, 2)
    grad_mine = lax.all_to_all(grad_blocks, "x", 0, 0, tiled=True)
    act_all, owners = xgather(act_mine.reshape(nj * tok, row_width), seq_ids)
    first_long = jnp.sum((owners < 1).astype(jnp.int32)) * (total // owners.size) > total // 2
    w_all = weights[0].astype(jnp.float32)
    chunks = 2
    width = col_width // chunks
    merged = []
    for k in range(chunks):
        cols = slice(k * width, (k + 1) * width)
        grad_all = lax.all_gather(grad_mine[..., cols], ("zh", "y"), axis=0, tiled=False)
        if merged:
            merged[-1], grad_all = lax.optimization_barrier((merged[-1], grad_all))

        def part(x):
            g = grad_all[:, x].reshape(nj * tok, width)
            return lax.dot_general(
                act_all[x], g, (((0,), (0,)), ((), ())), preferred_element_type=jnp.float32
            )

        head = part(0)
        mid = part(1) + part(2)
        tail = part(3)
        g0 = jnp.where(first_long, head + mid, head)
        g1 = jnp.where(first_long, tail, mid + tail)
        fisher = g0 * g0 + g1 * g1
        prior = fisher / SEQS + smoothing
        w = w_all[:, cols]
        both = prior[None] * jnp.stack([w, jnp.ones_like(w)], axis=0)
        merged.append(mp_merge(both, 2 + k))
    return jnp.concatenate(merged, axis=1)


def solution(mesh):
    assert mesh.shape["mp"] == 4 and mesh.shape["fsdp"] == 32
    fine = jax.sharding.Mesh(
        mesh.devices.reshape(2, 2, 4, 2, 4), ("zl", "c", "x", "zh", "y")
    )
    mp, fs = ("zl", "c"), ("x", "zh", "y")
    placed = (P(mp, fs, None), P(mp, fs, None), P(mp, fs), P(mp, fs, None))
    return jax.shard_map(
        per_device, mesh=fine, in_specs=placed, out_specs=P(fs, None), check_vma=False
    )
```

```python
import functools

import jax
import jax.numpy as jnp
from jax import lax
from jax.experimental import pallas as pl
from jax.experimental.pallas import tpu as pltpu
from jax.sharding import PartitionSpec as P

F = 7168
SEQS = 2
MESH = pl.DeviceIdType.MESH

smoothing = 0.05


def mp_merge_kernel(prior_ref, w_ref, out_ref, recv_p, recv_w, recv1, recv2, send_sem, recv_sem):
    c = lax.axis_index("c")
    z = lax.axis_index("zl")
    rows = prior_ref.shape[0]
    half, quarter = rows // 2, rows // 4
    step = 32
    core = {"c": 1 - c}
    chip = {"zl": 1 - z}

    barrier = pltpu.get_barrier_semaphore()
    pl.semaphore_signal(barrier, 1, device_id=core, device_id_type=MESH)
    pl.semaphore_signal(barrier, 1, device_id=chip, device_id_type=MESH)
    pl.semaphore_wait(barrier, 2)

    mine = pl.multiple_of(c * half, half)
    other = pl.multiple_of((1 - c) * half, half)
    first = pltpu.make_async_remote_copy(
        src_ref=prior_ref.at[pl.ds(other, half)], dst_ref=recv_p,
        send_sem=send_sem.at[0], recv_sem=recv_sem.at[0], device_id=core, device_id_type=MESH)
    first_w = pltpu.make_async_remote_copy(
        src_ref=w_ref.at[pl.ds(other, half)], dst_ref=recv_w,
        send_sem=send_sem.at[4], recv_sem=recv_sem.at[4], device_id=core, device_id_type=MESH)
    first_w.start()
    first.start()
    first_w.wait_recv()
    first.wait_recv()

    def add_half(i, carry):
        r = pl.multiple_of(i * step, step)
        p_me = prior_ref[pl.ds(mine + r, step)]
        p_ot = recv_p[pl.ds(r, step)]
        n_me = p_me * w_ref[pl.ds(mine + r, step)].astype(jnp.float32)
        n_ot = p_ot * recv_w[pl.ds(r, step)].astype(jnp.float32)
        recv1[0, pl.ds(r, step)] = n_ot + n_me
        recv1[1, pl.ds(r, step)] = p_ot + p_me
        return carry

    lax.fori_loop(0, half // step, add_half, 0)

    my_q = pl.multiple_of(z * quarter, quarter)
    far_q = pl.multiple_of((1 - z) * quarter, quarter)
    second = pltpu.make_async_remote_copy(
        src_ref=recv1.at[:, pl.ds(far_q, quarter)], dst_ref=recv2,
        send_sem=send_sem.at[1], recv_sem=recv_sem.at[1], device_id=chip, device_id_type=MESH)
    second.start()
    second.wait_recv()

    def merge(i, carry):
        r = pl.multiple_of(i * step, step)
        n = recv1[0, pl.ds(my_q + r, step)] + recv2[0, pl.ds(r, step)]
        d = recv1[1, pl.ds(my_q + r, step)] + recv2[1, pl.ds(r, step)]
        out_ref[pl.ds(mine + my_q + r, step)] = (n / d).astype(out_ref.dtype)
        return carry

    lax.fori_loop(0, quarter // step, merge, 0)

    third = pltpu.make_async_remote_copy(
        src_ref=out_ref.at[pl.ds(mine + my_q, quarter)], dst_ref=out_ref.at[pl.ds(mine + my_q, quarter)],
        send_sem=send_sem.at[2], recv_sem=recv_sem.at[2], device_id=chip, device_id_type=MESH)
    third.start()
    pltpu.make_async_remote_copy(
        src_ref=out_ref.at[pl.ds(mine + far_q, quarter)], dst_ref=out_ref.at[pl.ds(mine + far_q, quarter)],
        send_sem=send_sem.at[2], recv_sem=recv_sem.at[2], device_id=chip, device_id_type=MESH).wait_recv()
    fourth = pltpu.make_async_remote_copy(
        src_ref=out_ref.at[pl.ds(mine, half)], dst_ref=out_ref.at[pl.ds(mine, half)],
        send_sem=send_sem.at[3], recv_sem=recv_sem.at[3], device_id=core, device_id_type=MESH)
    fourth.start()
    pltpu.make_async_remote_copy(
        src_ref=out_ref.at[pl.ds(other, half)], dst_ref=out_ref.at[pl.ds(other, half)],
        send_sem=send_sem.at[3], recv_sem=recv_sem.at[3], device_id=core, device_id_type=MESH).wait_recv()
    first.wait_send()
    first_w.wait_send()
    second.wait_send()
    third.wait_send()
    fourth.wait_send()


def mp_merge(prior, w, cid):
    rows, cols = prior.shape
    vmem = pltpu.MemorySpace.VMEM
    return pl.pallas_call(
        mp_merge_kernel,
        out_shape=jax.ShapeDtypeStruct((rows, cols), jnp.bfloat16),
        in_specs=[pl.BlockSpec(memory_space=vmem)] * 2,
        out_specs=pl.BlockSpec(memory_space=vmem),
        scratch_shapes=[
            pltpu.VMEM((rows // 2, cols), jnp.float32),
            pltpu.VMEM((rows // 2, cols), w.dtype),
            pltpu.VMEM((2, rows // 2, cols), jnp.float32),
            pltpu.VMEM((2, rows // 4, cols), jnp.float32),
            pltpu.SemaphoreType.DMA((5,)),
            pltpu.SemaphoreType.DMA((5,)),
        ],
        compiler_params=pltpu.CompilerParams(
            collective_id=cid, has_side_effects=True, vmem_limit_bytes=60 * 1024 * 1024),
        cost_estimate=pl.CostEstimate(flops=rows * cols * 6, bytes_accessed=rows * cols * 12, transcendentals=0),
    )(prior, w)


def ring_copies(axis, me, n, src, slot, sems, base):
    right, left = lax.rem(me + 1, n), lax.rem(me + n - 1, n)
    far = lax.rem(me + 2, n)
    send, recv = sems
    half = src.shape[0] // 2

    def rc(s, d, k, dev):
        return pltpu.make_async_remote_copy(
            src_ref=s, dst_ref=d, send_sem=send.at[base + k], recv_sem=recv.at[base + k],
            device_id={axis: dev}, device_id_type=MESH)

    whole = pl.ds(0, 2 * half)
    lo, hi = pl.ds(0, half), pl.ds(half, half)
    first = [rc(src, slot(me, whole), 0, right), rc(src, slot(me, whole), 1, left)]
    arrive = [rc(src, slot(left, whole), 0, left), rc(src, slot(right, whole), 1, right)]
    relay = [
        rc(slot(right, lo), slot(right, lo), 2, left),
        rc(slot(left, hi), slot(left, hi), 3, right),
    ]
    land = [
        rc(slot(far, lo), slot(far, lo), 2, right),
        rc(slot(far, hi), slot(far, hi), 3, left),
    ]
    return first, arrive, relay, land


def gather_kernel(act_in, grad_in, seq_ref, act_out, grad_out, seq_out, act_ref, grad_ref,
                  send, recv, local, seq_send, seq_recv, p0_send, p0_recv, q0_send, q0_recv):
    nx = 4
    ny = 4
    x = lax.axis_index("x")
    y = lax.axis_index("y")
    zh = lax.axis_index("zh")
    xr, xl = lax.rem(x + 1, nx), lax.rem(x + nx - 1, nx)
    yr, yl = lax.rem(y + 1, ny), lax.rem(y + ny - 1, ny)

    nj = 2 * ny
    j = zh * ny + y
    rw = act_ref.shape[2]
    cw = grad_ref.shape[2]

    def plane(jd):
        return {"zh": jd // ny, "y": lax.rem(jd, ny)}

    barrier = pltpu.get_barrier_semaphore()
    for s in range(1, nj):
        pl.semaphore_signal(barrier, 1, device_id=plane(lax.rem(j + s, nj)), device_id_type=MESH)
    for s in range(1, nx):
        pl.semaphore_signal(barrier, 1, device_id={"x": lax.rem(x + s, nx)}, device_id_type=MESH)
    pl.semaphore_wait(barrier, nj - 1 + nx - 1)

    def act_p0(s, jd, js):
        return pltpu.make_async_remote_copy(
            src_ref=act_in.at[:, pl.ds(pl.multiple_of(jd * rw, 128), rw)], dst_ref=act_ref.at[js],
            send_sem=p0_send.at[s], recv_sem=p0_recv.at[s], device_id=plane(jd),
            device_id_type=MESH)

    def grad_p0(s, xd, xs):
        return pltpu.make_async_remote_copy(
            src_ref=grad_in.at[:, pl.ds(pl.multiple_of(xd * cw, 128), cw)], dst_ref=grad_ref.at[xs],
            send_sem=q0_send.at[s], recv_sem=q0_recv.at[s], device_id={"x": xd},
            device_id_type=MESH)

    p0_out = [act_p0(s, lax.rem(j + s, nj), j) for s in range(1, nj)]
    p0_in = [act_p0(s, j, lax.rem(j + nj - s, nj)) for s in range(1, nj)]
    q0_out = [grad_p0(s, lax.rem(x + s, nx), x) for s in range(1, nx)]
    q0_in = [grad_p0(s, x, lax.rem(x + nx - s, nx)) for s in range(1, nx)]
    own0 = [
        pltpu.make_async_copy(
            act_in.at[:, pl.ds(pl.multiple_of(j * rw, 128), rw)], act_ref.at[j], local.at[3]),
        pltpu.make_async_copy(
            grad_in.at[:, pl.ds(pl.multiple_of(x * cw, 128), cw)], grad_ref.at[x], local.at[4]),
    ]
    for c in own0 + q0_out + p0_out:
        c.start()
    for c in q0_in:
        c.wait_recv()
    own0[1].wait()

    sems = (send, recv)
    a_first, a_arrive, a_relay, a_land = ring_copies(
        "x", x, nx, act_ref, lambda i, p: act_out.at[i, p], sems, 0)
    g_first, g_arrive, g_relay, g_land = ring_copies(
        "y", y, ny, grad_ref, lambda i, p: grad_out.at[p, zh, i], sems, 4)
    p_first, p_arrive, p_relay, p_land = ring_copies(
        "y", y, ny, grad_out.at[:, 1 - zh, y], lambda i, p: grad_out.at[p, 1 - zh, i], sems, 8)
    swap = pltpu.make_async_remote_copy(
        src_ref=grad_ref, dst_ref=grad_out.at[:, zh, y], send_sem=send.at[12],
        recv_sem=recv.at[12], device_id={"zh": 1 - zh}, device_id_type=MESH)
    swap_in = pltpu.make_async_remote_copy(
        src_ref=grad_ref, dst_ref=grad_out.at[:, 1 - zh, y], send_sem=send.at[12],
        recv_sem=recv.at[12], device_id={"zh": 1 - zh}, device_id_type=MESH)

    own = [
        pltpu.make_async_copy(act_ref, act_out.at[x], local.at[0]),
        pltpu.make_async_copy(grad_ref, grad_out.at[:, zh, y], local.at[1]),
        pltpu.make_async_copy(seq_ref, seq_out.at[x], local.at[2]),
    ]

    def sc(s, d, k, dev):
        return pltpu.make_async_remote_copy(
            src_ref=s, dst_ref=d, send_sem=seq_send.at[k], recv_sem=seq_recv.at[k],
            device_id={"x": dev}, device_id_type=MESH)

    seq_first = [sc(seq_ref, seq_out.at[x], 0, xr), sc(seq_ref, seq_out.at[x], 1, xl)]

    swap.start()
    for c in g_first + seq_first + [own[1], own[2]]:
        c.start()
    for c in p0_in:
        c.wait_recv()
    own0[0].wait()
    for c in a_first + [own[0]]:
        c.start()
    for c in a_arrive:
        c.wait_recv()
    sc(seq_ref, seq_out.at[xl], 0, xl).wait_recv()
    sc(seq_ref, seq_out.at[xr], 1, xr).wait_recv()
    seq_relay = sc(seq_out.at[xr], seq_out.at[xr], 2, xl)
    seq_relay.start()
    for c in a_relay:
        c.start()
    for c in g_arrive:
        c.wait_recv()
    for c in g_relay:
        c.start()
    swap_in.wait_recv()
    for c in p_first:
        c.start()
    for c in p_arrive:
        c.wait_recv()
    for c in p_relay:
        c.start()
    for c in a_land + g_land + p_land:
        c.wait_recv()
    sc(seq_out.at[lax.rem(x + 2, nx)], seq_out.at[lax.rem(x + 2, nx)], 2, xr).wait_recv()
    for c in a_first + a_relay + g_first + g_relay + p_first + p_relay + seq_first:
        c.wait_send()
    seq_relay.wait_send()
    swap.wait_send()
    for c in p0_out + q0_out:
        c.wait_send()
    for c in own:
        c.wait()


def gather_all(act, grad, seq, nj, nx, rw, cw):
    tok = act.shape[0]
    any_space = pl.BlockSpec(memory_space=pl.ANY)
    return pl.pallas_call(
        gather_kernel,
        out_shape=(
            jax.ShapeDtypeStruct((nx, nj, tok, rw), act.dtype),
            jax.ShapeDtypeStruct((nx, 2, nj // 2, tok, cw), grad.dtype),
            jax.ShapeDtypeStruct((nx,) + seq.shape, seq.dtype),
            jax.ShapeDtypeStruct((nj, tok, rw), act.dtype),
            jax.ShapeDtypeStruct((nx, tok, cw), grad.dtype),
        ),
        in_specs=[any_space] * 3,
        out_specs=(any_space,) * 5,
        scratch_shapes=[
            pltpu.SemaphoreType.DMA((13,)),
            pltpu.SemaphoreType.DMA((13,)),
            pltpu.SemaphoreType.DMA((5,)),
            pltpu.SemaphoreType.DMA((3,)),
            pltpu.SemaphoreType.DMA((3,)),
            pltpu.SemaphoreType.DMA((nj,)),
            pltpu.SemaphoreType.DMA((nj,)),
            pltpu.SemaphoreType.DMA((nx,)),
            pltpu.SemaphoreType.DMA((nx,)),
        ],
        compiler_params=pltpu.CompilerParams(collective_id=1, has_side_effects=True),
        cost_estimate=pl.CostEstimate(
            flops=0, bytes_accessed=8 * tok * (nj * rw + 2 * nx * cw), transcendentals=0),
    )(act, grad, seq)


def per_device(activations, out_grads, seq_ids, weights):
    nx = lax.axis_size("x")
    nj = lax.axis_size(("zh", "y"))
    tok = activations.shape[1]
    col_width = weights.shape[2]
    row_width = weights.shape[1]
    total = nx * nj * tok
    act_all, grad_all, owners, _, _ = gather_all(
        activations[0], out_grads[0], seq_ids, nj, nx, row_width, col_width)
    act_all = act_all.reshape(total, row_width)
    grad_all = grad_all.reshape(total, col_width)
    first_long = jnp.sum((owners < 1).astype(jnp.int32)) * (total // owners.size) > total // 2

    def part(lo, hi):
        return lax.dot_general(
            act_all[lo:hi], grad_all[lo:hi], (((0,), (0,)), ((), ())),
            preferred_element_type=jnp.float32,
        )

    quarter = total // 4
    head = part(0, quarter)
    mid = part(quarter, 3 * quarter)
    tail = part(3 * quarter, total)
    g0 = jnp.where(first_long, head + mid, head)
    g1 = jnp.where(first_long, tail, mid + tail)
    fisher = g0 * g0 + g1 * g1
    prior = fisher / SEQS + smoothing
    return mp_merge(prior, weights[0], 2)


def solution(mesh):
    assert mesh.shape["mp"] == 4 and mesh.shape["fsdp"] == 32
    fine = jax.sharding.Mesh(
        mesh.devices.reshape(2, 2, 4, 2, 4), ("zl", "c", "x", "zh", "y")
    )
    mp, fs = ("zl", "c"), ("x", "zh", "y")
    placed = (P(mp, fs, None), P(mp, fs, None), P(mp, fs), P(mp, fs, None))
    return jax.shard_map(
        per_device, mesh=fine, in_specs=placed, out_specs=P(fs, None), check_vma=False
    )
```

```python
import functools

import jax
import jax.numpy as jnp
from jax import lax
from jax.experimental import pallas as pl
from jax.experimental.pallas import tpu as pltpu
from jax.sharding import PartitionSpec as P

F = 7168
SEQS = 2
MESH = pl.DeviceIdType.MESH

smoothing = 0.05


def mp_merge_kernel(prior_ref, w_ref, out_ref, recv_p, recv_w, recv1, recv2, send_sem, recv_sem):
    c = lax.axis_index("c")
    z = lax.axis_index("zl")
    rows = prior_ref.shape[0]
    half, quarter = rows // 2, rows // 4
    step = 32
    core = {"c": 1 - c}
    chip = {"zl": 1 - z}

    barrier = pltpu.get_barrier_semaphore()
    pl.semaphore_signal(barrier, 1, device_id=core, device_id_type=MESH)
    pl.semaphore_signal(barrier, 1, device_id=chip, device_id_type=MESH)
    pl.semaphore_wait(barrier, 2)

    mine = pl.multiple_of(c * half, half)
    other = pl.multiple_of((1 - c) * half, half)
    first = pltpu.make_async_remote_copy(
        src_ref=prior_ref.at[pl.ds(other, half)], dst_ref=recv_p,
        send_sem=send_sem.at[0], recv_sem=recv_sem.at[0], device_id=core, device_id_type=MESH)
    first_w = pltpu.make_async_remote_copy(
        src_ref=w_ref.at[pl.ds(other, half)], dst_ref=recv_w,
        send_sem=send_sem.at[4], recv_sem=recv_sem.at[4], device_id=core, device_id_type=MESH)
    first_w.start()
    first.start()
    first_w.wait_recv()
    first.wait_recv()

    def add_half(i, carry):
        r = pl.multiple_of(i * step, step)
        p_me = prior_ref[pl.ds(mine + r, step)]
        p_ot = recv_p[pl.ds(r, step)]
        n_me = p_me * w_ref[pl.ds(mine + r, step)].astype(jnp.float32)
        n_ot = p_ot * recv_w[pl.ds(r, step)].astype(jnp.float32)
        recv1[0, pl.ds(r, step)] = n_ot + n_me
        recv1[1, pl.ds(r, step)] = p_ot + p_me
        return carry

    lax.fori_loop(0, half // step, add_half, 0)

    my_q = pl.multiple_of(z * quarter, quarter)
    far_q = pl.multiple_of((1 - z) * quarter, quarter)
    second = pltpu.make_async_remote_copy(
        src_ref=recv1.at[:, pl.ds(far_q, quarter)], dst_ref=recv2,
        send_sem=send_sem.at[1], recv_sem=recv_sem.at[1], device_id=chip, device_id_type=MESH)
    second.start()
    second.wait_recv()

    def merge(i, carry):
        r = pl.multiple_of(i * step, step)
        n = recv1[0, pl.ds(my_q + r, step)] + recv2[0, pl.ds(r, step)]
        d = recv1[1, pl.ds(my_q + r, step)] + recv2[1, pl.ds(r, step)]
        out_ref[pl.ds(mine + my_q + r, step)] = (n / d).astype(out_ref.dtype)
        return carry

    lax.fori_loop(0, quarter // step, merge, 0)

    third = pltpu.make_async_remote_copy(
        src_ref=out_ref.at[pl.ds(mine + my_q, quarter)], dst_ref=out_ref.at[pl.ds(mine + my_q, quarter)],
        send_sem=send_sem.at[2], recv_sem=recv_sem.at[2], device_id=chip, device_id_type=MESH)
    third.start()
    pltpu.make_async_remote_copy(
        src_ref=out_ref.at[pl.ds(mine + far_q, quarter)], dst_ref=out_ref.at[pl.ds(mine + far_q, quarter)],
        send_sem=send_sem.at[2], recv_sem=recv_sem.at[2], device_id=chip, device_id_type=MESH).wait_recv()
    fourth = pltpu.make_async_remote_copy(
        src_ref=out_ref.at[pl.ds(mine, half)], dst_ref=out_ref.at[pl.ds(mine, half)],
        send_sem=send_sem.at[3], recv_sem=recv_sem.at[3], device_id=core, device_id_type=MESH)
    fourth.start()
    pltpu.make_async_remote_copy(
        src_ref=out_ref.at[pl.ds(other, half)], dst_ref=out_ref.at[pl.ds(other, half)],
        send_sem=send_sem.at[3], recv_sem=recv_sem.at[3], device_id=core, device_id_type=MESH).wait_recv()
    first.wait_send()
    first_w.wait_send()
    second.wait_send()
    third.wait_send()
    fourth.wait_send()


def mp_merge(prior, w, cid):
    rows, cols = prior.shape
    vmem = pltpu.MemorySpace.VMEM
    return pl.pallas_call(
        mp_merge_kernel,
        out_shape=jax.ShapeDtypeStruct((rows, cols), jnp.bfloat16),
        in_specs=[pl.BlockSpec(memory_space=vmem)] * 2,
        out_specs=pl.BlockSpec(memory_space=vmem),
        scratch_shapes=[
            pltpu.VMEM((rows // 2, cols), jnp.float32),
            pltpu.VMEM((rows // 2, cols), w.dtype),
            pltpu.VMEM((2, rows // 2, cols), jnp.float32),
            pltpu.VMEM((2, rows // 4, cols), jnp.float32),
            pltpu.SemaphoreType.DMA((5,)),
            pltpu.SemaphoreType.DMA((5,)),
        ],
        compiler_params=pltpu.CompilerParams(
            collective_id=cid, has_side_effects=True, vmem_limit_bytes=60 * 1024 * 1024),
        cost_estimate=pl.CostEstimate(flops=rows * cols * 6, bytes_accessed=rows * cols * 12, transcendentals=0),
    )(prior, w)


def ring_copies(axis, me, n, src, slot, sems, base):
    right, left = lax.rem(me + 1, n), lax.rem(me + n - 1, n)
    far = lax.rem(me + 2, n)
    send, recv = sems
    half = src.shape[0] // 2

    def rc(s, d, k, dev):
        return pltpu.make_async_remote_copy(
            src_ref=s, dst_ref=d, send_sem=send.at[base + k], recv_sem=recv.at[base + k],
            device_id={axis: dev}, device_id_type=MESH)

    whole = pl.ds(0, 2 * half)
    lo, hi = pl.ds(0, half), pl.ds(half, half)
    first = [rc(src, slot(me, whole), 0, right), rc(src, slot(me, whole), 1, left)]
    arrive = [rc(src, slot(left, whole), 0, left), rc(src, slot(right, whole), 1, right)]
    relay = [
        rc(slot(right, lo), slot(right, lo), 2, left),
        rc(slot(left, hi), slot(left, hi), 3, right),
    ]
    land = [
        rc(slot(far, lo), slot(far, lo), 2, right),
        rc(slot(far, hi), slot(far, hi), 3, left),
    ]
    return first, arrive, relay, land


def gather_kernel(act_in, grad_in, seq_ref, act_out, grad_out, seq_out, act_ref, grad_ref,
                  send, recv, local, seq_send, seq_recv, p0_send, p0_recv, q0_send, q0_recv,
                  z0_send, z0_recv):
    nx = 4
    ny = 4
    x = lax.axis_index("x")
    y = lax.axis_index("y")
    zh = lax.axis_index("zh")
    xr, xl = lax.rem(x + 1, nx), lax.rem(x + nx - 1, nx)
    yr, yl = lax.rem(y + 1, ny), lax.rem(y + ny - 1, ny)

    nj = 2 * ny
    j = zh * ny + y
    rw = act_ref.shape[2]
    cw = grad_ref.shape[2]

    def plane(jd):
        return {"zh": jd // ny, "y": lax.rem(jd, ny)}

    barrier = pltpu.get_barrier_semaphore()
    for s in range(1, nj):
        pl.semaphore_signal(barrier, 1, device_id=plane(lax.rem(j + s, nj)), device_id_type=MESH)
    for s in range(1, nx):
        pl.semaphore_signal(barrier, 1, device_id={"x": lax.rem(x + s, nx)}, device_id_type=MESH)
        pl.semaphore_signal(
            barrier, 1, device_id={"x": lax.rem(x + s, nx), "zh": 1 - zh}, device_id_type=MESH)
    pl.semaphore_wait(barrier, nj - 1 + 2 * (nx - 1))

    def act_p0(s, jd, js):
        return pltpu.make_async_remote_copy(
            src_ref=act_in.at[:, pl.ds(pl.multiple_of(jd * rw, 128), rw)], dst_ref=act_ref.at[js],
            send_sem=p0_send.at[s], recv_sem=p0_recv.at[s], device_id=plane(jd),
            device_id_type=MESH)

    def grad_p0(s, xd, xs):
        return pltpu.make_async_remote_copy(
            src_ref=grad_in.at[:, pl.ds(pl.multiple_of(xd * cw, 128), cw)], dst_ref=grad_ref.at[xs],
            send_sem=q0_send.at[s], recv_sem=q0_recv.at[s], device_id={"x": xd},
            device_id_type=MESH)

    def grad_z0(s, xd, xs, zs):
        return pltpu.make_async_remote_copy(
            src_ref=grad_in.at[:, pl.ds(pl.multiple_of(xd * cw, 128), cw)],
            dst_ref=grad_out.at[xs, zs, y],
            send_sem=z0_send.at[s], recv_sem=z0_recv.at[s],
            device_id={"x": xd, "zh": 1 - zh}, device_id_type=MESH)

    z0_out = [grad_z0(s, lax.rem(x + s, nx), x, zh) for s in range(nx)]
    z0_in = [grad_z0(s, x, lax.rem(x + nx - s, nx), 1 - zh) for s in range(nx)]
    p0_out = [act_p0(s, lax.rem(j + s, nj), j) for s in range(1, nj)]
    p0_in = [act_p0(s, j, lax.rem(j + nj - s, nj)) for s in range(1, nj)]
    q0_out = [grad_p0(s, lax.rem(x + s, nx), x) for s in range(1, nx)]
    q0_in = [grad_p0(s, x, lax.rem(x + nx - s, nx)) for s in range(1, nx)]
    own0 = [
        pltpu.make_async_copy(
            act_in.at[:, pl.ds(pl.multiple_of(j * rw, 128), rw)], act_ref.at[j], local.at[3]),
        pltpu.make_async_copy(
            grad_in.at[:, pl.ds(pl.multiple_of(x * cw, 128), cw)], grad_ref.at[x], local.at[4]),
    ]
    for c in z0_out + own0 + q0_out + p0_out:
        c.start()
    for c in q0_in:
        c.wait_recv()
    own0[1].wait()

    sems = (send, recv)
    a_first, a_arrive, a_relay, a_land = ring_copies(
        "x", x, nx, act_ref, lambda i, p: act_out.at[i, p], sems, 0)
    g_first, g_arrive, g_relay, g_land = ring_copies(
        "y", y, ny, grad_ref, lambda i, p: grad_out.at[p, zh, i], sems, 4)
    p_first, p_arrive, p_relay, p_land = ring_copies(
        "y", y, ny, grad_out.at[:, 1 - zh, y], lambda i, p: grad_out.at[p, 1 - zh, i], sems, 8)

    own = [
        pltpu.make_async_copy(act_ref, act_out.at[x], local.at[0]),
        pltpu.make_async_copy(grad_ref, grad_out.at[:, zh, y], local.at[1]),
        pltpu.make_async_copy(seq_ref, seq_out.at[x], local.at[2]),
    ]

    def sc(s, d, k, dev):
        return pltpu.make_async_remote_copy(
            src_ref=s, dst_ref=d, send_sem=seq_send.at[k], recv_sem=seq_recv.at[k],
            device_id={"x": dev}, device_id_type=MESH)

    seq_first = [sc(seq_ref, seq_out.at[x], 0, xr), sc(seq_ref, seq_out.at[x], 1, xl)]

    for c in g_first + seq_first + [own[1], own[2]]:
        c.start()
    for c in p0_in:
        c.wait_recv()
    own0[0].wait()
    for c in a_first + [own[0]]:
        c.start()
    for c in a_arrive:
        c.wait_recv()
    sc(seq_ref, seq_out.at[xl], 0, xl).wait_recv()
    sc(seq_ref, seq_out.at[xr], 1, xr).wait_recv()
    seq_relay = sc(seq_out.at[xr], seq_out.at[xr], 2, xl)
    seq_relay.start()
    for c in a_relay:
        c.start()
    for c in g_arrive:
        c.wait_recv()
    for c in g_relay:
        c.start()
    for c in z0_in:
        c.wait_recv()
    for c in p_first:
        c.start()
    for c in p_arrive:
        c.wait_recv()
    for c in p_relay:
        c.start()
    for c in a_land + g_land + p_land:
        c.wait_recv()
    sc(seq_out.at[lax.rem(x + 2, nx)], seq_out.at[lax.rem(x + 2, nx)], 2, xr).wait_recv()
    for c in a_first + a_relay + g_first + g_relay + p_first + p_relay + seq_first:
        c.wait_send()
    seq_relay.wait_send()
    for c in p0_out + q0_out + z0_out:
        c.wait_send()
    for c in own:
        c.wait()


def gather_all(act, grad, seq, nj, nx, rw, cw):
    tok = act.shape[0]
    any_space = pl.BlockSpec(memory_space=pl.ANY)
    return pl.pallas_call(
        gather_kernel,
        out_shape=(
            jax.ShapeDtypeStruct((nx, nj, tok, rw), act.dtype),
            jax.ShapeDtypeStruct((nx, 2, nj // 2, tok, cw), grad.dtype),
            jax.ShapeDtypeStruct((nx,) + seq.shape, seq.dtype),
            jax.ShapeDtypeStruct((nj, tok, rw), act.dtype),
            jax.ShapeDtypeStruct((nx, tok, cw), grad.dtype),
        ),
        in_specs=[any_space] * 3,
        out_specs=(any_space,) * 5,
        scratch_shapes=[
            pltpu.SemaphoreType.DMA((13,)),
            pltpu.SemaphoreType.DMA((13,)),
            pltpu.SemaphoreType.DMA((5,)),
            pltpu.SemaphoreType.DMA((3,)),
            pltpu.SemaphoreType.DMA((3,)),
            pltpu.SemaphoreType.DMA((nj,)),
            pltpu.SemaphoreType.DMA((nj,)),
            pltpu.SemaphoreType.DMA((nx,)),
            pltpu.SemaphoreType.DMA((nx,)),
            pltpu.SemaphoreType.DMA((nx,)),
            pltpu.SemaphoreType.DMA((nx,)),
        ],
        compiler_params=pltpu.CompilerParams(collective_id=1, has_side_effects=True),
        cost_estimate=pl.CostEstimate(
            flops=0, bytes_accessed=8 * tok * (nj * rw + 2 * nx * cw), transcendentals=0),
    )(act, grad, seq)


def per_device(activations, out_grads, seq_ids, weights):
    nx = lax.axis_size("x")
    nj = lax.axis_size(("zh", "y"))
    tok = activations.shape[1]
    col_width = weights.shape[2]
    row_width = weights.shape[1]
    total = nx * nj * tok
    act_all, grad_all, owners, _, _ = gather_all(
        activations[0], out_grads[0], seq_ids, nj, nx, row_width, col_width)
    act_all = act_all.reshape(total, row_width)
    grad_all = grad_all.reshape(total, col_width)
    first_long = jnp.sum((owners < 1).astype(jnp.int32)) * (total // owners.size) > total // 2

    def part(lo, hi):
        return lax.dot_general(
            act_all[lo:hi], grad_all[lo:hi], (((0,), (0,)), ((), ())),
            preferred_element_type=jnp.float32,
        )

    quarter = total // 4
    head = part(0, quarter)
    mid = part(quarter, 3 * quarter)
    tail = part(3 * quarter, total)
    g0 = jnp.where(first_long, head + mid, head)
    g1 = jnp.where(first_long, tail, mid + tail)
    fisher = g0 * g0 + g1 * g1
    prior = fisher / SEQS + smoothing
    return mp_merge(prior, weights[0], 2)


def solution(mesh):
    assert mesh.shape["mp"] == 4 and mesh.shape["fsdp"] == 32
    fine = jax.sharding.Mesh(
        mesh.devices.reshape(2, 2, 4, 2, 4), ("zl", "c", "x", "zh", "y")
    )
    mp, fs = ("zl", "c"), ("x", "zh", "y")
    placed = (P(mp, fs, None), P(mp, fs, None), P(mp, fs), P(mp, fs, None))
    return jax.shard_map(
        per_device, mesh=fine, in_specs=placed, out_specs=P(fs, None), check_vma=False
    )
```

```python
import functools

import jax
import jax.numpy as jnp
from jax import lax
from jax.experimental import pallas as pl
from jax.experimental.pallas import tpu as pltpu
from jax.sharding import PartitionSpec as P

F = 7168
SEQS = 2
MESH = pl.DeviceIdType.MESH

smoothing = 0.05


def mp_merge_kernel(prior_ref, w_ref, out_ref, recv_p, recv_w, part, recv2,
                    send_sem, recv_sem, s2_send, s2_recv, s3_send, s3_recv):
    c = lax.axis_index("c")
    z = lax.axis_index("zl")
    rows = prior_ref.shape[0]
    half, quarter = rows // 2, rows // 4
    nb = s2_send.shape[0]
    blk = quarter // nb
    step = 32
    core = {"c": 1 - c}
    chip = {"zl": 1 - z}

    barrier = pltpu.get_barrier_semaphore()
    pl.semaphore_signal(barrier, 1, device_id=core, device_id_type=MESH)
    pl.semaphore_signal(barrier, 1, device_id=chip, device_id_type=MESH)
    pl.semaphore_wait(barrier, 2)

    mine = pl.multiple_of(c * half, half)
    other = pl.multiple_of((1 - c) * half, half)
    my_q = pl.multiple_of(z * quarter, quarter)
    far_q = pl.multiple_of((1 - z) * quarter, quarter)

    def onchip(k, q):
        cp = pltpu.make_async_remote_copy(
            src_ref=prior_ref.at[pl.ds(other + q, quarter)], dst_ref=recv_p.at[pl.ds(q, quarter)],
            send_sem=send_sem.at[k], recv_sem=recv_sem.at[k], device_id=core, device_id_type=MESH)
        cw = pltpu.make_async_remote_copy(
            src_ref=w_ref.at[pl.ds(other + q, quarter)], dst_ref=recv_w.at[pl.ds(q, quarter)],
            send_sem=send_sem.at[2 + k], recv_sem=recv_sem.at[2 + k], device_id=core,
            device_id_type=MESH)
        return [cw, cp]

    far_in = onchip(0, far_q)
    near_in = onchip(1, my_q)
    for cp in far_in + near_in:
        cp.start()

    def add(lo, count):
        def body(i, carry):
            r = pl.multiple_of(lo + i * step, step)
            p_me = prior_ref[pl.ds(mine + r, step)]
            p_ot = recv_p[pl.ds(r, step)]
            n_me = p_me * w_ref[pl.ds(mine + r, step)].astype(jnp.float32)
            n_ot = p_ot * recv_w[pl.ds(r, step)].astype(jnp.float32)
            part[0, pl.ds(r, step)] = n_ot + n_me
            part[1, pl.ds(r, step)] = p_ot + p_me
            return carry

        lax.fori_loop(0, count // step, body, 0)

    def second(b, lo):
        return pltpu.make_async_remote_copy(
            src_ref=part.at[:, pl.ds(lo + b * blk, blk)], dst_ref=recv2.at[:, pl.ds(b * blk, blk)],
            send_sem=s2_send.at[b], recv_sem=s2_recv.at[b], device_id=chip, device_id_type=MESH)

    def third(b, q):
        rows_b = pl.ds(mine + q + b * blk, blk)
        return pltpu.make_async_remote_copy(
            src_ref=out_ref.at[rows_b], dst_ref=out_ref.at[rows_b],
            send_sem=s3_send.at[b], recv_sem=s3_recv.at[b], device_id=chip, device_id_type=MESH)

    for cp in far_in:
        cp.wait_recv()
    sent2 = []
    for b in range(nb):
        add(far_q + b * blk, blk)
        cp = second(b, far_q)
        cp.start()
        sent2.append(cp)
    for cp in near_in:
        cp.wait_recv()
    add(my_q, quarter)

    sent3 = []
    for b in range(nb):
        second(b, my_q).wait_recv()

        def merge(i, carry):
            r = pl.multiple_of(b * blk + i * step, step)
            n = part[0, pl.ds(my_q + r, step)] + recv2[0, pl.ds(r, step)]
            d = part[1, pl.ds(my_q + r, step)] + recv2[1, pl.ds(r, step)]
            out_ref[pl.ds(mine + my_q + r, step)] = (n / d).astype(out_ref.dtype)
            return carry

        lax.fori_loop(0, blk // step, merge, 0)
        cp = third(b, my_q)
        cp.start()
        sent3.append(cp)
    for b in range(nb):
        third(b, far_q).wait_recv()
    fourth = pltpu.make_async_remote_copy(
        src_ref=out_ref.at[pl.ds(mine, half)], dst_ref=out_ref.at[pl.ds(mine, half)],
        send_sem=send_sem.at[4], recv_sem=recv_sem.at[4], device_id=core, device_id_type=MESH)
    fourth.start()
    pltpu.make_async_remote_copy(
        src_ref=out_ref.at[pl.ds(other, half)], dst_ref=out_ref.at[pl.ds(other, half)],
        send_sem=send_sem.at[4], recv_sem=recv_sem.at[4], device_id=core, device_id_type=MESH).wait_recv()
    for cp in far_in + near_in + sent2 + sent3 + [fourth]:
        cp.wait_send()


def mp_merge(prior, w, cid, blocks=4):
    rows, cols = prior.shape
    vmem = pltpu.MemorySpace.VMEM
    return pl.pallas_call(
        mp_merge_kernel,
        out_shape=jax.ShapeDtypeStruct((rows, cols), jnp.bfloat16),
        in_specs=[pl.BlockSpec(memory_space=vmem)] * 2,
        out_specs=pl.BlockSpec(memory_space=vmem),
        scratch_shapes=[
            pltpu.VMEM((rows // 2, cols), jnp.float32),
            pltpu.VMEM((rows // 2, cols), w.dtype),
            pltpu.VMEM((2, rows // 2, cols), jnp.float32),
            pltpu.VMEM((2, rows // 4, cols), jnp.float32),
            pltpu.SemaphoreType.DMA((5,)),
            pltpu.SemaphoreType.DMA((5,)),
            pltpu.SemaphoreType.DMA((blocks,)),
            pltpu.SemaphoreType.DMA((blocks,)),
            pltpu.SemaphoreType.DMA((blocks,)),
            pltpu.SemaphoreType.DMA((blocks,)),
        ],
        compiler_params=pltpu.CompilerParams(
            collective_id=cid, has_side_effects=True, vmem_limit_bytes=60 * 1024 * 1024),
        cost_estimate=pl.CostEstimate(flops=rows * cols * 6, bytes_accessed=rows * cols * 12, transcendentals=0),
    )(prior, w)


def ring_copies(axis, me, n, src, slot, sems, base):
    right, left = lax.rem(me + 1, n), lax.rem(me + n - 1, n)
    far = lax.rem(me + 2, n)
    send, recv = sems
    half = src.shape[0] // 2

    def rc(s, d, k, dev):
        return pltpu.make_async_remote_copy(
            src_ref=s, dst_ref=d, send_sem=send.at[base + k], recv_sem=recv.at[base + k],
            device_id={axis: dev}, device_id_type=MESH)

    whole = pl.ds(0, 2 * half)
    lo, hi = pl.ds(0, half), pl.ds(half, half)
    first = [rc(src, slot(me, whole), 0, right), rc(src, slot(me, whole), 1, left)]
    arrive = [rc(src, slot(left, whole), 0, left), rc(src, slot(right, whole), 1, right)]
    relay = [
        rc(slot(right, lo), slot(right, lo), 2, left),
        rc(slot(left, hi), slot(left, hi), 3, right),
    ]
    land = [
        rc(slot(far, lo), slot(far, lo), 2, right),
        rc(slot(far, hi), slot(far, hi), 3, left),
    ]
    return first, arrive, relay, land


def gather_kernel(act_in, grad_in, seq_ref, act_out, grad_out, seq_out, act_ref, grad_ref,
                  send, recv, local, seq_send, seq_recv, p0_send, p0_recv, q0_send, q0_recv):
    nx = 4
    ny = 4
    x = lax.axis_index("x")
    y = lax.axis_index("y")
    zh = lax.axis_index("zh")
    xr, xl = lax.rem(x + 1, nx), lax.rem(x + nx - 1, nx)
    yr, yl = lax.rem(y + 1, ny), lax.rem(y + ny - 1, ny)

    nj = 2 * ny
    j = zh * ny + y
    rw = act_ref.shape[2]
    cw = grad_ref.shape[2]

    def plane(jd):
        return {"zh": jd // ny, "y": lax.rem(jd, ny)}

    barrier = pltpu.get_barrier_semaphore()
    for s in range(1, nj):
        pl.semaphore_signal(barrier, 1, device_id=plane(lax.rem(j + s, nj)), device_id_type=MESH)
    for s in range(1, nx):
        pl.semaphore_signal(barrier, 1, device_id={"x": lax.rem(x + s, nx)}, device_id_type=MESH)
    pl.semaphore_wait(barrier, nj - 1 + nx - 1)

    def act_p0(s, jd, js):
        return pltpu.make_async_remote_copy(
            src_ref=act_in.at[:, pl.ds(pl.multiple_of(jd * rw, 128), rw)], dst_ref=act_ref.at[js],
            send_sem=p0_send.at[s], recv_sem=p0_recv.at[s], device_id=plane(jd),
            device_id_type=MESH)

    def grad_p0(s, xd, xs):
        return pltpu.make_async_remote_copy(
            src_ref=grad_in.at[:, pl.ds(pl.multiple_of(xd * cw, 128), cw)], dst_ref=grad_ref.at[xs],
            send_sem=q0_send.at[s], recv_sem=q0_recv.at[s], device_id={"x": xd},
            device_id_type=MESH)

    p0_out = [act_p0(s, lax.rem(j + s, nj), j) for s in range(1, nj)]
    p0_in = [act_p0(s, j, lax.rem(j + nj - s, nj)) for s in range(1, nj)]
    q0_out = [grad_p0(s, lax.rem(x + s, nx), x) for s in range(1, nx)]
    q0_in = [grad_p0(s, x, lax.rem(x + nx - s, nx)) for s in range(1, nx)]
    own0 = [
        pltpu.make_async_copy(
            act_in.at[:, pl.ds(pl.multiple_of(j * rw, 128), rw)], act_ref.at[j], local.at[3]),
        pltpu.make_async_copy(
            grad_in.at[:, pl.ds(pl.multiple_of(x * cw, 128), cw)], grad_ref.at[x], local.at[4]),
    ]
    for c in own0 + q0_out + p0_out:
        c.start()
    for c in q0_in:
        c.wait_recv()
    own0[1].wait()

    sems = (send, recv)
    a_first, a_arrive, a_relay, a_land = ring_copies(
        "x", x, nx, act_ref, lambda i, p: act_out.at[i, p], sems, 0)
    g_first, g_arrive, g_relay, g_land = ring_copies(
        "y", y, ny, grad_ref, lambda i, p: grad_out.at[p, zh, i], sems, 4)
    p_first, p_arrive, p_relay, p_land = ring_copies(
        "y", y, ny, grad_out.at[:, 1 - zh, y], lambda i, p: grad_out.at[p, 1 - zh, i], sems, 8)
    swap = pltpu.make_async_remote_copy(
        src_ref=grad_ref, dst_ref=grad_out.at[:, zh, y], send_sem=send.at[12],
        recv_sem=recv.at[12], device_id={"zh": 1 - zh}, device_id_type=MESH)
    swap_in = pltpu.make_async_remote_copy(
        src_ref=grad_ref, dst_ref=grad_out.at[:, 1 - zh, y], send_sem=send.at[12],
        recv_sem=recv.at[12], device_id={"zh": 1 - zh}, device_id_type=MESH)

    own = [
        pltpu.make_async_copy(act_ref, act_out.at[x], local.at[0]),
        pltpu.make_async_copy(grad_ref, grad_out.at[:, zh, y], local.at[1]),
        pltpu.make_async_copy(seq_ref, seq_out.at[x], local.at[2]),
    ]

    def sc(s, d, k, dev):
        return pltpu.make_async_remote_copy(
            src_ref=s, dst_ref=d, send_sem=seq_send.at[k], recv_sem=seq_recv.at[k],
            device_id={"x": dev}, device_id_type=MESH)

    seq_first = [sc(seq_ref, seq_out.at[x], 0, xr), sc(seq_ref, seq_out.at[x], 1, xl)]

    swap.start()
    for c in g_first + seq_first + [own[1], own[2]]:
        c.start()
    for c in p0_in:
        c.wait_recv()
    own0[0].wait()
    for c in a_first + [own[0]]:
        c.start()
    for c in a_arrive:
        c.wait_recv()
    sc(seq_ref, seq_out.at[xl], 0, xl).wait_recv()
    sc(seq_ref, seq_out.at[xr], 1, xr).wait_recv()
    seq_relay = sc(seq_out.at[xr], seq_out.at[xr], 2, xl)
    seq_relay.start()
    for c in a_relay:
        c.start()
    for c in g_arrive:
        c.wait_recv()
    for c in g_relay:
        c.start()
    swap_in.wait_recv()
    for c in p_first:
        c.start()
    for c in p_arrive:
        c.wait_recv()
    for c in p_relay:
        c.start()
    for c in a_land + g_land + p_land:
        c.wait_recv()
    sc(seq_out.at[lax.rem(x + 2, nx)], seq_out.at[lax.rem(x + 2, nx)], 2, xr).wait_recv()
    for c in a_first + a_relay + g_first + g_relay + p_first + p_relay + seq_first:
        c.wait_send()
    seq_relay.wait_send()
    swap.wait_send()
    for c in p0_out + q0_out:
        c.wait_send()
    for c in own:
        c.wait()


def gather_all(act, grad, seq, nj, nx, rw, cw):
    tok = act.shape[0]
    any_space = pl.BlockSpec(memory_space=pl.ANY)
    return pl.pallas_call(
        gather_kernel,
        out_shape=(
            jax.ShapeDtypeStruct((nx, nj, tok, rw), act.dtype),
            jax.ShapeDtypeStruct((nx, 2, nj // 2, tok, cw), grad.dtype),
            jax.ShapeDtypeStruct((nx,) + seq.shape, seq.dtype),
            jax.ShapeDtypeStruct((nj, tok, rw), act.dtype),
            jax.ShapeDtypeStruct((nx, tok, cw), grad.dtype),
        ),
        in_specs=[any_space] * 3,
        out_specs=(any_space,) * 5,
        scratch_shapes=[
            pltpu.SemaphoreType.DMA((13,)),
            pltpu.SemaphoreType.DMA((13,)),
            pltpu.SemaphoreType.DMA((5,)),
            pltpu.SemaphoreType.DMA((3,)),
            pltpu.SemaphoreType.DMA((3,)),
            pltpu.SemaphoreType.DMA((nj,)),
            pltpu.SemaphoreType.DMA((nj,)),
            pltpu.SemaphoreType.DMA((nx,)),
            pltpu.SemaphoreType.DMA((nx,)),
        ],
        compiler_params=pltpu.CompilerParams(collective_id=1, has_side_effects=True),
        cost_estimate=pl.CostEstimate(
            flops=0, bytes_accessed=8 * tok * (nj * rw + 2 * nx * cw), transcendentals=0),
    )(act, grad, seq)


def per_device(activations, out_grads, seq_ids, weights):
    nx = lax.axis_size("x")
    nj = lax.axis_size(("zh", "y"))
    tok = activations.shape[1]
    col_width = weights.shape[2]
    row_width = weights.shape[1]
    total = nx * nj * tok
    act_all, grad_all, owners, _, _ = gather_all(
        activations[0], out_grads[0], seq_ids, nj, nx, row_width, col_width)
    act_all = act_all.reshape(total, row_width)
    grad_all = grad_all.reshape(total, col_width)
    first_long = jnp.sum((owners < 1).astype(jnp.int32)) * (total // owners.size) > total // 2

    def part(lo, hi):
        return lax.dot_general(
            act_all[lo:hi], grad_all[lo:hi], (((0,), (0,)), ((), ())),
            preferred_element_type=jnp.float32,
        )

    quarter = total // 4
    head = part(0, quarter)
    mid = part(quarter, 3 * quarter)
    tail = part(3 * quarter, total)
    g0 = jnp.where(first_long, head + mid, head)
    g1 = jnp.where(first_long, tail, mid + tail)
    fisher = g0 * g0 + g1 * g1
    prior = fisher / SEQS + smoothing
    return mp_merge(prior, weights[0], 2)


def solution(mesh):
    assert mesh.shape["mp"] == 4 and mesh.shape["fsdp"] == 32
    fine = jax.sharding.Mesh(
        mesh.devices.reshape(2, 2, 4, 2, 4), ("zl", "c", "x", "zh", "y")
    )
    mp, fs = ("zl", "c"), ("x", "zh", "y")
    placed = (P(mp, fs, None), P(mp, fs, None), P(mp, fs), P(mp, fs, None))
    return jax.shard_map(
        per_device, mesh=fine, in_specs=placed, out_specs=P(fs, None), check_vma=False
    )
```

```python
import functools

import jax
import jax.numpy as jnp
from jax import lax
from jax.experimental import pallas as pl
from jax.experimental.pallas import tpu as pltpu
from jax.sharding import PartitionSpec as P

F = 7168
SEQS = 2
MESH = pl.DeviceIdType.MESH

smoothing = 0.05


def mp_merge_kernel(prior_ref, w_ref, out_ref, recv_p, recv_w, part, recv2,
                    send_sem, recv_sem, s2_send, s2_recv, s3_send, s3_recv):
    c = lax.axis_index("c")
    z = lax.axis_index("zl")
    rows = prior_ref.shape[0]
    half, quarter = rows // 2, rows // 4
    nb = s2_send.shape[0]
    blk = quarter // nb
    step = 32
    core = {"c": 1 - c}
    chip = {"zl": 1 - z}

    barrier = pltpu.get_barrier_semaphore()
    pl.semaphore_signal(barrier, 1, device_id=core, device_id_type=MESH)
    pl.semaphore_signal(barrier, 1, device_id=chip, device_id_type=MESH)
    pl.semaphore_wait(barrier, 2)

    mine = pl.multiple_of(c * half, half)
    other = pl.multiple_of((1 - c) * half, half)
    my_q = pl.multiple_of(z * quarter, quarter)
    far_q = pl.multiple_of((1 - z) * quarter, quarter)

    def onchip(k, q):
        cp = pltpu.make_async_remote_copy(
            src_ref=prior_ref.at[pl.ds(other + q, quarter)], dst_ref=recv_p.at[pl.ds(q, quarter)],
            send_sem=send_sem.at[k], recv_sem=recv_sem.at[k], device_id=core, device_id_type=MESH)
        cw = pltpu.make_async_remote_copy(
            src_ref=w_ref.at[pl.ds(other + q, quarter)], dst_ref=recv_w.at[pl.ds(q, quarter)],
            send_sem=send_sem.at[2 + k], recv_sem=recv_sem.at[2 + k], device_id=core,
            device_id_type=MESH)
        return [cw, cp]

    far_in = onchip(0, far_q)
    near_in = onchip(1, my_q)
    for cp in far_in + near_in:
        cp.start()

    def add(lo, count):
        def body(i, carry):
            r = pl.multiple_of(lo + i * step, step)
            p_me = prior_ref[pl.ds(mine + r, step)]
            p_ot = recv_p[pl.ds(r, step)]
            n_me = p_me * w_ref[pl.ds(mine + r, step)].astype(jnp.float32)
            n_ot = p_ot * recv_w[pl.ds(r, step)].astype(jnp.float32)
            part[0, pl.ds(r, step)] = n_ot + n_me
            part[1, pl.ds(r, step)] = p_ot + p_me
            return carry

        lax.fori_loop(0, count // step, body, 0)

    def second(b, lo):
        return pltpu.make_async_remote_copy(
            src_ref=part.at[:, pl.ds(lo + b * blk, blk)], dst_ref=recv2.at[:, pl.ds(b * blk, blk)],
            send_sem=s2_send.at[b], recv_sem=s2_recv.at[b], device_id=chip, device_id_type=MESH)

    def third(b, q):
        rows_b = pl.ds(mine + q + b * blk, blk)
        return pltpu.make_async_remote_copy(
            src_ref=out_ref.at[rows_b], dst_ref=out_ref.at[rows_b],
            send_sem=s3_send.at[b], recv_sem=s3_recv.at[b], device_id=chip, device_id_type=MESH)

    for cp in far_in:
        cp.wait_recv()
    sent2 = []
    for b in range(nb):
        add(far_q + b * blk, blk)
        cp = second(b, far_q)
        cp.start()
        sent2.append(cp)
    for cp in near_in:
        cp.wait_recv()
    add(my_q, quarter)

    sent3 = []
    for b in range(nb):
        second(b, my_q).wait_recv()

        def merge(i, carry):
            r = pl.multiple_of(b * blk + i * step, step)
            n = part[0, pl.ds(my_q + r, step)] + recv2[0, pl.ds(r, step)]
            d = part[1, pl.ds(my_q + r, step)] + recv2[1, pl.ds(r, step)]
            out_ref[pl.ds(mine + my_q + r, step)] = (n / d).astype(out_ref.dtype)
            return carry

        lax.fori_loop(0, blk // step, merge, 0)
        cp = third(b, my_q)
        cp.start()
        sent3.append(cp)
    for b in range(nb):
        third(b, far_q).wait_recv()
    fourth = pltpu.make_async_remote_copy(
        src_ref=out_ref.at[pl.ds(mine, half)], dst_ref=out_ref.at[pl.ds(mine, half)],
        send_sem=send_sem.at[4], recv_sem=recv_sem.at[4], device_id=core, device_id_type=MESH)
    fourth.start()
    pltpu.make_async_remote_copy(
        src_ref=out_ref.at[pl.ds(other, half)], dst_ref=out_ref.at[pl.ds(other, half)],
        send_sem=send_sem.at[4], recv_sem=recv_sem.at[4], device_id=core, device_id_type=MESH).wait_recv()
    for cp in far_in + near_in + sent2 + sent3 + [fourth]:
        cp.wait_send()


def mp_merge(prior, w, cid, blocks=4):
    rows, cols = prior.shape
    vmem = pltpu.MemorySpace.VMEM
    return pl.pallas_call(
        mp_merge_kernel,
        out_shape=jax.ShapeDtypeStruct((rows, cols), jnp.bfloat16),
        in_specs=[pl.BlockSpec(memory_space=vmem)] * 2,
        out_specs=pl.BlockSpec(memory_space=vmem),
        scratch_shapes=[
            pltpu.VMEM((rows // 2, cols), jnp.float32),
            pltpu.VMEM((rows // 2, cols), w.dtype),
            pltpu.VMEM((2, rows // 2, cols), jnp.float32),
            pltpu.VMEM((2, rows // 4, cols), jnp.float32),
            pltpu.SemaphoreType.DMA((5,)),
            pltpu.SemaphoreType.DMA((5,)),
            pltpu.SemaphoreType.DMA((blocks,)),
            pltpu.SemaphoreType.DMA((blocks,)),
            pltpu.SemaphoreType.DMA((blocks,)),
            pltpu.SemaphoreType.DMA((blocks,)),
        ],
        compiler_params=pltpu.CompilerParams(
            collective_id=cid, has_side_effects=True, vmem_limit_bytes=60 * 1024 * 1024),
        cost_estimate=pl.CostEstimate(flops=rows * cols * 6, bytes_accessed=rows * cols * 12, transcendentals=0),
    )(prior, w)


def ring_copies(axis, me, n, src, slot, sems, base):
    right, left = lax.rem(me + 1, n), lax.rem(me + n - 1, n)
    far = lax.rem(me + 2, n)
    send, recv = sems
    half = src.shape[0] // 2

    def rc(s, d, k, dev):
        return pltpu.make_async_remote_copy(
            src_ref=s, dst_ref=d, send_sem=send.at[base + k], recv_sem=recv.at[base + k],
            device_id={axis: dev}, device_id_type=MESH)

    whole = pl.ds(0, 2 * half)
    lo, hi = pl.ds(0, half), pl.ds(half, half)
    first = [rc(src, slot(me, whole), 0, right), rc(src, slot(me, whole), 1, left)]
    arrive = [rc(src, slot(left, whole), 0, left), rc(src, slot(right, whole), 1, right)]
    relay = [
        rc(slot(right, lo), slot(right, lo), 2, left),
        rc(slot(left, hi), slot(left, hi), 3, right),
    ]
    land = [
        rc(slot(far, lo), slot(far, lo), 2, right),
        rc(slot(far, hi), slot(far, hi), 3, left),
    ]
    return first, arrive, relay, land


def gather_kernel(act_in, grad_in, seq_ref, act_out, grad_out, seq_out, act_ref, grad_ref,
                  send, recv, local, seq_send, seq_recv, p0_send, p0_recv, q0_send, q0_recv,
                  z_send, z_recv):
    nx = 4
    ny = 4
    x = lax.axis_index("x")
    y = lax.axis_index("y")
    zh = lax.axis_index("zh")
    xr, xl = lax.rem(x + 1, nx), lax.rem(x + nx - 1, nx)
    yr, yl = lax.rem(y + 1, ny), lax.rem(y + ny - 1, ny)

    nj = 2 * ny
    j = zh * ny + y
    rw = act_ref.shape[2]
    cw = grad_ref.shape[2]

    def plane(jd):
        return {"zh": jd // ny, "y": lax.rem(jd, ny)}

    barrier = pltpu.get_barrier_semaphore()
    for s in range(1, nj):
        pl.semaphore_signal(barrier, 1, device_id=plane(lax.rem(j + s, nj)), device_id_type=MESH)
    for s in range(1, nx):
        pl.semaphore_signal(barrier, 1, device_id={"x": lax.rem(x + s, nx)}, device_id_type=MESH)
    pl.semaphore_wait(barrier, nj - 1 + nx - 1)

    def act_p0(s, jd, js):
        return pltpu.make_async_remote_copy(
            src_ref=act_in.at[:, pl.ds(pl.multiple_of(jd * rw, 128), rw)], dst_ref=act_ref.at[js],
            send_sem=p0_send.at[s], recv_sem=p0_recv.at[s], device_id=plane(jd),
            device_id_type=MESH)

    def grad_p0(s, xd, xs):
        return pltpu.make_async_remote_copy(
            src_ref=grad_in.at[:, pl.ds(pl.multiple_of(xd * cw, 128), cw)], dst_ref=grad_ref.at[xs],
            send_sem=q0_send.at[s], recv_sem=q0_recv.at[s], device_id={"x": xd},
            device_id_type=MESH)

    p0_out = [act_p0(s, lax.rem(j + s, nj), j) for s in range(1, nj)]
    p0_in = [act_p0(s, j, lax.rem(j + nj - s, nj)) for s in range(1, nj)]
    q0_out = [grad_p0(s, lax.rem(x + s, nx), x) for s in range(1, nx)]
    q0_in = [grad_p0(s, x, lax.rem(x + nx - s, nx)) for s in range(1, nx)]
    own0 = [
        pltpu.make_async_copy(
            act_in.at[:, pl.ds(pl.multiple_of(j * rw, 128), rw)], act_ref.at[j], local.at[3]),
        pltpu.make_async_copy(
            grad_in.at[:, pl.ds(pl.multiple_of(x * cw, 128), cw)], grad_ref.at[x], local.at[4]),
    ]
    def zs(s, src_block, xs, zs_):
        return pltpu.make_async_remote_copy(
            src_ref=src_block, dst_ref=grad_out.at[xs, zs_, y], send_sem=z_send.at[s],
            recv_sem=z_recv.at[s], device_id={"zh": 1 - zh}, device_id_type=MESH)

    own_cols = grad_in.at[:, pl.ds(pl.multiple_of(x * cw, 128), cw)]
    swap_out = [zs(0, own_cols, x, zh)]
    swap_in = [zs(s, own_cols, lax.rem(x + nx - s, nx), 1 - zh) for s in range(nx)]
    swap_out[0].start()
    for c in own0 + q0_out + p0_out:
        c.start()
    for s, c in enumerate(q0_in, start=1):
        c.wait_recv()
        xs = lax.rem(x + nx - s, nx)
        piece = zs(s, grad_ref.at[xs], xs, zh)
        piece.start()
        swap_out.append(piece)
    own0[1].wait()

    sems = (send, recv)
    a_first, a_arrive, a_relay, a_land = ring_copies(
        "x", x, nx, act_ref, lambda i, p: act_out.at[i, p], sems, 0)
    g_first, g_arrive, g_relay, g_land = ring_copies(
        "y", y, ny, grad_ref, lambda i, p: grad_out.at[p, zh, i], sems, 4)
    p_first, p_arrive, p_relay, p_land = ring_copies(
        "y", y, ny, grad_out.at[:, 1 - zh, y], lambda i, p: grad_out.at[p, 1 - zh, i], sems, 8)

    own = [
        pltpu.make_async_copy(act_ref, act_out.at[x], local.at[0]),
        pltpu.make_async_copy(grad_ref, grad_out.at[:, zh, y], local.at[1]),
        pltpu.make_async_copy(seq_ref, seq_out.at[x], local.at[2]),
    ]

    def sc(s, d, k, dev):
        return pltpu.make_async_remote_copy(
            src_ref=s, dst_ref=d, send_sem=seq_send.at[k], recv_sem=seq_recv.at[k],
            device_id={"x": dev}, device_id_type=MESH)

    seq_first = [sc(seq_ref, seq_out.at[x], 0, xr), sc(seq_ref, seq_out.at[x], 1, xl)]

    for c in g_first + seq_first + [own[1], own[2]]:
        c.start()
    for c in p0_in:
        c.wait_recv()
    own0[0].wait()
    for c in a_first + [own[0]]:
        c.start()
    for c in a_arrive:
        c.wait_recv()
    sc(seq_ref, seq_out.at[xl], 0, xl).wait_recv()
    sc(seq_ref, seq_out.at[xr], 1, xr).wait_recv()
    seq_relay = sc(seq_out.at[xr], seq_out.at[xr], 2, xl)
    seq_relay.start()
    for c in a_relay:
        c.start()
    for c in g_arrive:
        c.wait_recv()
    for c in g_relay:
        c.start()
    for c in swap_in:
        c.wait_recv()
    for c in p_first:
        c.start()
    for c in p_arrive:
        c.wait_recv()
    for c in p_relay:
        c.start()
    for c in a_land + g_land + p_land:
        c.wait_recv()
    sc(seq_out.at[lax.rem(x + 2, nx)], seq_out.at[lax.rem(x + 2, nx)], 2, xr).wait_recv()
    for c in a_first + a_relay + g_first + g_relay + p_first + p_relay + seq_first:
        c.wait_send()
    seq_relay.wait_send()
    for c in swap_out:
        c.wait_send()
    for c in p0_out + q0_out:
        c.wait_send()
    for c in own:
        c.wait()


def gather_all(act, grad, seq, nj, nx, rw, cw):
    tok = act.shape[0]
    any_space = pl.BlockSpec(memory_space=pl.ANY)
    return pl.pallas_call(
        gather_kernel,
        out_shape=(
            jax.ShapeDtypeStruct((nx, nj, tok, rw), act.dtype),
            jax.ShapeDtypeStruct((nx, 2, nj // 2, tok, cw), grad.dtype),
            jax.ShapeDtypeStruct((nx,) + seq.shape, seq.dtype),
            jax.ShapeDtypeStruct((nj, tok, rw), act.dtype),
            jax.ShapeDtypeStruct((nx, tok, cw), grad.dtype),
        ),
        in_specs=[any_space] * 3,
        out_specs=(any_space,) * 5,
        scratch_shapes=[
            pltpu.SemaphoreType.DMA((13,)),
            pltpu.SemaphoreType.DMA((13,)),
            pltpu.SemaphoreType.DMA((5,)),
            pltpu.SemaphoreType.DMA((3,)),
            pltpu.SemaphoreType.DMA((3,)),
            pltpu.SemaphoreType.DMA((nj,)),
            pltpu.SemaphoreType.DMA((nj,)),
            pltpu.SemaphoreType.DMA((nx,)),
            pltpu.SemaphoreType.DMA((nx,)),
            pltpu.SemaphoreType.DMA((nx,)),
            pltpu.SemaphoreType.DMA((nx,)),
        ],
        compiler_params=pltpu.CompilerParams(collective_id=1, has_side_effects=True),
        cost_estimate=pl.CostEstimate(
            flops=0, bytes_accessed=8 * tok * (nj * rw + 2 * nx * cw), transcendentals=0),
    )(act, grad, seq)


def per_device(activations, out_grads, seq_ids, weights):
    nx = lax.axis_size("x")
    nj = lax.axis_size(("zh", "y"))
    tok = activations.shape[1]
    col_width = weights.shape[2]
    row_width = weights.shape[1]
    total = nx * nj * tok
    act_all, grad_all, owners, _, _ = gather_all(
        activations[0], out_grads[0], seq_ids, nj, nx, row_width, col_width)
    act_all = act_all.reshape(total, row_width)
    grad_all = grad_all.reshape(total, col_width)
    first_long = jnp.sum((owners < 1).astype(jnp.int32)) * (total // owners.size) > total // 2

    def part(lo, hi):
        return lax.dot_general(
            act_all[lo:hi], grad_all[lo:hi], (((0,), (0,)), ((), ())),
            preferred_element_type=jnp.float32,
        )

    quarter = total // 4
    head = part(0, quarter)
    mid = part(quarter, 3 * quarter)
    tail = part(3 * quarter, total)
    g0 = jnp.where(first_long, head + mid, head)
    g1 = jnp.where(first_long, tail, mid + tail)
    fisher = g0 * g0 + g1 * g1
    prior = fisher / SEQS + smoothing
    return mp_merge(prior, weights[0], 2)


def solution(mesh):
    assert mesh.shape["mp"] == 4 and mesh.shape["fsdp"] == 32
    fine = jax.sharding.Mesh(
        mesh.devices.reshape(2, 2, 4, 2, 4), ("zl", "c", "x", "zh", "y")
    )
    mp, fs = ("zl", "c"), ("x", "zh", "y")
    placed = (P(mp, fs, None), P(mp, fs, None), P(mp, fs), P(mp, fs, None))
    return jax.shard_map(
        per_device, mesh=fine, in_specs=placed, out_specs=P(fs, None), check_vma=False
    )
```

```python
import functools

import jax
import jax.numpy as jnp
from jax import lax
from jax.experimental import pallas as pl
from jax.experimental.pallas import tpu as pltpu
from jax.sharding import PartitionSpec as P

F = 7168
SEQS = 2
MESH = pl.DeviceIdType.MESH

smoothing = 0.05


def mp_merge_kernel(prior_ref, w_ref, out_ref, recv_p, recv_w, part, recv2,
                    send_sem, recv_sem, s2_send, s2_recv, s3_send, s3_recv, f_send, f_recv):
    c = lax.axis_index("c")
    z = lax.axis_index("zl")
    rows = prior_ref.shape[0]
    half, quarter = rows // 2, rows // 4
    nb = s2_send.shape[0]
    blk = quarter // nb
    step = 32
    core = {"c": 1 - c}
    chip = {"zl": 1 - z}

    barrier = pltpu.get_barrier_semaphore()
    pl.semaphore_signal(barrier, 1, device_id=core, device_id_type=MESH)
    pl.semaphore_signal(barrier, 1, device_id=chip, device_id_type=MESH)
    pl.semaphore_wait(barrier, 2)

    mine = pl.multiple_of(c * half, half)
    other = pl.multiple_of((1 - c) * half, half)
    my_q = pl.multiple_of(z * quarter, quarter)
    far_q = pl.multiple_of((1 - z) * quarter, quarter)

    def onchip(k, q):
        cp = pltpu.make_async_remote_copy(
            src_ref=prior_ref.at[pl.ds(other + q, quarter)], dst_ref=recv_p.at[pl.ds(q, quarter)],
            send_sem=send_sem.at[k], recv_sem=recv_sem.at[k], device_id=core, device_id_type=MESH)
        cw = pltpu.make_async_remote_copy(
            src_ref=w_ref.at[pl.ds(other + q, quarter)], dst_ref=recv_w.at[pl.ds(q, quarter)],
            send_sem=send_sem.at[2 + k], recv_sem=recv_sem.at[2 + k], device_id=core,
            device_id_type=MESH)
        return [cw, cp]

    def onchip_block(b):
        rows_b = pl.ds(far_q + b * blk, blk)
        cp = pltpu.make_async_remote_copy(
            src_ref=prior_ref.at[pl.ds(other + far_q + b * blk, blk)], dst_ref=recv_p.at[rows_b],
            send_sem=f_send.at[b], recv_sem=f_recv.at[b], device_id=core, device_id_type=MESH)
        cw = pltpu.make_async_remote_copy(
            src_ref=w_ref.at[pl.ds(other + far_q + b * blk, blk)], dst_ref=recv_w.at[rows_b],
            send_sem=f_send.at[nb + b], recv_sem=f_recv.at[nb + b], device_id=core,
            device_id_type=MESH)
        return [cw, cp]

    far_in = [onchip_block(b) for b in range(nb)]
    near_in = onchip(1, my_q)
    for pair in far_in:
        for cp in pair:
            cp.start()
    for cp in near_in:
        cp.start()

    def add(lo, count):
        def body(i, carry):
            r = pl.multiple_of(lo + i * step, step)
            p_me = prior_ref[pl.ds(mine + r, step)]
            p_ot = recv_p[pl.ds(r, step)]
            n_me = p_me * w_ref[pl.ds(mine + r, step)].astype(jnp.float32)
            n_ot = p_ot * recv_w[pl.ds(r, step)].astype(jnp.float32)
            part[0, pl.ds(r, step)] = n_ot + n_me
            part[1, pl.ds(r, step)] = p_ot + p_me
            return carry

        lax.fori_loop(0, count // step, body, 0)

    def second(b, lo):
        return pltpu.make_async_remote_copy(
            src_ref=part.at[:, pl.ds(lo + b * blk, blk)], dst_ref=recv2.at[:, pl.ds(b * blk, blk)],
            send_sem=s2_send.at[b], recv_sem=s2_recv.at[b], device_id=chip, device_id_type=MESH)

    def third(b, q):
        rows_b = pl.ds(mine + q + b * blk, blk)
        return pltpu.make_async_remote_copy(
            src_ref=out_ref.at[rows_b], dst_ref=out_ref.at[rows_b],
            send_sem=s3_send.at[b], recv_sem=s3_recv.at[b], device_id=chip, device_id_type=MESH)

    sent2 = []
    for b in range(nb):
        for cp in far_in[b]:
            cp.wait_recv()
        add(far_q + b * blk, blk)
        cp = second(b, far_q)
        cp.start()
        sent2.append(cp)
    for cp in near_in:
        cp.wait_recv()
    add(my_q, quarter)

    sent3 = []
    for b in range(nb):
        second(b, my_q).wait_recv()

        def merge(i, carry):
            r = pl.multiple_of(b * blk + i * step, step)
            n = part[0, pl.ds(my_q + r, step)] + recv2[0, pl.ds(r, step)]
            d = part[1, pl.ds(my_q + r, step)] + recv2[1, pl.ds(r, step)]
            out_ref[pl.ds(mine + my_q + r, step)] = (n / d).astype(out_ref.dtype)
            return carry

        lax.fori_loop(0, blk // step, merge, 0)
        cp = third(b, my_q)
        cp.start()
        sent3.append(cp)
    for b in range(nb):
        third(b, far_q).wait_recv()
    fourth = pltpu.make_async_remote_copy(
        src_ref=out_ref.at[pl.ds(mine, half)], dst_ref=out_ref.at[pl.ds(mine, half)],
        send_sem=send_sem.at[4], recv_sem=recv_sem.at[4], device_id=core, device_id_type=MESH)
    fourth.start()
    pltpu.make_async_remote_copy(
        src_ref=out_ref.at[pl.ds(other, half)], dst_ref=out_ref.at[pl.ds(other, half)],
        send_sem=send_sem.at[4], recv_sem=recv_sem.at[4], device_id=core, device_id_type=MESH).wait_recv()
    for cp in sum(far_in, []) + near_in + sent2 + sent3 + [fourth]:
        cp.wait_send()


def mp_merge(prior, w, cid, blocks=8):
    rows, cols = prior.shape
    vmem = pltpu.MemorySpace.VMEM
    return pl.pallas_call(
        mp_merge_kernel,
        out_shape=jax.ShapeDtypeStruct((rows, cols), jnp.bfloat16),
        in_specs=[pl.BlockSpec(memory_space=vmem)] * 2,
        out_specs=pl.BlockSpec(memory_space=vmem),
        scratch_shapes=[
            pltpu.VMEM((rows // 2, cols), jnp.float32),
            pltpu.VMEM((rows // 2, cols), w.dtype),
            pltpu.VMEM((2, rows // 2, cols), jnp.float32),
            pltpu.VMEM((2, rows // 4, cols), jnp.float32),
            pltpu.SemaphoreType.DMA((5,)),
            pltpu.SemaphoreType.DMA((5,)),
            pltpu.SemaphoreType.DMA((blocks,)),
            pltpu.SemaphoreType.DMA((blocks,)),
            pltpu.SemaphoreType.DMA((blocks,)),
            pltpu.SemaphoreType.DMA((blocks,)),
            pltpu.SemaphoreType.DMA((2 * blocks,)),
            pltpu.SemaphoreType.DMA((2 * blocks,)),
        ],
        compiler_params=pltpu.CompilerParams(
            collective_id=cid, has_side_effects=True, vmem_limit_bytes=60 * 1024 * 1024),
        cost_estimate=pl.CostEstimate(flops=rows * cols * 6, bytes_accessed=rows * cols * 12, transcendentals=0),
    )(prior, w)


def ring_copies(axis, me, n, src, slot, sems, base):
    right, left = lax.rem(me + 1, n), lax.rem(me + n - 1, n)
    far = lax.rem(me + 2, n)
    send, recv = sems
    half = src.shape[0] // 2

    def rc(s, d, k, dev):
        return pltpu.make_async_remote_copy(
            src_ref=s, dst_ref=d, send_sem=send.at[base + k], recv_sem=recv.at[base + k],
            device_id={axis: dev}, device_id_type=MESH)

    whole = pl.ds(0, 2 * half)
    lo, hi = pl.ds(0, half), pl.ds(half, half)
    first = [rc(src, slot(me, whole), 0, right), rc(src, slot(me, whole), 1, left)]
    arrive = [rc(src, slot(left, whole), 0, left), rc(src, slot(right, whole), 1, right)]
    relay = [
        rc(slot(right, lo), slot(right, lo), 2, left),
        rc(slot(left, hi), slot(left, hi), 3, right),
    ]
    land = [
        rc(slot(far, lo), slot(far, lo), 2, right),
        rc(slot(far, hi), slot(far, hi), 3, left),
    ]
    return first, arrive, relay, land


def gather_kernel(act_in, grad_in, seq_ref, act_out, grad_out, seq_out, act_ref, grad_ref,
                  send, recv, local, seq_send, seq_recv, p0_send, p0_recv, q0_send, q0_recv):
    nx = 4
    ny = 4
    x = lax.axis_index("x")
    y = lax.axis_index("y")
    zh = lax.axis_index("zh")
    xr, xl = lax.rem(x + 1, nx), lax.rem(x + nx - 1, nx)
    yr, yl = lax.rem(y + 1, ny), lax.rem(y + ny - 1, ny)

    nj = 2 * ny
    j = zh * ny + y
    rw = act_ref.shape[2]
    cw = grad_ref.shape[2]

    def plane(jd):
        return {"zh": jd // ny, "y": lax.rem(jd, ny)}

    barrier = pltpu.get_barrier_semaphore()
    for s in range(1, nj):
        pl.semaphore_signal(barrier, 1, device_id=plane(lax.rem(j + s, nj)), device_id_type=MESH)
    for s in range(1, nx):
        pl.semaphore_signal(barrier, 1, device_id={"x": lax.rem(x + s, nx)}, device_id_type=MESH)
    pl.semaphore_wait(barrier, nj - 1 + nx - 1)

    def act_p0(s, jd, js):
        return pltpu.make_async_remote_copy(
            src_ref=act_in.at[:, pl.ds(pl.multiple_of(jd * rw, 128), rw)], dst_ref=act_ref.at[js],
            send_sem=p0_send.at[s], recv_sem=p0_recv.at[s], device_id=plane(jd),
            device_id_type=MESH)

    def grad_p0(s, xd, xs):
        return pltpu.make_async_remote_copy(
            src_ref=grad_in.at[:, pl.ds(pl.multiple_of(xd * cw, 128), cw)], dst_ref=grad_ref.at[xs],
            send_sem=q0_send.at[s], recv_sem=q0_recv.at[s], device_id={"x": xd},
            device_id_type=MESH)

    p0_out = [act_p0(s, lax.rem(j + s, nj), j) for s in range(1, nj)]
    p0_in = [act_p0(s, j, lax.rem(j + nj - s, nj)) for s in range(1, nj)]
    q0_out = [grad_p0(s, lax.rem(x + s, nx), x) for s in range(1, nx)]
    q0_in = [grad_p0(s, x, lax.rem(x + nx - s, nx)) for s in range(1, nx)]
    own0 = [
        pltpu.make_async_copy(
            act_in.at[:, pl.ds(pl.multiple_of(j * rw, 128), rw)], act_ref.at[j], local.at[3]),
        pltpu.make_async_copy(
            grad_in.at[:, pl.ds(pl.multiple_of(x * cw, 128), cw)], grad_ref.at[x], local.at[4]),
    ]
    for c in own0 + q0_out + p0_out:
        c.start()
    for c in q0_in:
        c.wait_recv()
    own0[1].wait()

    sems = (send, recv)
    a_first, a_arrive, a_relay, a_land = ring_copies(
        "x", x, nx, act_ref, lambda i, p: act_out.at[i, p], sems, 0)
    g_first, g_arrive, g_relay, g_land = ring_copies(
        "y", y, ny, grad_ref, lambda i, p: grad_out.at[p, zh, i], sems, 4)
    p_first, p_arrive, p_relay, p_land = ring_copies(
        "y", y, ny, grad_out.at[:, 1 - zh, y], lambda i, p: grad_out.at[p, 1 - zh, i], sems, 8)
    swap = pltpu.make_async_remote_copy(
        src_ref=grad_ref, dst_ref=grad_out.at[:, zh, y], send_sem=send.at[12],
        recv_sem=recv.at[12], device_id={"zh": 1 - zh}, device_id_type=MESH)
    swap_in = pltpu.make_async_remote_copy(
        src_ref=grad_ref, dst_ref=grad_out.at[:, 1 - zh, y], send_sem=send.at[12],
        recv_sem=recv.at[12], device_id={"zh": 1 - zh}, device_id_type=MESH)

    own = [
        pltpu.make_async_copy(act_ref, act_out.at[x], local.at[0]),
        pltpu.make_async_copy(grad_ref, grad_out.at[:, zh, y], local.at[1]),
        pltpu.make_async_copy(seq_ref, seq_out.at[x], local.at[2]),
    ]

    def sc(s, d, k, dev):
        return pltpu.make_async_remote_copy(
            src_ref=s, dst_ref=d, send_sem=seq_send.at[k], recv_sem=seq_recv.at[k],
            device_id={"x": dev}, device_id_type=MESH)

    seq_first = [sc(seq_ref, seq_out.at[x], 0, xr), sc(seq_ref, seq_out.at[x], 1, xl)]

    swap.start()
    for c in g_first + seq_first + [own[1], own[2]]:
        c.start()
    for c in p0_in:
        c.wait_recv()
    own0[0].wait()
    for c in a_first + [own[0]]:
        c.start()
    for c in a_arrive:
        c.wait_recv()
    sc(seq_ref, seq_out.at[xl], 0, xl).wait_recv()
    sc(seq_ref, seq_out.at[xr], 1, xr).wait_recv()
    seq_relay = sc(seq_out.at[xr], seq_out.at[xr], 2, xl)
    seq_relay.start()
    for c in a_relay:
        c.start()
    for c in g_arrive:
        c.wait_recv()
    for c in g_relay:
        c.start()
    swap_in.wait_recv()
    for c in p_first:
        c.start()
    for c in p_arrive:
        c.wait_recv()
    for c in p_relay:
        c.start()
    for c in a_land + g_land + p_land:
        c.wait_recv()
    sc(seq_out.at[lax.rem(x + 2, nx)], seq_out.at[lax.rem(x + 2, nx)], 2, xr).wait_recv()
    for c in a_first + a_relay + g_first + g_relay + p_first + p_relay + seq_first:
        c.wait_send()
    seq_relay.wait_send()
    swap.wait_send()
    for c in p0_out + q0_out:
        c.wait_send()
    for c in own:
        c.wait()


def gather_all(act, grad, seq, nj, nx, rw, cw):
    tok = act.shape[0]
    any_space = pl.BlockSpec(memory_space=pl.ANY)
    return pl.pallas_call(
        gather_kernel,
        out_shape=(
            jax.ShapeDtypeStruct((nx, nj, tok, rw), act.dtype),
            jax.ShapeDtypeStruct((nx, 2, nj // 2, tok, cw), grad.dtype),
            jax.ShapeDtypeStruct((nx,) + seq.shape, seq.dtype),
            jax.ShapeDtypeStruct((nj, tok, rw), act.dtype),
            jax.ShapeDtypeStruct((nx, tok, cw), grad.dtype),
        ),
        in_specs=[any_space] * 3,
        out_specs=(any_space,) * 5,
        scratch_shapes=[
            pltpu.SemaphoreType.DMA((13,)),
            pltpu.SemaphoreType.DMA((13,)),
            pltpu.SemaphoreType.DMA((5,)),
            pltpu.SemaphoreType.DMA((3,)),
            pltpu.SemaphoreType.DMA((3,)),
            pltpu.SemaphoreType.DMA((nj,)),
            pltpu.SemaphoreType.DMA((nj,)),
            pltpu.SemaphoreType.DMA((nx,)),
            pltpu.SemaphoreType.DMA((nx,)),
        ],
        compiler_params=pltpu.CompilerParams(collective_id=1, has_side_effects=True),
        cost_estimate=pl.CostEstimate(
            flops=0, bytes_accessed=8 * tok * (nj * rw + 2 * nx * cw), transcendentals=0),
    )(act, grad, seq)


def per_device(activations, out_grads, seq_ids, weights):
    nx = lax.axis_size("x")
    nj = lax.axis_size(("zh", "y"))
    tok = activations.shape[1]
    col_width = weights.shape[2]
    row_width = weights.shape[1]
    total = nx * nj * tok
    act_all, grad_all, owners, _, _ = gather_all(
        activations[0], out_grads[0], seq_ids, nj, nx, row_width, col_width)
    act_all = act_all.reshape(total, row_width)
    grad_all = grad_all.reshape(total, col_width)
    first_long = jnp.sum((owners < 1).astype(jnp.int32)) * (total // owners.size) > total // 2

    def part(lo, hi):
        return lax.dot_general(
            act_all[lo:hi], grad_all[lo:hi], (((0,), (0,)), ((), ())),
            preferred_element_type=jnp.float32,
        )

    quarter = total // 4
    head = part(0, quarter)
    mid = part(quarter, 3 * quarter)
    tail = part(3 * quarter, total)
    g0 = jnp.where(first_long, head + mid, head)
    g1 = jnp.where(first_long, tail, mid + tail)
    fisher = g0 * g0 + g1 * g1
    prior = fisher / SEQS + smoothing
    return mp_merge(prior, weights[0], 2)


def solution(mesh):
    assert mesh.shape["mp"] == 4 and mesh.shape["fsdp"] == 32
    fine = jax.sharding.Mesh(
        mesh.devices.reshape(2, 2, 4, 2, 4), ("zl", "c", "x", "zh", "y")
    )
    mp, fs = ("zl", "c"), ("x", "zh", "y")
    placed = (P(mp, fs, None), P(mp, fs, None), P(mp, fs), P(mp, fs, None))
    return jax.shard_map(
        per_device, mesh=fine, in_specs=placed, out_specs=P(fs, None), check_vma=False
    )
```

```python
import functools

import jax
import jax.numpy as jnp
from jax import lax
from jax.experimental import pallas as pl
from jax.experimental.pallas import tpu as pltpu
from jax.sharding import PartitionSpec as P

F = 7168
SEQS = 2
MESH = pl.DeviceIdType.MESH

smoothing = 0.05


def mp_merge_kernel(prior_ref, w_ref, out_ref, recv_p, recv_w, part, recv2,
                    send_sem, recv_sem, s2_send, s2_recv, s3_send, s3_recv, f_send, f_recv,
                    t_send, t_recv):
    c = lax.axis_index("c")
    z = lax.axis_index("zl")
    rows = prior_ref.shape[0]
    half, quarter = rows // 2, rows // 4
    nb = s2_send.shape[0]
    blk = quarter // nb
    step = 32
    core = {"c": 1 - c}
    chip = {"zl": 1 - z}

    barrier = pltpu.get_barrier_semaphore()
    pl.semaphore_signal(barrier, 1, device_id=core, device_id_type=MESH)
    pl.semaphore_signal(barrier, 1, device_id=chip, device_id_type=MESH)
    pl.semaphore_wait(barrier, 2)

    mine = pl.multiple_of(c * half, half)
    other = pl.multiple_of((1 - c) * half, half)
    my_q = pl.multiple_of(z * quarter, quarter)
    far_q = pl.multiple_of((1 - z) * quarter, quarter)

    def onchip(k, q):
        cp = pltpu.make_async_remote_copy(
            src_ref=prior_ref.at[pl.ds(other + q, quarter)], dst_ref=recv_p.at[pl.ds(q, quarter)],
            send_sem=send_sem.at[k], recv_sem=recv_sem.at[k], device_id=core, device_id_type=MESH)
        cw = pltpu.make_async_remote_copy(
            src_ref=w_ref.at[pl.ds(other + q, quarter)], dst_ref=recv_w.at[pl.ds(q, quarter)],
            send_sem=send_sem.at[2 + k], recv_sem=recv_sem.at[2 + k], device_id=core,
            device_id_type=MESH)
        return [cw, cp]

    def onchip_block(b):
        rows_b = pl.ds(far_q + b * blk, blk)
        cp = pltpu.make_async_remote_copy(
            src_ref=prior_ref.at[pl.ds(other + far_q + b * blk, blk)], dst_ref=recv_p.at[rows_b],
            send_sem=f_send.at[b], recv_sem=f_recv.at[b], device_id=core, device_id_type=MESH)
        cw = pltpu.make_async_remote_copy(
            src_ref=w_ref.at[pl.ds(other + far_q + b * blk, blk)], dst_ref=recv_w.at[rows_b],
            send_sem=f_send.at[nb + b], recv_sem=f_recv.at[nb + b], device_id=core,
            device_id_type=MESH)
        return [cw, cp]

    far_in = [onchip_block(b) for b in range(nb)]
    near_in = onchip(1, my_q)
    for pair in far_in:
        for cp in pair:
            cp.start()
    for cp in near_in:
        cp.start()

    def add(lo, count):
        def body(i, carry):
            r = pl.multiple_of(lo + i * step, step)
            p_me = prior_ref[pl.ds(mine + r, step)]
            p_ot = recv_p[pl.ds(r, step)]
            n_me = p_me * w_ref[pl.ds(mine + r, step)].astype(jnp.float32)
            n_ot = p_ot * recv_w[pl.ds(r, step)].astype(jnp.float32)
            part[0, pl.ds(r, step)] = n_ot + n_me
            part[1, pl.ds(r, step)] = p_ot + p_me
            return carry

        lax.fori_loop(0, count // step, body, 0)

    def second(b, lo):
        return pltpu.make_async_remote_copy(
            src_ref=part.at[:, pl.ds(lo + b * blk, blk)], dst_ref=recv2.at[:, pl.ds(b * blk, blk)],
            send_sem=s2_send.at[b], recv_sem=s2_recv.at[b], device_id=chip, device_id_type=MESH)

    def third(b, q):
        rows_b = pl.ds(mine + q + b * blk, blk)
        return pltpu.make_async_remote_copy(
            src_ref=out_ref.at[rows_b], dst_ref=out_ref.at[rows_b],
            send_sem=s3_send.at[b], recv_sem=s3_recv.at[b], device_id=chip, device_id_type=MESH)

    sent2 = []
    for b in range(nb):
        for cp in far_in[b]:
            cp.wait_recv()
        add(far_q + b * blk, blk)
        cp = second(b, far_q)
        cp.start()
        sent2.append(cp)
    for cp in near_in:
        cp.wait_recv()
    add(my_q, quarter)

    def fourth(k, lo):
        rows_k = pl.ds(lo, blk)
        return pltpu.make_async_remote_copy(
            src_ref=out_ref.at[rows_k], dst_ref=out_ref.at[rows_k],
            send_sem=t_send.at[k], recv_sem=t_recv.at[k], device_id=core, device_id_type=MESH)

    sent3 = []
    sent4 = []
    for b in range(nb):
        second(b, my_q).wait_recv()

        def merge(i, carry):
            r = pl.multiple_of(b * blk + i * step, step)
            n = part[0, pl.ds(my_q + r, step)] + recv2[0, pl.ds(r, step)]
            d = part[1, pl.ds(my_q + r, step)] + recv2[1, pl.ds(r, step)]
            out_ref[pl.ds(mine + my_q + r, step)] = (n / d).astype(out_ref.dtype)
            return carry

        lax.fori_loop(0, blk // step, merge, 0)
        cp = third(b, my_q)
        cp.start()
        sent3.append(cp)
        cp = fourth(b, mine + my_q + b * blk)
        cp.start()
        sent4.append(cp)
    for b in range(nb):
        third(b, far_q).wait_recv()
        cp = fourth(nb + b, mine + far_q + b * blk)
        cp.start()
        sent4.append(cp)
    for b in range(nb):
        fourth(b, other + my_q + b * blk).wait_recv()
        fourth(nb + b, other + far_q + b * blk).wait_recv()
    for cp in sum(far_in, []) + near_in + sent2 + sent3 + sent4:
        cp.wait_send()


def mp_merge(prior, w, cid, blocks=8):
    rows, cols = prior.shape
    vmem = pltpu.MemorySpace.VMEM
    return pl.pallas_call(
        mp_merge_kernel,
        out_shape=jax.ShapeDtypeStruct((rows, cols), jnp.bfloat16),
        in_specs=[pl.BlockSpec(memory_space=vmem)] * 2,
        out_specs=pl.BlockSpec(memory_space=vmem),
        scratch_shapes=[
            pltpu.VMEM((rows // 2, cols), jnp.float32),
            pltpu.VMEM((rows // 2, cols), w.dtype),
            pltpu.VMEM((2, rows // 2, cols), jnp.float32),
            pltpu.VMEM((2, rows // 4, cols), jnp.float32),
            pltpu.SemaphoreType.DMA((5,)),
            pltpu.SemaphoreType.DMA((5,)),
            pltpu.SemaphoreType.DMA((blocks,)),
            pltpu.SemaphoreType.DMA((blocks,)),
            pltpu.SemaphoreType.DMA((blocks,)),
            pltpu.SemaphoreType.DMA((blocks,)),
            pltpu.SemaphoreType.DMA((2 * blocks,)),
            pltpu.SemaphoreType.DMA((2 * blocks,)),
            pltpu.SemaphoreType.DMA((2 * blocks,)),
            pltpu.SemaphoreType.DMA((2 * blocks,)),
        ],
        compiler_params=pltpu.CompilerParams(
            collective_id=cid, has_side_effects=True, vmem_limit_bytes=60 * 1024 * 1024),
        cost_estimate=pl.CostEstimate(flops=rows * cols * 6, bytes_accessed=rows * cols * 12, transcendentals=0),
    )(prior, w)


def ring_copies(axis, me, n, src, slot, sems, base):
    right, left = lax.rem(me + 1, n), lax.rem(me + n - 1, n)
    far = lax.rem(me + 2, n)
    send, recv = sems
    half = src.shape[0] // 2

    def rc(s, d, k, dev):
        return pltpu.make_async_remote_copy(
            src_ref=s, dst_ref=d, send_sem=send.at[base + k], recv_sem=recv.at[base + k],
            device_id={axis: dev}, device_id_type=MESH)

    whole = pl.ds(0, 2 * half)
    lo, hi = pl.ds(0, half), pl.ds(half, half)
    first = [rc(src, slot(me, whole), 0, right), rc(src, slot(me, whole), 1, left)]
    arrive = [rc(src, slot(left, whole), 0, left), rc(src, slot(right, whole), 1, right)]
    relay = [
        rc(slot(right, lo), slot(right, lo), 2, left),
        rc(slot(left, hi), slot(left, hi), 3, right),
    ]
    land = [
        rc(slot(far, lo), slot(far, lo), 2, right),
        rc(slot(far, hi), slot(far, hi), 3, left),
    ]
    return first, arrive, relay, land


def gather_kernel(act_in, grad_in, seq_ref, act_out, grad_out, seq_out, act_ref, grad_ref,
                  send, recv, local, seq_send, seq_recv, p0_send, p0_recv, q0_send, q0_recv):
    nx = 4
    ny = 4
    x = lax.axis_index("x")
    y = lax.axis_index("y")
    zh = lax.axis_index("zh")
    xr, xl = lax.rem(x + 1, nx), lax.rem(x + nx - 1, nx)
    yr, yl = lax.rem(y + 1, ny), lax.rem(y + ny - 1, ny)

    nj = 2 * ny
    j = zh * ny + y
    rw = act_ref.shape[2]
    cw = grad_ref.shape[2]

    def plane(jd):
        return {"zh": jd // ny, "y": lax.rem(jd, ny)}

    barrier = pltpu.get_barrier_semaphore()
    for s in range(1, nj):
        pl.semaphore_signal(barrier, 1, device_id=plane(lax.rem(j + s, nj)), device_id_type=MESH)
    for s in range(1, nx):
        pl.semaphore_signal(barrier, 1, device_id={"x": lax.rem(x + s, nx)}, device_id_type=MESH)
    pl.semaphore_wait(barrier, nj - 1 + nx - 1)

    def act_p0(s, jd, js):
        return pltpu.make_async_remote_copy(
            src_ref=act_in.at[:, pl.ds(pl.multiple_of(jd * rw, 128), rw)], dst_ref=act_ref.at[js],
            send_sem=p0_send.at[s], recv_sem=p0_recv.at[s], device_id=plane(jd),
            device_id_type=MESH)

    def grad_p0(s, xd, xs):
        return pltpu.make_async_remote_copy(
            src_ref=grad_in.at[:, pl.ds(pl.multiple_of(xd * cw, 128), cw)], dst_ref=grad_ref.at[xs],
            send_sem=q0_send.at[s], recv_sem=q0_recv.at[s], device_id={"x": xd},
            device_id_type=MESH)

    p0_out = [act_p0(s, lax.rem(j + s, nj), j) for s in range(1, nj)]
    p0_in = [act_p0(s, j, lax.rem(j + nj - s, nj)) for s in range(1, nj)]
    q0_out = [grad_p0(s, lax.rem(x + s, nx), x) for s in range(1, nx)]
    q0_in = [grad_p0(s, x, lax.rem(x + nx - s, nx)) for s in range(1, nx)]
    own0 = [
        pltpu.make_async_copy(
            act_in.at[:, pl.ds(pl.multiple_of(j * rw, 128), rw)], act_ref.at[j], local.at[3]),
        pltpu.make_async_copy(
            grad_in.at[:, pl.ds(pl.multiple_of(x * cw, 128), cw)], grad_ref.at[x], local.at[4]),
    ]
    for c in own0 + q0_out + p0_out:
        c.start()
    for c in q0_in:
        c.wait_recv()
    own0[1].wait()

    sems = (send, recv)
    a_first, a_arrive, a_relay, a_land = ring_copies(
        "x", x, nx, act_ref, lambda i, p: act_out.at[i, p], sems, 0)
    g_first, g_arrive, g_relay, g_land = ring_copies(
        "y", y, ny, grad_ref, lambda i, p: grad_out.at[p, zh, i], sems, 4)
    p_first, p_arrive, p_relay, p_land = ring_copies(
        "y", y, ny, grad_out.at[:, 1 - zh, y], lambda i, p: grad_out.at[p, 1 - zh, i], sems, 8)
    swap = pltpu.make_async_remote_copy(
        src_ref=grad_ref, dst_ref=grad_out.at[:, zh, y], send_sem=send.at[12],
        recv_sem=recv.at[12], device_id={"zh": 1 - zh}, device_id_type=MESH)
    swap_in = pltpu.make_async_remote_copy(
        src_ref=grad_ref, dst_ref=grad_out.at[:, 1 - zh, y], send_sem=send.at[12],
        recv_sem=recv.at[12], device_id={"zh": 1 - zh}, device_id_type=MESH)

    own = [
        pltpu.make_async_copy(act_ref, act_out.at[x], local.at[0]),
        pltpu.make_async_copy(grad_ref, grad_out.at[:, zh, y], local.at[1]),
        pltpu.make_async_copy(seq_ref, seq_out.at[x], local.at[2]),
    ]

    def sc(s, d, k, dev):
        return pltpu.make_async_remote_copy(
            src_ref=s, dst_ref=d, send_sem=seq_send.at[k], recv_sem=seq_recv.at[k],
            device_id={"x": dev}, device_id_type=MESH)

    seq_first = [sc(seq_ref, seq_out.at[x], 0, xr), sc(seq_ref, seq_out.at[x], 1, xl)]

    swap.start()
    for c in g_first + seq_first + [own[1], own[2]]:
        c.start()
    for c in p0_in:
        c.wait_recv()
    own0[0].wait()
    for c in a_first + [own[0]]:
        c.start()
    for c in a_arrive:
        c.wait_recv()
    sc(seq_ref, seq_out.at[xl], 0, xl).wait_recv()
    sc(seq_ref, seq_out.at[xr], 1, xr).wait_recv()
    seq_relay = sc(seq_out.at[xr], seq_out.at[xr], 2, xl)
    seq_relay.start()
    for c in a_relay:
        c.start()
    for c in g_arrive:
        c.wait_recv()
    for c in g_relay:
        c.start()
    swap_in.wait_recv()
    for c in p_first:
        c.start()
    for c in p_arrive:
        c.wait_recv()
    for c in p_relay:
        c.start()
    for c in a_land + g_land + p_land:
        c.wait_recv()
    sc(seq_out.at[lax.rem(x + 2, nx)], seq_out.at[lax.rem(x + 2, nx)], 2, xr).wait_recv()
    for c in a_first + a_relay + g_first + g_relay + p_first + p_relay + seq_first:
        c.wait_send()
    seq_relay.wait_send()
    swap.wait_send()
    for c in p0_out + q0_out:
        c.wait_send()
    for c in own:
        c.wait()


def gather_all(act, grad, seq, nj, nx, rw, cw):
    tok = act.shape[0]
    any_space = pl.BlockSpec(memory_space=pl.ANY)
    return pl.pallas_call(
        gather_kernel,
        out_shape=(
            jax.ShapeDtypeStruct((nx, nj, tok, rw), act.dtype),
            jax.ShapeDtypeStruct((nx, 2, nj // 2, tok, cw), grad.dtype),
            jax.ShapeDtypeStruct((nx,) + seq.shape, seq.dtype),
            jax.ShapeDtypeStruct((nj, tok, rw), act.dtype),
            jax.ShapeDtypeStruct((nx, tok, cw), grad.dtype),
        ),
        in_specs=[any_space] * 3,
        out_specs=(any_space,) * 5,
        scratch_shapes=[
            pltpu.SemaphoreType.DMA((13,)),
            pltpu.SemaphoreType.DMA((13,)),
            pltpu.SemaphoreType.DMA((5,)),
            pltpu.SemaphoreType.DMA((3,)),
            pltpu.SemaphoreType.DMA((3,)),
            pltpu.SemaphoreType.DMA((nj,)),
            pltpu.SemaphoreType.DMA((nj,)),
            pltpu.SemaphoreType.DMA((nx,)),
            pltpu.SemaphoreType.DMA((nx,)),
        ],
        compiler_params=pltpu.CompilerParams(collective_id=1, has_side_effects=True),
        cost_estimate=pl.CostEstimate(
            flops=0, bytes_accessed=8 * tok * (nj * rw + 2 * nx * cw), transcendentals=0),
    )(act, grad, seq)


def per_device(activations, out_grads, seq_ids, weights):
    nx = lax.axis_size("x")
    nj = lax.axis_size(("zh", "y"))
    tok = activations.shape[1]
    col_width = weights.shape[2]
    row_width = weights.shape[1]
    total = nx * nj * tok
    act_all, grad_all, owners, _, _ = gather_all(
        activations[0], out_grads[0], seq_ids, nj, nx, row_width, col_width)
    act_all = act_all.reshape(total, row_width)
    grad_all = grad_all.reshape(total, col_width)
    first_long = jnp.sum((owners < 1).astype(jnp.int32)) * (total // owners.size) > total // 2

    def part(lo, hi):
        return lax.dot_general(
            act_all[lo:hi], grad_all[lo:hi], (((0,), (0,)), ((), ())),
            preferred_element_type=jnp.float32,
        )

    quarter = total // 4
    head = part(0, quarter)
    mid = part(quarter, 3 * quarter)
    tail = part(3 * quarter, total)
    g0 = jnp.where(first_long, head + mid, head)
    g1 = jnp.where(first_long, tail, mid + tail)
    fisher = g0 * g0 + g1 * g1
    prior = fisher / SEQS + smoothing
    return mp_merge(prior, weights[0], 2)


def solution(mesh):
    assert mesh.shape["mp"] == 4 and mesh.shape["fsdp"] == 32
    fine = jax.sharding.Mesh(
        mesh.devices.reshape(2, 2, 4, 2, 4), ("zl", "c", "x", "zh", "y")
    )
    mp, fs = ("zl", "c"), ("x", "zh", "y")
    placed = (P(mp, fs, None), P(mp, fs, None), P(mp, fs), P(mp, fs, None))
    return jax.shard_map(
        per_device, mesh=fine, in_specs=placed, out_specs=P(fs, None), check_vma=False
    )
```

```python
import functools

import jax
import jax.numpy as jnp
from jax import lax
from jax.experimental import pallas as pl
from jax.experimental.pallas import tpu as pltpu
from jax.sharding import PartitionSpec as P

F = 7168
SEQS = 2
MESH = pl.DeviceIdType.MESH

smoothing = 0.05


def mp_merge_kernel(prior_ref, w_ref, out_ref, recv_p, recv_w, part, recv2,
                    send_sem, recv_sem, s2_send, s2_recv, s3_send, s3_recv, f_send, f_recv,
                    t_send, t_recv):
    c = lax.axis_index("c")
    z = lax.axis_index("zl")
    rows = prior_ref.shape[0]
    half, quarter = rows // 2, rows // 4
    nb = s2_send.shape[0]
    blk = quarter // nb
    step = 32
    core = {"c": 1 - c}
    chip = {"zl": 1 - z}

    barrier = pltpu.get_barrier_semaphore()
    pl.semaphore_signal(barrier, 1, device_id=core, device_id_type=MESH)
    pl.semaphore_signal(barrier, 1, device_id=chip, device_id_type=MESH)
    pl.semaphore_wait(barrier, 2)

    mine = pl.multiple_of(c * half, half)
    other = pl.multiple_of((1 - c) * half, half)
    my_q = pl.multiple_of(z * quarter, quarter)
    far_q = pl.multiple_of((1 - z) * quarter, quarter)

    def onchip(k, q):
        cp = pltpu.make_async_remote_copy(
            src_ref=prior_ref.at[pl.ds(other + q, quarter)], dst_ref=recv_p.at[pl.ds(q, quarter)],
            send_sem=send_sem.at[k], recv_sem=recv_sem.at[k], device_id=core, device_id_type=MESH)
        cw = pltpu.make_async_remote_copy(
            src_ref=w_ref.at[pl.ds(other + q, quarter)], dst_ref=recv_w.at[pl.ds(q, quarter)],
            send_sem=send_sem.at[2 + k], recv_sem=recv_sem.at[2 + k], device_id=core,
            device_id_type=MESH)
        return [cw, cp]

    def onchip_block(b):
        rows_b = pl.ds(far_q + b * blk, blk)
        cp = pltpu.make_async_remote_copy(
            src_ref=prior_ref.at[pl.ds(other + far_q + b * blk, blk)], dst_ref=recv_p.at[rows_b],
            send_sem=f_send.at[b], recv_sem=f_recv.at[b], device_id=core, device_id_type=MESH)
        cw = pltpu.make_async_remote_copy(
            src_ref=w_ref.at[pl.ds(other + far_q + b * blk, blk)], dst_ref=recv_w.at[rows_b],
            send_sem=f_send.at[nb + b], recv_sem=f_recv.at[nb + b], device_id=core,
            device_id_type=MESH)
        return [cw, cp]

    far_in = [onchip_block(b) for b in range(nb)]
    near_in = onchip(1, my_q)
    for pair in far_in:
        for cp in pair:
            cp.start()
    for cp in near_in:
        cp.start()

    def add(lo, count):
        def body(i, carry):
            r = pl.multiple_of(lo + i * step, step)
            p_me = prior_ref[pl.ds(mine + r, step)]
            p_ot = recv_p[pl.ds(r, step)]
            n_me = p_me * w_ref[pl.ds(mine + r, step)].astype(jnp.float32)
            n_ot = p_ot * recv_w[pl.ds(r, step)].astype(jnp.float32)
            part[0, pl.ds(r, step)] = n_ot + n_me
            part[1, pl.ds(r, step)] = p_ot + p_me
            return carry

        lax.fori_loop(0, count // step, body, 0)

    def second(b, lo):
        return pltpu.make_async_remote_copy(
            src_ref=part.at[:, pl.ds(lo + b * blk, blk)], dst_ref=recv2.at[:, pl.ds(b * blk, blk)],
            send_sem=s2_send.at[b], recv_sem=s2_recv.at[b], device_id=chip, device_id_type=MESH)

    def third(b, q):
        rows_b = pl.ds(mine + q + b * blk, blk)
        return pltpu.make_async_remote_copy(
            src_ref=out_ref.at[rows_b], dst_ref=out_ref.at[rows_b],
            send_sem=s3_send.at[b], recv_sem=s3_recv.at[b], device_id=chip, device_id_type=MESH)

    sent2 = []
    for b in range(nb):
        for cp in far_in[b]:
            cp.wait_recv()
        add(far_q + b * blk, blk)
        cp = second(b, far_q)
        cp.start()
        sent2.append(cp)
    for cp in near_in:
        cp.wait_recv()
    add(my_q, quarter)

    def fourth(k, lo):
        rows_k = pl.ds(lo, blk)
        return pltpu.make_async_remote_copy(
            src_ref=out_ref.at[rows_k], dst_ref=out_ref.at[rows_k],
            send_sem=t_send.at[k], recv_sem=t_recv.at[k], device_id=core, device_id_type=MESH)

    sent3 = []
    sent4 = []
    for b in range(nb):
        second(b, my_q).wait_recv()

        def merge(i, carry):
            r = pl.multiple_of(b * blk + i * step, step)
            n = part[0, pl.ds(my_q + r, step)] + recv2[0, pl.ds(r, step)]
            d = part[1, pl.ds(my_q + r, step)] + recv2[1, pl.ds(r, step)]
            out_ref[pl.ds(mine + my_q + r, step)] = (n / d).astype(out_ref.dtype)
            return carry

        lax.fori_loop(0, blk // step, merge, 0)
        cp = third(b, my_q)
        cp.start()
        sent3.append(cp)
        cp = fourth(b, mine + my_q + b * blk)
        cp.start()
        sent4.append(cp)
    for b in range(nb):
        third(b, far_q).wait_recv()
        cp = fourth(nb + b, mine + far_q + b * blk)
        cp.start()
        sent4.append(cp)
    for b in range(nb):
        fourth(b, other + my_q + b * blk).wait_recv()
        fourth(nb + b, other + far_q + b * blk).wait_recv()
    for cp in sum(far_in, []) + near_in + sent2 + sent3 + sent4:
        cp.wait_send()


def mp_merge(prior, w, cid, blocks=8):
    rows, cols = prior.shape
    vmem = pltpu.MemorySpace.VMEM
    return pl.pallas_call(
        mp_merge_kernel,
        out_shape=jax.ShapeDtypeStruct((rows, cols), jnp.bfloat16),
        in_specs=[pl.BlockSpec(memory_space=vmem)] * 2,
        out_specs=pl.BlockSpec(memory_space=vmem),
        scratch_shapes=[
            pltpu.VMEM((rows // 2, cols), jnp.float32),
            pltpu.VMEM((rows // 2, cols), w.dtype),
            pltpu.VMEM((2, rows // 2, cols), jnp.float32),
            pltpu.VMEM((2, rows // 4, cols), jnp.float32),
            pltpu.SemaphoreType.DMA((5,)),
            pltpu.SemaphoreType.DMA((5,)),
            pltpu.SemaphoreType.DMA((blocks,)),
            pltpu.SemaphoreType.DMA((blocks,)),
            pltpu.SemaphoreType.DMA((blocks,)),
            pltpu.SemaphoreType.DMA((blocks,)),
            pltpu.SemaphoreType.DMA((2 * blocks,)),
            pltpu.SemaphoreType.DMA((2 * blocks,)),
            pltpu.SemaphoreType.DMA((2 * blocks,)),
            pltpu.SemaphoreType.DMA((2 * blocks,)),
        ],
        compiler_params=pltpu.CompilerParams(
            collective_id=cid, has_side_effects=True, vmem_limit_bytes=60 * 1024 * 1024),
        cost_estimate=pl.CostEstimate(flops=rows * cols * 6, bytes_accessed=rows * cols * 12, transcendentals=0),
    )(prior, w)


def ring_copies(axis, me, n, src, slot, sems, base):
    right, left = lax.rem(me + 1, n), lax.rem(me + n - 1, n)
    far = lax.rem(me + 2, n)
    send, recv = sems
    half = src.shape[0] // 2

    def rc(s, d, k, dev):
        return pltpu.make_async_remote_copy(
            src_ref=s, dst_ref=d, send_sem=send.at[base + k], recv_sem=recv.at[base + k],
            device_id={axis: dev}, device_id_type=MESH)

    whole = pl.ds(0, 2 * half)
    lo, hi = pl.ds(0, half), pl.ds(half, half)
    first = [rc(src, slot(me, whole), 0, right), rc(src, slot(me, whole), 1, left)]
    arrive = [rc(src, slot(left, whole), 0, left), rc(src, slot(right, whole), 1, right)]
    relay = [
        rc(slot(right, lo), slot(right, lo), 2, left),
        rc(slot(left, hi), slot(left, hi), 3, right),
    ]
    land = [
        rc(slot(far, lo), slot(far, lo), 2, right),
        rc(slot(far, hi), slot(far, hi), 3, left),
    ]
    return first, arrive, relay, land


def gather_kernel(act_in, grad_in, seq_ref, act_out, grad_out, seq_out, act_ref, grad_ref,
                  send, recv, local, seq_send, seq_recv, p0_send, p0_recv, q0_send, q0_recv):
    nx = 4
    ny = 4
    x = lax.axis_index("x")
    y = lax.axis_index("y")
    zh = lax.axis_index("zh")
    xr, xl = lax.rem(x + 1, nx), lax.rem(x + nx - 1, nx)
    yr, yl = lax.rem(y + 1, ny), lax.rem(y + ny - 1, ny)

    nj = 2 * ny
    j = zh * ny + y
    rw = act_ref.shape[2]
    cw = grad_ref.shape[2]

    def plane(jd):
        return {"zh": jd // ny, "y": lax.rem(jd, ny)}

    barrier = pltpu.get_barrier_semaphore()
    for s in range(1, nj):
        pl.semaphore_signal(barrier, 1, device_id=plane(lax.rem(j + s, nj)), device_id_type=MESH)
    for s in range(1, nx):
        pl.semaphore_signal(barrier, 1, device_id={"x": lax.rem(x + s, nx)}, device_id_type=MESH)
    pl.semaphore_wait(barrier, nj - 1 + nx - 1)

    def act_p0(s, jd, js):
        return pltpu.make_async_remote_copy(
            src_ref=act_in.at[:, pl.ds(pl.multiple_of(jd * rw, 128), rw)], dst_ref=act_ref.at[js],
            send_sem=p0_send.at[s], recv_sem=p0_recv.at[s], device_id=plane(jd),
            device_id_type=MESH)

    def grad_p0(s, xd, xs):
        return pltpu.make_async_remote_copy(
            src_ref=grad_in.at[:, pl.ds(pl.multiple_of(xd * cw, 128), cw)], dst_ref=grad_ref.at[xs],
            send_sem=q0_send.at[s], recv_sem=q0_recv.at[s], device_id={"x": xd},
            device_id_type=MESH)

    p0_out = [act_p0(s, lax.rem(j + s, nj), j) for s in range(1, nj)]
    p0_in = [act_p0(s, j, lax.rem(j + nj - s, nj)) for s in range(1, nj)]
    q0_out = [grad_p0(s, lax.rem(x + s, nx), x) for s in range(1, nx)]
    q0_in = [grad_p0(s, x, lax.rem(x + nx - s, nx)) for s in range(1, nx)]
    own0 = [
        pltpu.make_async_copy(
            act_in.at[:, pl.ds(pl.multiple_of(j * rw, 128), rw)], act_ref.at[j], local.at[3]),
        pltpu.make_async_copy(
            grad_in.at[:, pl.ds(pl.multiple_of(x * cw, 128), cw)], grad_ref.at[x], local.at[4]),
    ]
    for c in own0 + q0_out + p0_out:
        c.start()
    for c in q0_in:
        c.wait_recv()
    own0[1].wait()

    sems = (send, recv)
    a_first, a_arrive, a_relay, a_land = ring_copies(
        "x", x, nx, act_ref, lambda i, p: act_out.at[i, p], sems, 0)
    g_first, g_arrive, g_relay, g_land = ring_copies(
        "y", y, ny, grad_ref, lambda i, p: grad_out.at[p, zh, i], sems, 4)
    p_first, p_arrive, p_relay, p_land = ring_copies(
        "y", y, ny, grad_out.at[:, 1 - zh, y], lambda i, p: grad_out.at[p, 1 - zh, i], sems, 8)
    swap = pltpu.make_async_remote_copy(
        src_ref=grad_ref, dst_ref=grad_out.at[:, zh, y], send_sem=send.at[12],
        recv_sem=recv.at[12], device_id={"zh": 1 - zh}, device_id_type=MESH)
    swap_in = pltpu.make_async_remote_copy(
        src_ref=grad_ref, dst_ref=grad_out.at[:, 1 - zh, y], send_sem=send.at[12],
        recv_sem=recv.at[12], device_id={"zh": 1 - zh}, device_id_type=MESH)

    own = [
        pltpu.make_async_copy(act_ref, act_out.at[x], local.at[0]),
        pltpu.make_async_copy(grad_ref, grad_out.at[:, zh, y], local.at[1]),
        pltpu.make_async_copy(seq_ref, seq_out.at[x], local.at[2]),
    ]

    def sc(s, d, k, dev):
        return pltpu.make_async_remote_copy(
            src_ref=s, dst_ref=d, send_sem=seq_send.at[k], recv_sem=seq_recv.at[k],
            device_id={"x": dev}, device_id_type=MESH)

    seq_first = [sc(seq_ref, seq_out.at[x], 0, xr), sc(seq_ref, seq_out.at[x], 1, xl)]

    swap.start()
    for c in g_first + seq_first + [own[1], own[2]]:
        c.start()
    swap_in.wait_recv()
    for c in p_first:
        c.start()
    for c in g_arrive:
        c.wait_recv()
    for c in g_relay:
        c.start()
    for c in p0_in:
        c.wait_recv()
    own0[0].wait()
    for c in a_first + [own[0]]:
        c.start()
    for c in p_arrive:
        c.wait_recv()
    for c in p_relay:
        c.start()
    for c in a_arrive:
        c.wait_recv()
    sc(seq_ref, seq_out.at[xl], 0, xl).wait_recv()
    sc(seq_ref, seq_out.at[xr], 1, xr).wait_recv()
    seq_relay = sc(seq_out.at[xr], seq_out.at[xr], 2, xl)
    seq_relay.start()
    for c in a_relay:
        c.start()
    for c in a_land + g_land + p_land:
        c.wait_recv()
    sc(seq_out.at[lax.rem(x + 2, nx)], seq_out.at[lax.rem(x + 2, nx)], 2, xr).wait_recv()
    for c in a_first + a_relay + g_first + g_relay + p_first + p_relay + seq_first:
        c.wait_send()
    seq_relay.wait_send()
    swap.wait_send()
    for c in p0_out + q0_out:
        c.wait_send()
    for c in own:
        c.wait()


def gather_all(act, grad, seq, nj, nx, rw, cw):
    tok = act.shape[0]
    any_space = pl.BlockSpec(memory_space=pl.ANY)
    return pl.pallas_call(
        gather_kernel,
        out_shape=(
            jax.ShapeDtypeStruct((nx, nj, tok, rw), act.dtype),
            jax.ShapeDtypeStruct((nx, 2, nj // 2, tok, cw), grad.dtype),
            jax.ShapeDtypeStruct((nx,) + seq.shape, seq.dtype),
            jax.ShapeDtypeStruct((nj, tok, rw), act.dtype),
            jax.ShapeDtypeStruct((nx, tok, cw), grad.dtype),
        ),
        in_specs=[any_space] * 3,
        out_specs=(any_space,) * 5,
        scratch_shapes=[
            pltpu.SemaphoreType.DMA((13,)),
            pltpu.SemaphoreType.DMA((13,)),
            pltpu.SemaphoreType.DMA((5,)),
            pltpu.SemaphoreType.DMA((3,)),
            pltpu.SemaphoreType.DMA((3,)),
            pltpu.SemaphoreType.DMA((nj,)),
            pltpu.SemaphoreType.DMA((nj,)),
            pltpu.SemaphoreType.DMA((nx,)),
            pltpu.SemaphoreType.DMA((nx,)),
        ],
        compiler_params=pltpu.CompilerParams(collective_id=1, has_side_effects=True),
        cost_estimate=pl.CostEstimate(
            flops=0, bytes_accessed=8 * tok * (nj * rw + 2 * nx * cw), transcendentals=0),
    )(act, grad, seq)


def per_device(activations, out_grads, seq_ids, weights):
    nx = lax.axis_size("x")
    nj = lax.axis_size(("zh", "y"))
    tok = activations.shape[1]
    col_width = weights.shape[2]
    row_width = weights.shape[1]
    total = nx * nj * tok
    act_all, grad_all, owners, _, _ = gather_all(
        activations[0], out_grads[0], seq_ids, nj, nx, row_width, col_width)
    act_all = act_all.reshape(total, row_width)
    grad_all = grad_all.reshape(total, col_width)
    first_long = jnp.sum((owners < 1).astype(jnp.int32)) * (total // owners.size) > total // 2

    def part(lo, hi):
        return lax.dot_general(
            act_all[lo:hi], grad_all[lo:hi], (((0,), (0,)), ((), ())),
            preferred_element_type=jnp.float32,
        )

    quarter = total // 4
    head = part(0, quarter)
    mid = part(quarter, 3 * quarter)
    tail = part(3 * quarter, total)
    g0 = jnp.where(first_long, head + mid, head)
    g1 = jnp.where(first_long, tail, mid + tail)
    fisher = g0 * g0 + g1 * g1
    prior = fisher / SEQS + smoothing
    return mp_merge(prior, weights[0], 2)


def solution(mesh):
    assert mesh.shape["mp"] == 4 and mesh.shape["fsdp"] == 32
    fine = jax.sharding.Mesh(
        mesh.devices.reshape(2, 2, 4, 2, 4), ("zl", "c", "x", "zh", "y")
    )
    mp, fs = ("zl", "c"), ("x", "zh", "y")
    placed = (P(mp, fs, None), P(mp, fs, None), P(mp, fs), P(mp, fs, None))
    return jax.shard_map(
        per_device, mesh=fine, in_specs=placed, out_specs=P(fs, None), check_vma=False
    )
```

```python
import functools

import jax
import jax.numpy as jnp
from jax import lax
from jax.experimental import pallas as pl
from jax.experimental.pallas import tpu as pltpu
from jax.sharding import PartitionSpec as P

F = 7168
SEQS = 2
MESH = pl.DeviceIdType.MESH

smoothing = 0.05


def mp_merge_kernel(prior_ref, w_ref, out_ref, recv_p, recv_w, part, recv2,
                    send_sem, recv_sem, s2_send, s2_recv, s3_send, s3_recv, f_send, f_recv,
                    t_send, t_recv):
    c = lax.axis_index("c")
    z = lax.axis_index("zl")
    rows = prior_ref.shape[0]
    half, quarter = rows // 2, rows // 4
    nb = s2_send.shape[0]
    blk = quarter // nb
    step = 32
    core = {"c": 1 - c}
    chip = {"zl": 1 - z}

    barrier = pltpu.get_barrier_semaphore()
    pl.semaphore_signal(barrier, 1, device_id=core, device_id_type=MESH)
    pl.semaphore_signal(barrier, 1, device_id=chip, device_id_type=MESH)
    pl.semaphore_wait(barrier, 2)

    mine = pl.multiple_of(c * half, half)
    other = pl.multiple_of((1 - c) * half, half)
    my_q = pl.multiple_of(z * quarter, quarter)
    far_q = pl.multiple_of((1 - z) * quarter, quarter)

    def onchip(k, q):
        cp = pltpu.make_async_remote_copy(
            src_ref=prior_ref.at[pl.ds(other + q, quarter)], dst_ref=recv_p.at[pl.ds(q, quarter)],
            send_sem=send_sem.at[k], recv_sem=recv_sem.at[k], device_id=core, device_id_type=MESH)
        cw = pltpu.make_async_remote_copy(
            src_ref=w_ref.at[pl.ds(other + q, quarter)], dst_ref=recv_w.at[pl.ds(q, quarter)],
            send_sem=send_sem.at[2 + k], recv_sem=recv_sem.at[2 + k], device_id=core,
            device_id_type=MESH)
        return [cw, cp]

    def onchip_block(b):
        rows_b = pl.ds(far_q + b * blk, blk)
        cp = pltpu.make_async_remote_copy(
            src_ref=prior_ref.at[pl.ds(other + far_q + b * blk, blk)], dst_ref=recv_p.at[rows_b],
            send_sem=f_send.at[b], recv_sem=f_recv.at[b], device_id=core, device_id_type=MESH)
        cw = pltpu.make_async_remote_copy(
            src_ref=w_ref.at[pl.ds(other + far_q + b * blk, blk)], dst_ref=recv_w.at[rows_b],
            send_sem=f_send.at[nb + b], recv_sem=f_recv.at[nb + b], device_id=core,
            device_id_type=MESH)
        return [cw, cp]

    far_in = [onchip_block(b) for b in range(nb)]
    near_in = onchip(1, my_q)
    for pair in far_in:
        for cp in pair:
            cp.start()
    for cp in near_in:
        cp.start()

    def add(lo, count):
        def body(i, carry):
            r = pl.multiple_of(lo + i * step, step)
            p_me = prior_ref[pl.ds(mine + r, step)]
            p_ot = recv_p[pl.ds(r, step)]
            n_me = p_me * w_ref[pl.ds(mine + r, step)].astype(jnp.float32)
            n_ot = p_ot * recv_w[pl.ds(r, step)].astype(jnp.float32)
            part[0, pl.ds(r, step)] = n_ot + n_me
            part[1, pl.ds(r, step)] = p_ot + p_me
            return carry

        lax.fori_loop(0, count // step, body, 0)

    def second(b, lo):
        return pltpu.make_async_remote_copy(
            src_ref=part.at[:, pl.ds(lo + b * blk, blk)], dst_ref=recv2.at[:, pl.ds(b * blk, blk)],
            send_sem=s2_send.at[b], recv_sem=s2_recv.at[b], device_id=chip, device_id_type=MESH)

    def third(b, q):
        rows_b = pl.ds(mine + q + b * blk, blk)
        return pltpu.make_async_remote_copy(
            src_ref=out_ref.at[rows_b], dst_ref=out_ref.at[rows_b],
            send_sem=s3_send.at[b], recv_sem=s3_recv.at[b], device_id=chip, device_id_type=MESH)

    sent2 = []
    for b in range(nb):
        for cp in far_in[b]:
            cp.wait_recv()
        add(far_q + b * blk, blk)
        cp = second(b, far_q)
        cp.start()
        sent2.append(cp)
    for cp in near_in:
        cp.wait_recv()
    add(my_q, quarter)

    def fourth(k, lo):
        rows_k = pl.ds(lo, blk)
        return pltpu.make_async_remote_copy(
            src_ref=out_ref.at[rows_k], dst_ref=out_ref.at[rows_k],
            send_sem=t_send.at[k], recv_sem=t_recv.at[k], device_id=core, device_id_type=MESH)

    sent3 = []
    sent4 = []
    for b in range(nb):
        second(b, my_q).wait_recv()

        def merge(i, carry):
            r = pl.multiple_of(b * blk + i * step, step)
            n = part[0, pl.ds(my_q + r, step)] + recv2[0, pl.ds(r, step)]
            d = part[1, pl.ds(my_q + r, step)] + recv2[1, pl.ds(r, step)]
            out_ref[pl.ds(mine + my_q + r, step)] = (n / d).astype(out_ref.dtype)
            return carry

        lax.fori_loop(0, blk // step, merge, 0)
        cp = third(b, my_q)
        cp.start()
        sent3.append(cp)
        cp = fourth(b, mine + my_q + b * blk)
        cp.start()
        sent4.append(cp)
    for b in range(nb):
        third(b, far_q).wait_recv()
        cp = fourth(nb + b, mine + far_q + b * blk)
        cp.start()
        sent4.append(cp)
    for b in range(nb):
        fourth(b, other + my_q + b * blk).wait_recv()
        fourth(nb + b, other + far_q + b * blk).wait_recv()
    for cp in sum(far_in, []) + near_in + sent2 + sent3 + sent4:
        cp.wait_send()


def mp_merge(prior, w, cid, blocks=8):
    rows, cols = prior.shape
    vmem = pltpu.MemorySpace.VMEM
    return pl.pallas_call(
        mp_merge_kernel,
        out_shape=jax.ShapeDtypeStruct((rows, cols), jnp.bfloat16),
        in_specs=[pl.BlockSpec(memory_space=vmem)] * 2,
        out_specs=pl.BlockSpec(memory_space=vmem),
        scratch_shapes=[
            pltpu.VMEM((rows // 2, cols), jnp.float32),
            pltpu.VMEM((rows // 2, cols), w.dtype),
            pltpu.VMEM((2, rows // 2, cols), jnp.float32),
            pltpu.VMEM((2, rows // 4, cols), jnp.float32),
            pltpu.SemaphoreType.DMA((5,)),
            pltpu.SemaphoreType.DMA((5,)),
            pltpu.SemaphoreType.DMA((blocks,)),
            pltpu.SemaphoreType.DMA((blocks,)),
            pltpu.SemaphoreType.DMA((blocks,)),
            pltpu.SemaphoreType.DMA((blocks,)),
            pltpu.SemaphoreType.DMA((2 * blocks,)),
            pltpu.SemaphoreType.DMA((2 * blocks,)),
            pltpu.SemaphoreType.DMA((2 * blocks,)),
            pltpu.SemaphoreType.DMA((2 * blocks,)),
        ],
        compiler_params=pltpu.CompilerParams(
            collective_id=cid, has_side_effects=True, vmem_limit_bytes=60 * 1024 * 1024),
        cost_estimate=pl.CostEstimate(flops=rows * cols * 6, bytes_accessed=rows * cols * 12, transcendentals=0),
    )(prior, w)


def ring_copies(axis, me, n, src, slot, sems, base):
    right, left = lax.rem(me + 1, n), lax.rem(me + n - 1, n)
    far = lax.rem(me + 2, n)
    send, recv = sems
    half = src.shape[0] // 2

    def rc(s, d, k, dev):
        return pltpu.make_async_remote_copy(
            src_ref=s, dst_ref=d, send_sem=send.at[base + k], recv_sem=recv.at[base + k],
            device_id={axis: dev}, device_id_type=MESH)

    whole = pl.ds(0, 2 * half)
    lo, hi = pl.ds(0, half), pl.ds(half, half)
    first = [rc(src, slot(me, whole), 0, right), rc(src, slot(me, whole), 1, left)]
    arrive = [rc(src, slot(left, whole), 0, left), rc(src, slot(right, whole), 1, right)]
    relay = [
        rc(slot(right, lo), slot(right, lo), 2, left),
        rc(slot(left, hi), slot(left, hi), 3, right),
    ]
    land = [
        rc(slot(far, lo), slot(far, lo), 2, right),
        rc(slot(far, hi), slot(far, hi), 3, left),
    ]
    return first, arrive, relay, land


def gather_kernel(act_in, grad_in, seq_ref, act_out, grad_out, seq_out, act_ref, grad_ref,
                  send, recv, local, seq_send, seq_recv, p0_send, p0_recv, q0_send, q0_recv):
    nx = 4
    ny = 4
    x = lax.axis_index("x")
    y = lax.axis_index("y")
    zh = lax.axis_index("zh")
    xr, xl = lax.rem(x + 1, nx), lax.rem(x + nx - 1, nx)
    yr, yl = lax.rem(y + 1, ny), lax.rem(y + ny - 1, ny)

    nj = 2 * ny
    j = zh * ny + y
    rw = act_ref.shape[2]
    cw = grad_ref.shape[2]

    def plane(jd):
        return {"zh": jd // ny, "y": lax.rem(jd, ny)}

    barrier = pltpu.get_barrier_semaphore()
    for s in range(1, nj):
        pl.semaphore_signal(barrier, 1, device_id=plane(lax.rem(j + s, nj)), device_id_type=MESH)
    for s in range(1, nx):
        pl.semaphore_signal(barrier, 1, device_id={"x": lax.rem(x + s, nx)}, device_id_type=MESH)
    pl.semaphore_wait(barrier, nj - 1 + nx - 1)

    def act_p0(s, jd, js):
        return pltpu.make_async_remote_copy(
            src_ref=act_in.at[:, pl.ds(pl.multiple_of(jd * rw, 128), rw)], dst_ref=act_ref.at[js],
            send_sem=p0_send.at[s], recv_sem=p0_recv.at[s], device_id=plane(jd),
            device_id_type=MESH)

    def grad_p0(s, xd, xs):
        return pltpu.make_async_remote_copy(
            src_ref=grad_in.at[:, pl.ds(pl.multiple_of(xd * cw, 128), cw)], dst_ref=grad_ref.at[xs],
            send_sem=q0_send.at[s], recv_sem=q0_recv.at[s], device_id={"x": xd},
            device_id_type=MESH)

    p0_out = [act_p0(s, lax.rem(j + s, nj), j) for s in range(1, nj)]
    p0_in = [act_p0(s, j, lax.rem(j + nj - s, nj)) for s in range(1, nj)]
    q0_out = [grad_p0(s, lax.rem(x + s, nx), x) for s in range(1, nx)]
    q0_in = [grad_p0(s, x, lax.rem(x + nx - s, nx)) for s in range(1, nx)]
    own0 = [
        pltpu.make_async_copy(
            act_in.at[:, pl.ds(pl.multiple_of(j * rw, 128), rw)], act_ref.at[j], local.at[3]),
        pltpu.make_async_copy(
            grad_in.at[:, pl.ds(pl.multiple_of(x * cw, 128), cw)], grad_ref.at[x], local.at[4]),
    ]
    for c in own0 + q0_out:
        c.start()
    for c in q0_in:
        c.wait_recv()
    own0[1].wait()

    sems = (send, recv)
    a_first, a_arrive, a_relay, a_land = ring_copies(
        "x", x, nx, act_ref, lambda i, p: act_out.at[i, p], sems, 0)
    g_first, g_arrive, g_relay, g_land = ring_copies(
        "y", y, ny, grad_ref, lambda i, p: grad_out.at[p, zh, i], sems, 4)
    p_first, p_arrive, p_relay, p_land = ring_copies(
        "y", y, ny, grad_out.at[:, 1 - zh, y], lambda i, p: grad_out.at[p, 1 - zh, i], sems, 8)
    swap = pltpu.make_async_remote_copy(
        src_ref=grad_ref, dst_ref=grad_out.at[:, zh, y], send_sem=send.at[12],
        recv_sem=recv.at[12], device_id={"zh": 1 - zh}, device_id_type=MESH)
    swap_in = pltpu.make_async_remote_copy(
        src_ref=grad_ref, dst_ref=grad_out.at[:, 1 - zh, y], send_sem=send.at[12],
        recv_sem=recv.at[12], device_id={"zh": 1 - zh}, device_id_type=MESH)

    own = [
        pltpu.make_async_copy(act_ref, act_out.at[x], local.at[0]),
        pltpu.make_async_copy(grad_ref, grad_out.at[:, zh, y], local.at[1]),
        pltpu.make_async_copy(seq_ref, seq_out.at[x], local.at[2]),
    ]

    def sc(s, d, k, dev):
        return pltpu.make_async_remote_copy(
            src_ref=s, dst_ref=d, send_sem=seq_send.at[k], recv_sem=seq_recv.at[k],
            device_id={"x": dev}, device_id_type=MESH)

    seq_first = [sc(seq_ref, seq_out.at[x], 0, xr), sc(seq_ref, seq_out.at[x], 1, xl)]

    swap.start()
    for c in g_first + seq_first + [own[1], own[2]]:
        c.start()
    for c in p0_out:
        c.start()
    swap_in.wait_recv()
    for c in p_first:
        c.start()
    for c in g_arrive:
        c.wait_recv()
    for c in g_relay:
        c.start()
    for c in p0_in:
        c.wait_recv()
    own0[0].wait()
    for c in a_first + [own[0]]:
        c.start()
    for c in p_arrive:
        c.wait_recv()
    for c in p_relay:
        c.start()
    for c in a_arrive:
        c.wait_recv()
    sc(seq_ref, seq_out.at[xl], 0, xl).wait_recv()
    sc(seq_ref, seq_out.at[xr], 1, xr).wait_recv()
    seq_relay = sc(seq_out.at[xr], seq_out.at[xr], 2, xl)
    seq_relay.start()
    for c in a_relay:
        c.start()
    for c in a_land + g_land + p_land:
        c.wait_recv()
    sc(seq_out.at[lax.rem(x + 2, nx)], seq_out.at[lax.rem(x + 2, nx)], 2, xr).wait_recv()
    for c in a_first + a_relay + g_first + g_relay + p_first + p_relay + seq_first:
        c.wait_send()
    seq_relay.wait_send()
    swap.wait_send()
    for c in p0_out + q0_out:
        c.wait_send()
    for c in own:
        c.wait()


def gather_all(act, grad, seq, nj, nx, rw, cw):
    tok = act.shape[0]
    any_space = pl.BlockSpec(memory_space=pl.ANY)
    return pl.pallas_call(
        gather_kernel,
        out_shape=(
            jax.ShapeDtypeStruct((nx, nj, tok, rw), act.dtype),
            jax.ShapeDtypeStruct((nx, 2, nj // 2, tok, cw), grad.dtype),
            jax.ShapeDtypeStruct((nx,) + seq.shape, seq.dtype),
            jax.ShapeDtypeStruct((nj, tok, rw), act.dtype),
            jax.ShapeDtypeStruct((nx, tok, cw), grad.dtype),
        ),
        in_specs=[any_space] * 3,
        out_specs=(any_space,) * 5,
        scratch_shapes=[
            pltpu.SemaphoreType.DMA((13,)),
            pltpu.SemaphoreType.DMA((13,)),
            pltpu.SemaphoreType.DMA((5,)),
            pltpu.SemaphoreType.DMA((3,)),
            pltpu.SemaphoreType.DMA((3,)),
            pltpu.SemaphoreType.DMA((nj,)),
            pltpu.SemaphoreType.DMA((nj,)),
            pltpu.SemaphoreType.DMA((nx,)),
            pltpu.SemaphoreType.DMA((nx,)),
        ],
        compiler_params=pltpu.CompilerParams(collective_id=1, has_side_effects=True),
        cost_estimate=pl.CostEstimate(
            flops=0, bytes_accessed=8 * tok * (nj * rw + 2 * nx * cw), transcendentals=0),
    )(act, grad, seq)


def per_device(activations, out_grads, seq_ids, weights):
    nx = lax.axis_size("x")
    nj = lax.axis_size(("zh", "y"))
    tok = activations.shape[1]
    col_width = weights.shape[2]
    row_width = weights.shape[1]
    total = nx * nj * tok
    act_all, grad_all, owners, _, _ = gather_all(
        activations[0], out_grads[0], seq_ids, nj, nx, row_width, col_width)
    act_all = act_all.reshape(total, row_width)
    grad_all = grad_all.reshape(total, col_width)
    first_long = jnp.sum((owners < 1).astype(jnp.int32)) * (total // owners.size) > total // 2

    def part(lo, hi):
        return lax.dot_general(
            act_all[lo:hi], grad_all[lo:hi], (((0,), (0,)), ((), ())),
            preferred_element_type=jnp.float32,
        )

    quarter = total // 4
    head = part(0, quarter)
    mid = part(quarter, 3 * quarter)
    tail = part(3 * quarter, total)
    g0 = jnp.where(first_long, head + mid, head)
    g1 = jnp.where(first_long, tail, mid + tail)
    fisher = g0 * g0 + g1 * g1
    prior = fisher / SEQS + smoothing
    return mp_merge(prior, weights[0], 2)


def solution(mesh):
    assert mesh.shape["mp"] == 4 and mesh.shape["fsdp"] == 32
    fine = jax.sharding.Mesh(
        mesh.devices.reshape(2, 2, 4, 2, 4), ("zl", "c", "x", "zh", "y")
    )
    mp, fs = ("zl", "c"), ("x", "zh", "y")
    placed = (P(mp, fs, None), P(mp, fs, None), P(mp, fs), P(mp, fs, None))
    return jax.shard_map(
        per_device, mesh=fine, in_specs=placed, out_specs=P(fs, None), check_vma=False
    )
```

```python
import functools

import jax
import jax.numpy as jnp
from jax import lax
from jax.experimental import pallas as pl
from jax.experimental.pallas import tpu as pltpu
from jax.sharding import PartitionSpec as P

F = 7168
SEQS = 2
MESH = pl.DeviceIdType.MESH

smoothing = 0.05


def mp_merge_kernel(prior_ref, w_ref, out_ref, recv_p, recv_w, part, recv2,
                    send_sem, recv_sem, s2_send, s2_recv, s3_send, s3_recv, f_send, f_recv,
                    t_send, t_recv):
    c = lax.axis_index("c")
    z = lax.axis_index("zl")
    rows = prior_ref.shape[0]
    half, quarter = rows // 2, rows // 4
    nb = s2_send.shape[0]
    blk = quarter // nb
    step = 32
    core = {"c": 1 - c}
    chip = {"zl": 1 - z}

    barrier = pltpu.get_barrier_semaphore()
    pl.semaphore_signal(barrier, 1, device_id=core, device_id_type=MESH)
    pl.semaphore_signal(barrier, 1, device_id=chip, device_id_type=MESH)
    pl.semaphore_wait(barrier, 2)

    mine = pl.multiple_of(c * half, half)
    other = pl.multiple_of((1 - c) * half, half)
    my_q = pl.multiple_of(z * quarter, quarter)
    far_q = pl.multiple_of((1 - z) * quarter, quarter)

    def onchip(k, q):
        cp = pltpu.make_async_remote_copy(
            src_ref=prior_ref.at[pl.ds(other + q, quarter)], dst_ref=recv_p.at[pl.ds(q, quarter)],
            send_sem=send_sem.at[k], recv_sem=recv_sem.at[k], device_id=core, device_id_type=MESH)
        cw = pltpu.make_async_remote_copy(
            src_ref=w_ref.at[pl.ds(other + q, quarter)], dst_ref=recv_w.at[pl.ds(q, quarter)],
            send_sem=send_sem.at[2 + k], recv_sem=recv_sem.at[2 + k], device_id=core,
            device_id_type=MESH)
        return [cw, cp]

    def onchip_block(b):
        rows_b = pl.ds(far_q + b * blk, blk)
        cp = pltpu.make_async_remote_copy(
            src_ref=prior_ref.at[pl.ds(other + far_q + b * blk, blk)], dst_ref=recv_p.at[rows_b],
            send_sem=f_send.at[b], recv_sem=f_recv.at[b], device_id=core, device_id_type=MESH)
        cw = pltpu.make_async_remote_copy(
            src_ref=w_ref.at[pl.ds(other + far_q + b * blk, blk)], dst_ref=recv_w.at[rows_b],
            send_sem=f_send.at[nb + b], recv_sem=f_recv.at[nb + b], device_id=core,
            device_id_type=MESH)
        return [cw, cp]

    far_in = [onchip_block(b) for b in range(nb)]
    near_in = onchip(1, my_q)
    for pair in far_in:
        for cp in pair:
            cp.start()
    for cp in near_in:
        cp.start()

    def add(lo, count):
        def body(i, carry):
            r = pl.multiple_of(lo + i * step, step)
            p_me = prior_ref[pl.ds(mine + r, step)]
            p_ot = recv_p[pl.ds(r, step)]
            n_me = p_me * w_ref[pl.ds(mine + r, step)].astype(jnp.float32)
            n_ot = p_ot * recv_w[pl.ds(r, step)].astype(jnp.float32)
            part[0, pl.ds(r, step)] = n_ot + n_me
            part[1, pl.ds(r, step)] = p_ot + p_me
            return carry

        lax.fori_loop(0, count // step, body, 0)

    def second(b, lo):
        return pltpu.make_async_remote_copy(
            src_ref=part.at[:, pl.ds(lo + b * blk, blk)], dst_ref=recv2.at[:, pl.ds(b * blk, blk)],
            send_sem=s2_send.at[b], recv_sem=s2_recv.at[b], device_id=chip, device_id_type=MESH)

    def third(b, q):
        rows_b = pl.ds(mine + q + b * blk, blk)
        return pltpu.make_async_remote_copy(
            src_ref=out_ref.at[rows_b], dst_ref=out_ref.at[rows_b],
            send_sem=s3_send.at[b], recv_sem=s3_recv.at[b], device_id=chip, device_id_type=MESH)

    sent2 = []
    for b in range(nb):
        for cp in far_in[b]:
            cp.wait_recv()
        add(far_q + b * blk, blk)
        cp = second(b, far_q)
        cp.start()
        sent2.append(cp)
    for cp in near_in:
        cp.wait_recv()
    add(my_q, quarter)

    def fourth(k, lo):
        rows_k = pl.ds(lo, blk)
        return pltpu.make_async_remote_copy(
            src_ref=out_ref.at[rows_k], dst_ref=out_ref.at[rows_k],
            send_sem=t_send.at[k], recv_sem=t_recv.at[k], device_id=core, device_id_type=MESH)

    sent3 = []
    sent4 = []
    for b in range(nb):
        second(b, my_q).wait_recv()

        def merge(i, carry):
            r = pl.multiple_of(b * blk + i * step, step)
            n = part[0, pl.ds(my_q + r, step)] + recv2[0, pl.ds(r, step)]
            d = part[1, pl.ds(my_q + r, step)] + recv2[1, pl.ds(r, step)]
            out_ref[pl.ds(mine + my_q + r, step)] = (n / d).astype(out_ref.dtype)
            return carry

        lax.fori_loop(0, blk // step, merge, 0)
        cp = third(b, my_q)
        cp.start()
        sent3.append(cp)
        cp = fourth(b, mine + my_q + b * blk)
        cp.start()
        sent4.append(cp)
    for b in range(nb):
        third(b, far_q).wait_recv()
        cp = fourth(nb + b, mine + far_q + b * blk)
        cp.start()
        sent4.append(cp)
    for b in range(nb):
        fourth(b, other + my_q + b * blk).wait_recv()
        fourth(nb + b, other + far_q + b * blk).wait_recv()
    for cp in sum(far_in, []) + near_in + sent2 + sent3 + sent4:
        cp.wait_send()


def mp_merge(prior, w, cid, blocks=8):
    rows, cols = prior.shape
    vmem = pltpu.MemorySpace.VMEM
    return pl.pallas_call(
        mp_merge_kernel,
        out_shape=jax.ShapeDtypeStruct((rows, cols), jnp.bfloat16),
        in_specs=[pl.BlockSpec(memory_space=vmem)] * 2,
        out_specs=pl.BlockSpec(memory_space=vmem),
        scratch_shapes=[
            pltpu.VMEM((rows // 2, cols), jnp.float32),
            pltpu.VMEM((rows // 2, cols), w.dtype),
            pltpu.VMEM((2, rows // 2, cols), jnp.float32),
            pltpu.VMEM((2, rows // 4, cols), jnp.float32),
            pltpu.SemaphoreType.DMA((5,)),
            pltpu.SemaphoreType.DMA((5,)),
            pltpu.SemaphoreType.DMA((blocks,)),
            pltpu.SemaphoreType.DMA((blocks,)),
            pltpu.SemaphoreType.DMA((blocks,)),
            pltpu.SemaphoreType.DMA((blocks,)),
            pltpu.SemaphoreType.DMA((2 * blocks,)),
            pltpu.SemaphoreType.DMA((2 * blocks,)),
            pltpu.SemaphoreType.DMA((2 * blocks,)),
            pltpu.SemaphoreType.DMA((2 * blocks,)),
        ],
        compiler_params=pltpu.CompilerParams(
            collective_id=cid, has_side_effects=True, vmem_limit_bytes=60 * 1024 * 1024),
        cost_estimate=pl.CostEstimate(flops=rows * cols * 6, bytes_accessed=rows * cols * 12, transcendentals=0),
    )(prior, w)


def ring_copies(axis, me, n, src, slot, sems, base):
    right, left = lax.rem(me + 1, n), lax.rem(me + n - 1, n)
    far = lax.rem(me + 2, n)
    send, recv = sems
    half = src.shape[0] // 2

    def rc(s, d, k, dev):
        return pltpu.make_async_remote_copy(
            src_ref=s, dst_ref=d, send_sem=send.at[base + k], recv_sem=recv.at[base + k],
            device_id={axis: dev}, device_id_type=MESH)

    whole = pl.ds(0, 2 * half)
    lo, hi = pl.ds(0, half), pl.ds(half, half)
    first = [rc(src, slot(me, whole), 0, right), rc(src, slot(me, whole), 1, left)]
    arrive = [rc(src, slot(left, whole), 0, left), rc(src, slot(right, whole), 1, right)]
    relay = [
        rc(slot(right, lo), slot(right, lo), 2, left),
        rc(slot(left, hi), slot(left, hi), 3, right),
    ]
    land = [
        rc(slot(far, lo), slot(far, lo), 2, right),
        rc(slot(far, hi), slot(far, hi), 3, left),
    ]
    return first, arrive, relay, land


def gather_kernel(act_in, grad_in, seq_ref, act_out, grad_out, seq_out, act_ref, grad_ref,
                  send, recv, local, seq_send, seq_recv, p0_send, p0_recv, q0_send, q0_recv):
    nx = 4
    ny = 4
    x = lax.axis_index("x")
    y = lax.axis_index("y")
    zh = lax.axis_index("zh")
    xr, xl = lax.rem(x + 1, nx), lax.rem(x + nx - 1, nx)
    yr, yl = lax.rem(y + 1, ny), lax.rem(y + ny - 1, ny)

    nj = 2 * ny
    j = zh * ny + y
    rw = act_ref.shape[2]
    cw = grad_ref.shape[2]

    def plane(jd):
        return {"zh": jd // ny, "y": lax.rem(jd, ny)}

    barrier = pltpu.get_barrier_semaphore()
    for s in range(1, nj):
        pl.semaphore_signal(barrier, 1, device_id=plane(lax.rem(j + s, nj)), device_id_type=MESH)
    for s in range(1, nx):
        pl.semaphore_signal(barrier, 1, device_id={"x": lax.rem(x + s, nx)}, device_id_type=MESH)
    pl.semaphore_wait(barrier, nj - 1 + nx - 1)

    def act_p0(s, jd, js):
        return pltpu.make_async_remote_copy(
            src_ref=act_in.at[:, pl.ds(pl.multiple_of(jd * rw, 128), rw)], dst_ref=act_ref.at[js],
            send_sem=p0_send.at[s], recv_sem=p0_recv.at[s], device_id=plane(jd),
            device_id_type=MESH)

    def grad_p0(s, xd, xs):
        return pltpu.make_async_remote_copy(
            src_ref=grad_in.at[:, pl.ds(pl.multiple_of(xd * cw, 128), cw)], dst_ref=grad_ref.at[xs],
            send_sem=q0_send.at[s], recv_sem=q0_recv.at[s], device_id={"x": xd},
            device_id_type=MESH)

    p0_out = [act_p0(s, lax.rem(j + s, nj), j) for s in range(1, nj)]
    p0_in = [act_p0(s, j, lax.rem(j + nj - s, nj)) for s in range(1, nj)]
    q0_out = [grad_p0(s, lax.rem(x + s, nx), x) for s in range(1, nx)]
    q0_in = [grad_p0(s, x, lax.rem(x + nx - s, nx)) for s in range(1, nx)]
    own0 = [
        pltpu.make_async_copy(
            act_in.at[:, pl.ds(pl.multiple_of(j * rw, 128), rw)], act_ref.at[j], local.at[3]),
        pltpu.make_async_copy(
            grad_in.at[:, pl.ds(pl.multiple_of(x * cw, 128), cw)], grad_ref.at[x], local.at[4]),
    ]
    for c in own0 + q0_out + p0_out:
        c.start()
    for c in q0_in:
        c.wait_recv()
    own0[1].wait()

    sems = (send, recv)
    a_first, a_arrive, a_relay, a_land = ring_copies(
        "x", x, nx, act_ref, lambda i, p: act_out.at[i, p], sems, 0)
    g_first, g_arrive, g_relay, g_land = ring_copies(
        "y", y, ny, grad_ref, lambda i, p: grad_out.at[p, zh, i], sems, 4)
    p_first, p_arrive, p_relay, p_land = ring_copies(
        "y", y, ny, grad_out.at[:, 1 - zh, y], lambda i, p: grad_out.at[p, 1 - zh, i], sems, 8)
    swap = pltpu.make_async_remote_copy(
        src_ref=grad_ref, dst_ref=grad_out.at[:, zh, y], send_sem=send.at[12],
        recv_sem=recv.at[12], device_id={"zh": 1 - zh}, device_id_type=MESH)
    swap_in = pltpu.make_async_remote_copy(
        src_ref=grad_ref, dst_ref=grad_out.at[:, 1 - zh, y], send_sem=send.at[12],
        recv_sem=recv.at[12], device_id={"zh": 1 - zh}, device_id_type=MESH)

    own = [
        pltpu.make_async_copy(act_ref, act_out.at[x], local.at[0]),
        pltpu.make_async_copy(grad_ref, grad_out.at[:, zh, y], local.at[1]),
        pltpu.make_async_copy(seq_ref, seq_out.at[x], local.at[2]),
    ]

    def sc(s, d, k, dev):
        return pltpu.make_async_remote_copy(
            src_ref=s, dst_ref=d, send_sem=seq_send.at[k], recv_sem=seq_recv.at[k],
            device_id={"x": dev}, device_id_type=MESH)

    seq_first = [sc(seq_ref, seq_out.at[x], 0, xr), sc(seq_ref, seq_out.at[x], 1, xl)]

    swap.start()
    for c in g_first + seq_first + [own[1], own[2]]:
        c.start()
    for c in p0_in:
        c.wait_recv()
    own0[0].wait()
    for c in a_first + [own[0]]:
        c.start()
    swap_in.wait_recv()
    for c in p_first:
        c.start()
    for c in g_arrive:
        c.wait_recv()
    for c in g_relay:
        c.start()
    for c in p_arrive:
        c.wait_recv()
    for c in p_relay:
        c.start()
    for c in a_arrive:
        c.wait_recv()
    sc(seq_ref, seq_out.at[xl], 0, xl).wait_recv()
    sc(seq_ref, seq_out.at[xr], 1, xr).wait_recv()
    seq_relay = sc(seq_out.at[xr], seq_out.at[xr], 2, xl)
    seq_relay.start()
    for c in a_relay:
        c.start()
    for c in a_land + g_land + p_land:
        c.wait_recv()
    sc(seq_out.at[lax.rem(x + 2, nx)], seq_out.at[lax.rem(x + 2, nx)], 2, xr).wait_recv()
    for c in a_first + a_relay + g_first + g_relay + p_first + p_relay + seq_first:
        c.wait_send()
    seq_relay.wait_send()
    swap.wait_send()
    for c in p0_out + q0_out:
        c.wait_send()
    for c in own:
        c.wait()


def gather_all(act, grad, seq, nj, nx, rw, cw):
    tok = act.shape[0]
    any_space = pl.BlockSpec(memory_space=pl.ANY)
    return pl.pallas_call(
        gather_kernel,
        out_shape=(
            jax.ShapeDtypeStruct((nx, nj, tok, rw), act.dtype),
            jax.ShapeDtypeStruct((nx, 2, nj // 2, tok, cw), grad.dtype),
            jax.ShapeDtypeStruct((nx,) + seq.shape, seq.dtype),
            jax.ShapeDtypeStruct((nj, tok, rw), act.dtype),
            jax.ShapeDtypeStruct((nx, tok, cw), grad.dtype),
        ),
        in_specs=[any_space] * 3,
        out_specs=(any_space,) * 5,
        scratch_shapes=[
            pltpu.SemaphoreType.DMA((13,)),
            pltpu.SemaphoreType.DMA((13,)),
            pltpu.SemaphoreType.DMA((5,)),
            pltpu.SemaphoreType.DMA((3,)),
            pltpu.SemaphoreType.DMA((3,)),
            pltpu.SemaphoreType.DMA((nj,)),
            pltpu.SemaphoreType.DMA((nj,)),
            pltpu.SemaphoreType.DMA((nx,)),
            pltpu.SemaphoreType.DMA((nx,)),
        ],
        compiler_params=pltpu.CompilerParams(collective_id=1, has_side_effects=True),
        cost_estimate=pl.CostEstimate(
            flops=0, bytes_accessed=8 * tok * (nj * rw + 2 * nx * cw), transcendentals=0),
    )(act, grad, seq)


def per_device(activations, out_grads, seq_ids, weights):
    nx = lax.axis_size("x")
    nj = lax.axis_size(("zh", "y"))
    tok = activations.shape[1]
    col_width = weights.shape[2]
    row_width = weights.shape[1]
    total = nx * nj * tok
    act_all, grad_all, owners, _, _ = gather_all(
        activations[0], out_grads[0], seq_ids, nj, nx, row_width, col_width)
    act_all = act_all.reshape(total, row_width)
    grad_all = grad_all.reshape(total, col_width)
    first_long = jnp.sum((owners < 1).astype(jnp.int32)) * (total // owners.size) > total // 2

    def part(lo, hi):
        return lax.dot_general(
            act_all[lo:hi], grad_all[lo:hi], (((0,), (0,)), ((), ())),
            preferred_element_type=jnp.float32,
        )

    quarter = total // 4
    head = part(0, quarter)
    mid = part(quarter, 3 * quarter)
    tail = part(3 * quarter, total)
    g0 = jnp.where(first_long, head + mid, head)
    g1 = jnp.where(first_long, tail, mid + tail)
    fisher = g0 * g0 + g1 * g1
    prior = fisher / SEQS + smoothing
    return mp_merge(prior, weights[0], 2)


def solution(mesh):
    assert mesh.shape["mp"] == 4 and mesh.shape["fsdp"] == 32
    fine = jax.sharding.Mesh(
        mesh.devices.reshape(2, 2, 4, 2, 4), ("zl", "c", "x", "zh", "y")
    )
    mp, fs = ("zl", "c"), ("x", "zh", "y")
    placed = (P(mp, fs, None), P(mp, fs, None), P(mp, fs), P(mp, fs, None))
    return jax.shard_map(
        per_device, mesh=fine, in_specs=placed, out_specs=P(fs, None), check_vma=False
    )
```

```python
import functools

import jax
import jax.numpy as jnp
from jax import lax
from jax.experimental import pallas as pl
from jax.experimental.pallas import tpu as pltpu
from jax.sharding import PartitionSpec as P

F = 7168
SEQS = 2
MESH = pl.DeviceIdType.MESH

smoothing = 0.05


def mp_merge_kernel(prior_ref, w_ref, out_ref, recv_p, recv_w, part, recv2,
                    send_sem, recv_sem, s2_send, s2_recv, s3_send, s3_recv, f_send, f_recv,
                    t_send, t_recv):
    c = lax.axis_index("c")
    z = lax.axis_index("zl")
    rows = prior_ref.shape[0]
    half, quarter = rows // 2, rows // 4
    nb = s2_send.shape[0]
    blk = quarter // nb
    step = 32
    core = {"c": 1 - c}
    chip = {"zl": 1 - z}

    barrier = pltpu.get_barrier_semaphore()
    pl.semaphore_signal(barrier, 1, device_id=core, device_id_type=MESH)
    pl.semaphore_signal(barrier, 1, device_id=chip, device_id_type=MESH)
    pl.semaphore_wait(barrier, 2)

    mine = pl.multiple_of(c * half, half)
    other = pl.multiple_of((1 - c) * half, half)
    my_q = pl.multiple_of(z * quarter, quarter)
    far_q = pl.multiple_of((1 - z) * quarter, quarter)

    def onchip(k, q):
        cp = pltpu.make_async_remote_copy(
            src_ref=prior_ref.at[pl.ds(other + q, quarter)], dst_ref=recv_p.at[pl.ds(q, quarter)],
            send_sem=send_sem.at[k], recv_sem=recv_sem.at[k], device_id=core, device_id_type=MESH)
        cw = pltpu.make_async_remote_copy(
            src_ref=w_ref.at[pl.ds(other + q, quarter)], dst_ref=recv_w.at[pl.ds(q, quarter)],
            send_sem=send_sem.at[2 + k], recv_sem=recv_sem.at[2 + k], device_id=core,
            device_id_type=MESH)
        return [cw, cp]

    def onchip_block(b):
        rows_b = pl.ds(far_q + b * blk, blk)
        cp = pltpu.make_async_remote_copy(
            src_ref=prior_ref.at[pl.ds(other + far_q + b * blk, blk)], dst_ref=recv_p.at[rows_b],
            send_sem=f_send.at[b], recv_sem=f_recv.at[b], device_id=core, device_id_type=MESH)
        cw = pltpu.make_async_remote_copy(
            src_ref=w_ref.at[pl.ds(other + far_q + b * blk, blk)], dst_ref=recv_w.at[rows_b],
            send_sem=f_send.at[nb + b], recv_sem=f_recv.at[nb + b], device_id=core,
            device_id_type=MESH)
        return [cw, cp]

    far_in = [onchip_block(b) for b in range(nb)]
    near_in = onchip(1, my_q)
    for pair in far_in:
        for cp in pair:
            cp.start()
    for cp in near_in:
        cp.start()

    def add(lo, count):
        def body(i, carry):
            r = pl.multiple_of(lo + i * step, step)
            p_me = prior_ref[pl.ds(mine + r, step)]
            p_ot = recv_p[pl.ds(r, step)]
            n_me = p_me * w_ref[pl.ds(mine + r, step)].astype(jnp.float32)
            n_ot = p_ot * recv_w[pl.ds(r, step)].astype(jnp.float32)
            part[0, pl.ds(r, step)] = n_ot + n_me
            part[1, pl.ds(r, step)] = p_ot + p_me
            return carry

        lax.fori_loop(0, count // step, body, 0)

    def second(b, lo):
        return pltpu.make_async_remote_copy(
            src_ref=part.at[:, pl.ds(lo + b * blk, blk)], dst_ref=recv2.at[:, pl.ds(b * blk, blk)],
            send_sem=s2_send.at[b], recv_sem=s2_recv.at[b], device_id=chip, device_id_type=MESH)

    def third(b, q):
        rows_b = pl.ds(mine + q + b * blk, blk)
        return pltpu.make_async_remote_copy(
            src_ref=out_ref.at[rows_b], dst_ref=out_ref.at[rows_b],
            send_sem=s3_send.at[b], recv_sem=s3_recv.at[b], device_id=chip, device_id_type=MESH)

    sent2 = []
    for b in range(nb):
        for cp in far_in[b]:
            cp.wait_recv()
        add(far_q + b * blk, blk)
        cp = second(b, far_q)
        cp.start()
        sent2.append(cp)
    for cp in near_in:
        cp.wait_recv()
    add(my_q, quarter)

    def fourth(k, lo):
        rows_k = pl.ds(lo, blk)
        return pltpu.make_async_remote_copy(
            src_ref=out_ref.at[rows_k], dst_ref=out_ref.at[rows_k],
            send_sem=t_send.at[k], recv_sem=t_recv.at[k], device_id=core, device_id_type=MESH)

    sent3 = []
    sent4 = []
    for b in range(nb):
        second(b, my_q).wait_recv()

        def merge(i, carry):
            r = pl.multiple_of(b * blk + i * step, step)
            n = part[0, pl.ds(my_q + r, step)] + recv2[0, pl.ds(r, step)]
            d = part[1, pl.ds(my_q + r, step)] + recv2[1, pl.ds(r, step)]
            out_ref[pl.ds(mine + my_q + r, step)] = (n / d).astype(out_ref.dtype)
            return carry

        lax.fori_loop(0, blk // step, merge, 0)
        cp = third(b, my_q)
        cp.start()
        sent3.append(cp)
        cp = fourth(b, mine + my_q + b * blk)
        cp.start()
        sent4.append(cp)
    for b in range(nb):
        third(b, far_q).wait_recv()
        cp = fourth(nb + b, mine + far_q + b * blk)
        cp.start()
        sent4.append(cp)
    for b in range(nb):
        fourth(b, other + my_q + b * blk).wait_recv()
        fourth(nb + b, other + far_q + b * blk).wait_recv()
    for cp in sum(far_in, []) + near_in + sent2 + sent3 + sent4:
        cp.wait_send()


def mp_merge(prior, w, cid, blocks=8):
    rows, cols = prior.shape
    vmem = pltpu.MemorySpace.VMEM
    return pl.pallas_call(
        mp_merge_kernel,
        out_shape=jax.ShapeDtypeStruct((rows, cols), jnp.bfloat16),
        in_specs=[pl.BlockSpec(memory_space=vmem)] * 2,
        out_specs=pl.BlockSpec(memory_space=vmem),
        scratch_shapes=[
            pltpu.VMEM((rows // 2, cols), jnp.float32),
            pltpu.VMEM((rows // 2, cols), w.dtype),
            pltpu.VMEM((2, rows // 2, cols), jnp.float32),
            pltpu.VMEM((2, rows // 4, cols), jnp.float32),
            pltpu.SemaphoreType.DMA((5,)),
            pltpu.SemaphoreType.DMA((5,)),
            pltpu.SemaphoreType.DMA((blocks,)),
            pltpu.SemaphoreType.DMA((blocks,)),
            pltpu.SemaphoreType.DMA((blocks,)),
            pltpu.SemaphoreType.DMA((blocks,)),
            pltpu.SemaphoreType.DMA((2 * blocks,)),
            pltpu.SemaphoreType.DMA((2 * blocks,)),
            pltpu.SemaphoreType.DMA((2 * blocks,)),
            pltpu.SemaphoreType.DMA((2 * blocks,)),
        ],
        compiler_params=pltpu.CompilerParams(
            collective_id=cid, has_side_effects=True, vmem_limit_bytes=60 * 1024 * 1024),
        cost_estimate=pl.CostEstimate(flops=rows * cols * 6, bytes_accessed=rows * cols * 12, transcendentals=0),
    )(prior, w)


def ring_copies(axis, me, n, src, slot, sems, base):
    right, left = lax.rem(me + 1, n), lax.rem(me + n - 1, n)
    far = lax.rem(me + 2, n)
    send, recv = sems
    half = src.shape[0] // 2

    def rc(s, d, k, dev):
        return pltpu.make_async_remote_copy(
            src_ref=s, dst_ref=d, send_sem=send.at[base + k], recv_sem=recv.at[base + k],
            device_id={axis: dev}, device_id_type=MESH)

    whole = pl.ds(0, 2 * half)
    lo, hi = pl.ds(0, half), pl.ds(half, half)
    first = [rc(src, slot(me, whole), 0, right), rc(src, slot(me, whole), 1, left)]
    arrive = [rc(src, slot(left, whole), 0, left), rc(src, slot(right, whole), 1, right)]
    relay = [
        rc(slot(right, lo), slot(right, lo), 2, left),
        rc(slot(left, hi), slot(left, hi), 3, right),
    ]
    land = [
        rc(slot(far, lo), slot(far, lo), 2, right),
        rc(slot(far, hi), slot(far, hi), 3, left),
    ]
    return first, arrive, relay, land


def gather_kernel(act_in, grad_in, seq_ref, act_out, grad_out, seq_out, act_ref, grad_ref,
                  send, recv, local, seq_send, seq_recv, p0_send, p0_recv, q0_send, q0_recv):
    nx = 4
    ny = 4
    x = lax.axis_index("x")
    y = lax.axis_index("y")
    zh = lax.axis_index("zh")
    xr, xl = lax.rem(x + 1, nx), lax.rem(x + nx - 1, nx)
    yr, yl = lax.rem(y + 1, ny), lax.rem(y + ny - 1, ny)

    nj = 2 * ny
    j = zh * ny + y
    rw = act_ref.shape[2]
    cw = grad_ref.shape[2]

    def plane(jd):
        return {"zh": jd // ny, "y": lax.rem(jd, ny)}

    barrier = pltpu.get_barrier_semaphore()
    for s in range(1, nj):
        pl.semaphore_signal(barrier, 1, device_id=plane(lax.rem(j + s, nj)), device_id_type=MESH)
    for s in range(1, nx):
        pl.semaphore_signal(barrier, 1, device_id={"x": lax.rem(x + s, nx)}, device_id_type=MESH)
    pl.semaphore_wait(barrier, nj - 1 + nx - 1)

    def act_p0(s, jd, js):
        return pltpu.make_async_remote_copy(
            src_ref=act_in.at[:, pl.ds(pl.multiple_of(jd * rw, 128), rw)], dst_ref=act_ref.at[js],
            send_sem=p0_send.at[s], recv_sem=p0_recv.at[s], device_id=plane(jd),
            device_id_type=MESH)

    def grad_p0(s, xd, xs):
        return pltpu.make_async_remote_copy(
            src_ref=grad_in.at[:, pl.ds(pl.multiple_of(xd * cw, 128), cw)], dst_ref=grad_ref.at[xs],
            send_sem=q0_send.at[s], recv_sem=q0_recv.at[s], device_id={"x": xd},
            device_id_type=MESH)

    p0_out = [act_p0(s, lax.rem(j + s, nj), j) for s in range(1, nj)]
    p0_in = [act_p0(s, j, lax.rem(j + nj - s, nj)) for s in range(1, nj)]
    q0_out = [grad_p0(s, lax.rem(x + s, nx), x) for s in range(1, nx)]
    q0_in = [grad_p0(s, x, lax.rem(x + nx - s, nx)) for s in range(1, nx)]
    own0 = [
        pltpu.make_async_copy(
            act_in.at[:, pl.ds(pl.multiple_of(j * rw, 128), rw)], act_ref.at[j], local.at[3]),
        pltpu.make_async_copy(
            grad_in.at[:, pl.ds(pl.multiple_of(x * cw, 128), cw)], grad_ref.at[x], local.at[4]),
    ]
    for c in own0 + q0_out + p0_out:
        c.start()
    for c in q0_in:
        c.wait_recv()
    own0[1].wait()

    sems = (send, recv)
    a_first, a_arrive, a_relay, a_land = ring_copies(
        "x", x, nx, act_ref, lambda i, p: act_out.at[i, p], sems, 0)
    g_first, g_arrive, g_relay, g_land = ring_copies(
        "y", y, ny, grad_ref, lambda i, p: grad_out.at[p, zh, i], sems, 4)
    p_first, p_arrive, p_relay, p_land = ring_copies(
        "y", y, ny, grad_out.at[:, 1 - zh, y], lambda i, p: grad_out.at[p, 1 - zh, i], sems, 8)
    swap = pltpu.make_async_remote_copy(
        src_ref=grad_ref, dst_ref=grad_out.at[:, zh, y], send_sem=send.at[12],
        recv_sem=recv.at[12], device_id={"zh": 1 - zh}, device_id_type=MESH)
    swap_in = pltpu.make_async_remote_copy(
        src_ref=grad_ref, dst_ref=grad_out.at[:, 1 - zh, y], send_sem=send.at[12],
        recv_sem=recv.at[12], device_id={"zh": 1 - zh}, device_id_type=MESH)

    own = [
        pltpu.make_async_copy(act_ref, act_out.at[x], local.at[0]),
        pltpu.make_async_copy(grad_ref, grad_out.at[:, zh, y], local.at[1]),
        pltpu.make_async_copy(seq_ref, seq_out.at[x], local.at[2]),
    ]

    def sc(s, d, k, dev):
        return pltpu.make_async_remote_copy(
            src_ref=s, dst_ref=d, send_sem=seq_send.at[k], recv_sem=seq_recv.at[k],
            device_id={"x": dev}, device_id_type=MESH)

    seq_first = [sc(seq_ref, seq_out.at[x], 0, xr), sc(seq_ref, seq_out.at[x], 1, xl)]

    swap.start()
    for c in g_first + seq_first + [own[1], own[2]]:
        c.start()
    for c in p0_in:
        c.wait_recv()
    own0[0].wait()
    for c in a_first + [own[0]]:
        c.start()
    swap_in.wait_recv()
    for c in p_first:
        c.start()
    for c in g_arrive:
        c.wait_recv()
    for c in g_relay:
        c.start()
    for c in a_arrive:
        c.wait_recv()
    for c in a_relay:
        c.start()
    for c in p_arrive:
        c.wait_recv()
    for c in p_relay:
        c.start()
    sc(seq_ref, seq_out.at[xl], 0, xl).wait_recv()
    sc(seq_ref, seq_out.at[xr], 1, xr).wait_recv()
    seq_relay = sc(seq_out.at[xr], seq_out.at[xr], 2, xl)
    seq_relay.start()
    for c in a_land + g_land + p_land:
        c.wait_recv()
    sc(seq_out.at[lax.rem(x + 2, nx)], seq_out.at[lax.rem(x + 2, nx)], 2, xr).wait_recv()
    for c in a_first + a_relay + g_first + g_relay + p_first + p_relay + seq_first:
        c.wait_send()
    seq_relay.wait_send()
    swap.wait_send()
    for c in p0_out + q0_out:
        c.wait_send()
    for c in own:
        c.wait()


def gather_all(act, grad, seq, nj, nx, rw, cw):
    tok = act.shape[0]
    any_space = pl.BlockSpec(memory_space=pl.ANY)
    return pl.pallas_call(
        gather_kernel,
        out_shape=(
            jax.ShapeDtypeStruct((nx, nj, tok, rw), act.dtype),
            jax.ShapeDtypeStruct((nx, 2, nj // 2, tok, cw), grad.dtype),
            jax.ShapeDtypeStruct((nx,) + seq.shape, seq.dtype),
            jax.ShapeDtypeStruct((nj, tok, rw), act.dtype),
            jax.ShapeDtypeStruct((nx, tok, cw), grad.dtype),
        ),
        in_specs=[any_space] * 3,
        out_specs=(any_space,) * 5,
        scratch_shapes=[
            pltpu.SemaphoreType.DMA((13,)),
            pltpu.SemaphoreType.DMA((13,)),
            pltpu.SemaphoreType.DMA((5,)),
            pltpu.SemaphoreType.DMA((3,)),
            pltpu.SemaphoreType.DMA((3,)),
            pltpu.SemaphoreType.DMA((nj,)),
            pltpu.SemaphoreType.DMA((nj,)),
            pltpu.SemaphoreType.DMA((nx,)),
            pltpu.SemaphoreType.DMA((nx,)),
        ],
        compiler_params=pltpu.CompilerParams(collective_id=1, has_side_effects=True),
        cost_estimate=pl.CostEstimate(
            flops=0, bytes_accessed=8 * tok * (nj * rw + 2 * nx * cw), transcendentals=0),
    )(act, grad, seq)


def per_device(activations, out_grads, seq_ids, weights):
    nx = lax.axis_size("x")
    nj = lax.axis_size(("zh", "y"))
    tok = activations.shape[1]
    col_width = weights.shape[2]
    row_width = weights.shape[1]
    total = nx * nj * tok
    act_all, grad_all, owners, _, _ = gather_all(
        activations[0], out_grads[0], seq_ids, nj, nx, row_width, col_width)
    act_all = act_all.reshape(total, row_width)
    grad_all = grad_all.reshape(total, col_width)
    first_long = jnp.sum((owners < 1).astype(jnp.int32)) * (total // owners.size) > total // 2

    def part(lo, hi):
        return lax.dot_general(
            act_all[lo:hi], grad_all[lo:hi], (((0,), (0,)), ((), ())),
            preferred_element_type=jnp.float32,
        )

    quarter = total // 4
    head = part(0, quarter)
    mid = part(quarter, 3 * quarter)
    tail = part(3 * quarter, total)
    g0 = jnp.where(first_long, head + mid, head)
    g1 = jnp.where(first_long, tail, mid + tail)
    fisher = g0 * g0 + g1 * g1
    prior = fisher / SEQS + smoothing
    return mp_merge(prior, weights[0], 2)


def solution(mesh):
    assert mesh.shape["mp"] == 4 and mesh.shape["fsdp"] == 32
    fine = jax.sharding.Mesh(
        mesh.devices.reshape(2, 2, 4, 2, 4), ("zl", "c", "x", "zh", "y")
    )
    mp, fs = ("zl", "c"), ("x", "zh", "y")
    placed = (P(mp, fs, None), P(mp, fs, None), P(mp, fs), P(mp, fs, None))
    return jax.shard_map(
        per_device, mesh=fine, in_specs=placed, out_specs=P(fs, None), check_vma=False
    )
```

```python
import functools

import jax
import jax.numpy as jnp
from jax import lax
from jax.experimental import pallas as pl
from jax.experimental.pallas import tpu as pltpu
from jax.sharding import PartitionSpec as P

F = 7168
SEQS = 2
MESH = pl.DeviceIdType.MESH

smoothing = 0.05


def mp_merge_kernel(prior_ref, w_ref, out_ref, recv_p, recv_w, part, recv2,
                    send_sem, recv_sem, s2_send, s2_recv, s3_send, s3_recv, f_send, f_recv,
                    t_send, t_recv):
    c = lax.axis_index("c")
    z = lax.axis_index("zl")
    rows = prior_ref.shape[0]
    half, quarter = rows // 2, rows // 4
    nb = s2_send.shape[0]
    blk = quarter // nb
    step = min(32, blk)
    core = {"c": 1 - c}
    chip = {"zl": 1 - z}

    barrier = pltpu.get_barrier_semaphore()
    pl.semaphore_signal(barrier, 1, device_id=core, device_id_type=MESH)
    pl.semaphore_signal(barrier, 1, device_id=chip, device_id_type=MESH)
    pl.semaphore_wait(barrier, 2)

    mine = pl.multiple_of(c * half, half)
    other = pl.multiple_of((1 - c) * half, half)
    my_q = pl.multiple_of(z * quarter, quarter)
    far_q = pl.multiple_of((1 - z) * quarter, quarter)

    def onchip(k, q):
        cp = pltpu.make_async_remote_copy(
            src_ref=prior_ref.at[pl.ds(other + q, quarter)], dst_ref=recv_p.at[pl.ds(q, quarter)],
            send_sem=send_sem.at[k], recv_sem=recv_sem.at[k], device_id=core, device_id_type=MESH)
        cw = pltpu.make_async_remote_copy(
            src_ref=w_ref.at[pl.ds(other + q, quarter)], dst_ref=recv_w.at[pl.ds(q, quarter)],
            send_sem=send_sem.at[2 + k], recv_sem=recv_sem.at[2 + k], device_id=core,
            device_id_type=MESH)
        return [cw, cp]

    def onchip_block(b):
        rows_b = pl.ds(far_q + b * blk, blk)
        cp = pltpu.make_async_remote_copy(
            src_ref=prior_ref.at[pl.ds(other + far_q + b * blk, blk)], dst_ref=recv_p.at[rows_b],
            send_sem=f_send.at[b], recv_sem=f_recv.at[b], device_id=core, device_id_type=MESH)
        cw = pltpu.make_async_remote_copy(
            src_ref=w_ref.at[pl.ds(other + far_q + b * blk, blk)], dst_ref=recv_w.at[rows_b],
            send_sem=f_send.at[nb + b], recv_sem=f_recv.at[nb + b], device_id=core,
            device_id_type=MESH)
        return [cw, cp]

    far_in = [onchip_block(b) for b in range(nb)]
    near_in = onchip(1, my_q)
    for pair in far_in:
        for cp in pair:
            cp.start()
    for cp in near_in:
        cp.start()

    def add(lo, count):
        def body(i, carry):
            r = pl.multiple_of(lo + i * step, step)
            p_me = prior_ref[pl.ds(mine + r, step)]
            p_ot = recv_p[pl.ds(r, step)]
            n_me = p_me * w_ref[pl.ds(mine + r, step)].astype(jnp.float32)
            n_ot = p_ot * recv_w[pl.ds(r, step)].astype(jnp.float32)
            part[0, pl.ds(r, step)] = n_ot + n_me
            part[1, pl.ds(r, step)] = p_ot + p_me
            return carry

        lax.fori_loop(0, count // step, body, 0)

    def second(b, lo):
        return pltpu.make_async_remote_copy(
            src_ref=part.at[:, pl.ds(lo + b * blk, blk)], dst_ref=recv2.at[:, pl.ds(b * blk, blk)],
            send_sem=s2_send.at[b], recv_sem=s2_recv.at[b], device_id=chip, device_id_type=MESH)

    def third(b, q):
        rows_b = pl.ds(mine + q + b * blk, blk)
        return pltpu.make_async_remote_copy(
            src_ref=out_ref.at[rows_b], dst_ref=out_ref.at[rows_b],
            send_sem=s3_send.at[b], recv_sem=s3_recv.at[b], device_id=chip, device_id_type=MESH)

    sent2 = []
    for b in range(nb):
        for cp in far_in[b]:
            cp.wait_recv()
        add(far_q + b * blk, blk)
        cp = second(b, far_q)
        cp.start()
        sent2.append(cp)
    for cp in near_in:
        cp.wait_recv()
    add(my_q, quarter)

    def fourth(k, lo):
        rows_k = pl.ds(lo, blk)
        return pltpu.make_async_remote_copy(
            src_ref=out_ref.at[rows_k], dst_ref=out_ref.at[rows_k],
            send_sem=t_send.at[k], recv_sem=t_recv.at[k], device_id=core, device_id_type=MESH)

    sent3 = []
    sent4 = []
    for b in range(nb):
        second(b, my_q).wait_recv()

        def merge(i, carry):
            r = pl.multiple_of(b * blk + i * step, step)
            n = part[0, pl.ds(my_q + r, step)] + recv2[0, pl.ds(r, step)]
            d = part[1, pl.ds(my_q + r, step)] + recv2[1, pl.ds(r, step)]
            out_ref[pl.ds(mine + my_q + r, step)] = (n / d).astype(out_ref.dtype)
            return carry

        lax.fori_loop(0, blk // step, merge, 0)
        cp = third(b, my_q)
        cp.start()
        sent3.append(cp)
        cp = fourth(b, mine + my_q + b * blk)
        cp.start()
        sent4.append(cp)
    for b in range(nb):
        third(b, far_q).wait_recv()
        cp = fourth(nb + b, mine + far_q + b * blk)
        cp.start()
        sent4.append(cp)
    for b in range(nb):
        fourth(b, other + my_q + b * blk).wait_recv()
        fourth(nb + b, other + far_q + b * blk).wait_recv()
    for cp in sum(far_in, []) + near_in + sent2 + sent3 + sent4:
        cp.wait_send()


def mp_merge(prior, w, cid, blocks=16):
    rows, cols = prior.shape
    vmem = pltpu.MemorySpace.VMEM
    return pl.pallas_call(
        mp_merge_kernel,
        out_shape=jax.ShapeDtypeStruct((rows, cols), jnp.bfloat16),
        in_specs=[pl.BlockSpec(memory_space=vmem)] * 2,
        out_specs=pl.BlockSpec(memory_space=vmem),
        scratch_shapes=[
            pltpu.VMEM((rows // 2, cols), jnp.float32),
            pltpu.VMEM((rows // 2, cols), w.dtype),
            pltpu.VMEM((2, rows // 2, cols), jnp.float32),
            pltpu.VMEM((2, rows // 4, cols), jnp.float32),
            pltpu.SemaphoreType.DMA((5,)),
            pltpu.SemaphoreType.DMA((5,)),
            pltpu.SemaphoreType.DMA((blocks,)),
            pltpu.SemaphoreType.DMA((blocks,)),
            pltpu.SemaphoreType.DMA((blocks,)),
            pltpu.SemaphoreType.DMA((blocks,)),
            pltpu.SemaphoreType.DMA((2 * blocks,)),
            pltpu.SemaphoreType.DMA((2 * blocks,)),
            pltpu.SemaphoreType.DMA((2 * blocks,)),
            pltpu.SemaphoreType.DMA((2 * blocks,)),
        ],
        compiler_params=pltpu.CompilerParams(
            collective_id=cid, has_side_effects=True, vmem_limit_bytes=60 * 1024 * 1024),
        cost_estimate=pl.CostEstimate(flops=rows * cols * 6, bytes_accessed=rows * cols * 12, transcendentals=0),
    )(prior, w)


def ring_copies(axis, me, n, src, slot, sems, base):
    right, left = lax.rem(me + 1, n), lax.rem(me + n - 1, n)
    far = lax.rem(me + 2, n)
    send, recv = sems
    half = src.shape[0] // 2

    def rc(s, d, k, dev):
        return pltpu.make_async_remote_copy(
            src_ref=s, dst_ref=d, send_sem=send.at[base + k], recv_sem=recv.at[base + k],
            device_id={axis: dev}, device_id_type=MESH)

    whole = pl.ds(0, 2 * half)
    lo, hi = pl.ds(0, half), pl.ds(half, half)
    first = [rc(src, slot(me, whole), 0, right), rc(src, slot(me, whole), 1, left)]
    arrive = [rc(src, slot(left, whole), 0, left), rc(src, slot(right, whole), 1, right)]
    relay = [
        rc(slot(right, lo), slot(right, lo), 2, left),
        rc(slot(left, hi), slot(left, hi), 3, right),
    ]
    land = [
        rc(slot(far, lo), slot(far, lo), 2, right),
        rc(slot(far, hi), slot(far, hi), 3, left),
    ]
    return first, arrive, relay, land


def gather_kernel(act_in, grad_in, seq_ref, act_out, grad_out, seq_out, act_ref, grad_ref,
                  send, recv, local, seq_send, seq_recv, p0_send, p0_recv, q0_send, q0_recv):
    nx = 4
    ny = 4
    x = lax.axis_index("x")
    y = lax.axis_index("y")
    zh = lax.axis_index("zh")
    xr, xl = lax.rem(x + 1, nx), lax.rem(x + nx - 1, nx)
    yr, yl = lax.rem(y + 1, ny), lax.rem(y + ny - 1, ny)

    nj = 2 * ny
    j = zh * ny + y
    rw = act_ref.shape[2]
    cw = grad_ref.shape[2]

    def plane(jd):
        return {"zh": jd // ny, "y": lax.rem(jd, ny)}

    barrier = pltpu.get_barrier_semaphore()
    for s in range(1, nj):
        pl.semaphore_signal(barrier, 1, device_id=plane(lax.rem(j + s, nj)), device_id_type=MESH)
    for s in range(1, nx):
        pl.semaphore_signal(barrier, 1, device_id={"x": lax.rem(x + s, nx)}, device_id_type=MESH)
    pl.semaphore_wait(barrier, nj - 1 + nx - 1)

    def act_p0(s, jd, js):
        return pltpu.make_async_remote_copy(
            src_ref=act_in.at[:, pl.ds(pl.multiple_of(jd * rw, 128), rw)], dst_ref=act_ref.at[js],
            send_sem=p0_send.at[s], recv_sem=p0_recv.at[s], device_id=plane(jd),
            device_id_type=MESH)

    def grad_p0(s, xd, xs):
        return pltpu.make_async_remote_copy(
            src_ref=grad_in.at[:, pl.ds(pl.multiple_of(xd * cw, 128), cw)], dst_ref=grad_ref.at[xs],
            send_sem=q0_send.at[s], recv_sem=q0_recv.at[s], device_id={"x": xd},
            device_id_type=MESH)

    p0_out = [act_p0(s, lax.rem(j + s, nj), j) for s in range(1, nj)]
    p0_in = [act_p0(s, j, lax.rem(j + nj - s, nj)) for s in range(1, nj)]
    q0_out = [grad_p0(s, lax.rem(x + s, nx), x) for s in range(1, nx)]
    q0_in = [grad_p0(s, x, lax.rem(x + nx - s, nx)) for s in range(1, nx)]
    own0 = [
        pltpu.make_async_copy(
            act_in.at[:, pl.ds(pl.multiple_of(j * rw, 128), rw)], act_ref.at[j], local.at[3]),
        pltpu.make_async_copy(
            grad_in.at[:, pl.ds(pl.multiple_of(x * cw, 128), cw)], grad_ref.at[x], local.at[4]),
    ]
    for c in own0 + q0_out + p0_out:
        c.start()
    for c in q0_in:
        c.wait_recv()
    own0[1].wait()

    sems = (send, recv)
    a_first, a_arrive, a_relay, a_land = ring_copies(
        "x", x, nx, act_ref, lambda i, p: act_out.at[i, p], sems, 0)
    g_first, g_arrive, g_relay, g_land = ring_copies(
        "y", y, ny, grad_ref, lambda i, p: grad_out.at[p, zh, i], sems, 4)
    p_first, p_arrive, p_relay, p_land = ring_copies(
        "y", y, ny, grad_out.at[:, 1 - zh, y], lambda i, p: grad_out.at[p, 1 - zh, i], sems, 8)
    swap = pltpu.make_async_remote_copy(
        src_ref=grad_ref, dst_ref=grad_out.at[:, zh, y], send_sem=send.at[12],
        recv_sem=recv.at[12], device_id={"zh": 1 - zh}, device_id_type=MESH)
    swap_in = pltpu.make_async_remote_copy(
        src_ref=grad_ref, dst_ref=grad_out.at[:, 1 - zh, y], send_sem=send.at[12],
        recv_sem=recv.at[12], device_id={"zh": 1 - zh}, device_id_type=MESH)

    own = [
        pltpu.make_async_copy(act_ref, act_out.at[x], local.at[0]),
        pltpu.make_async_copy(grad_ref, grad_out.at[:, zh, y], local.at[1]),
        pltpu.make_async_copy(seq_ref, seq_out.at[x], local.at[2]),
    ]

    def sc(s, d, k, dev):
        return pltpu.make_async_remote_copy(
            src_ref=s, dst_ref=d, send_sem=seq_send.at[k], recv_sem=seq_recv.at[k],
            device_id={"x": dev}, device_id_type=MESH)

    seq_first = [sc(seq_ref, seq_out.at[x], 0, xr), sc(seq_ref, seq_out.at[x], 1, xl)]

    swap.start()
    for c in g_first + seq_first + [own[1], own[2]]:
        c.start()
    for c in p0_in:
        c.wait_recv()
    own0[0].wait()
    for c in a_first + [own[0]]:
        c.start()
    swap_in.wait_recv()
    for c in p_first:
        c.start()
    for c in g_arrive:
        c.wait_recv()
    for c in g_relay:
        c.start()
    for c in a_arrive:
        c.wait_recv()
    for c in a_relay:
        c.start()
    for c in p_arrive:
        c.wait_recv()
    for c in p_relay:
        c.start()
    sc(seq_ref, seq_out.at[xl], 0, xl).wait_recv()
    sc(seq_ref, seq_out.at[xr], 1, xr).wait_recv()
    seq_relay = sc(seq_out.at[xr], seq_out.at[xr], 2, xl)
    seq_relay.start()
    for c in a_land + g_land + p_land:
        c.wait_recv()
    sc(seq_out.at[lax.rem(x + 2, nx)], seq_out.at[lax.rem(x + 2, nx)], 2, xr).wait_recv()
    for c in a_first + a_relay + g_first + g_relay + p_first + p_relay + seq_first:
        c.wait_send()
    seq_relay.wait_send()
    swap.wait_send()
    for c in p0_out + q0_out:
        c.wait_send()
    for c in own:
        c.wait()


def gather_all(act, grad, seq, nj, nx, rw, cw):
    tok = act.shape[0]
    any_space = pl.BlockSpec(memory_space=pl.ANY)
    return pl.pallas_call(
        gather_kernel,
        out_shape=(
            jax.ShapeDtypeStruct((nx, nj, tok, rw), act.dtype),
            jax.ShapeDtypeStruct((nx, 2, nj // 2, tok, cw), grad.dtype),
            jax.ShapeDtypeStruct((nx,) + seq.shape, seq.dtype),
            jax.ShapeDtypeStruct((nj, tok, rw), act.dtype),
            jax.ShapeDtypeStruct((nx, tok, cw), grad.dtype),
        ),
        in_specs=[any_space] * 3,
        out_specs=(any_space,) * 5,
        scratch_shapes=[
            pltpu.SemaphoreType.DMA((13,)),
            pltpu.SemaphoreType.DMA((13,)),
            pltpu.SemaphoreType.DMA((5,)),
            pltpu.SemaphoreType.DMA((3,)),
            pltpu.SemaphoreType.DMA((3,)),
            pltpu.SemaphoreType.DMA((nj,)),
            pltpu.SemaphoreType.DMA((nj,)),
            pltpu.SemaphoreType.DMA((nx,)),
            pltpu.SemaphoreType.DMA((nx,)),
        ],
        compiler_params=pltpu.CompilerParams(collective_id=1, has_side_effects=True),
        cost_estimate=pl.CostEstimate(
            flops=0, bytes_accessed=8 * tok * (nj * rw + 2 * nx * cw), transcendentals=0),
    )(act, grad, seq)


def per_device(activations, out_grads, seq_ids, weights):
    nx = lax.axis_size("x")
    nj = lax.axis_size(("zh", "y"))
    tok = activations.shape[1]
    col_width = weights.shape[2]
    row_width = weights.shape[1]
    total = nx * nj * tok
    act_all, grad_all, owners, _, _ = gather_all(
        activations[0], out_grads[0], seq_ids, nj, nx, row_width, col_width)
    act_all = act_all.reshape(total, row_width)
    grad_all = grad_all.reshape(total, col_width)
    first_long = jnp.sum((owners < 1).astype(jnp.int32)) * (total // owners.size) > total // 2

    def part(lo, hi):
        return lax.dot_general(
            act_all[lo:hi], grad_all[lo:hi], (((0,), (0,)), ((), ())),
            preferred_element_type=jnp.float32,
        )

    quarter = total // 4
    head = part(0, quarter)
    mid = part(quarter, 3 * quarter)
    tail = part(3 * quarter, total)
    g0 = jnp.where(first_long, head + mid, head)
    g1 = jnp.where(first_long, tail, mid + tail)
    fisher = g0 * g0 + g1 * g1
    prior = fisher / SEQS + smoothing
    return mp_merge(prior, weights[0], 2)


def solution(mesh):
    assert mesh.shape["mp"] == 4 and mesh.shape["fsdp"] == 32
    fine = jax.sharding.Mesh(
        mesh.devices.reshape(2, 2, 4, 2, 4), ("zl", "c", "x", "zh", "y")
    )
    mp, fs = ("zl", "c"), ("x", "zh", "y")
    placed = (P(mp, fs, None), P(mp, fs, None), P(mp, fs), P(mp, fs, None))
    return jax.shard_map(
        per_device, mesh=fine, in_specs=placed, out_specs=P(fs, None), check_vma=False
    )
```

```python
import functools

import jax
import jax.numpy as jnp
from jax import lax
from jax.experimental import pallas as pl
from jax.experimental.pallas import tpu as pltpu
from jax.sharding import PartitionSpec as P

F = 7168
SEQS = 2
MESH = pl.DeviceIdType.MESH

smoothing = 0.05


def mp_merge_kernel(prior_ref, w_ref, out_ref, recv_p, recv_w, part, recv2,
                    send_sem, recv_sem, s2_send, s2_recv, s3_send, s3_recv, f_send, f_recv,
                    t_send, t_recv):
    c = lax.axis_index("c")
    z = lax.axis_index("zl")
    rows = prior_ref.shape[0]
    half, quarter = rows // 2, rows // 4
    nb = s2_send.shape[0]
    blk = quarter // nb
    step = 32
    core = {"c": 1 - c}
    chip = {"zl": 1 - z}

    barrier = pltpu.get_barrier_semaphore()
    pl.semaphore_signal(barrier, 1, device_id=core, device_id_type=MESH)
    pl.semaphore_signal(barrier, 1, device_id=chip, device_id_type=MESH)
    pl.semaphore_wait(barrier, 2)

    mine = pl.multiple_of(c * half, half)
    other = pl.multiple_of((1 - c) * half, half)
    my_q = pl.multiple_of(z * quarter, quarter)
    far_q = pl.multiple_of((1 - z) * quarter, quarter)

    def onchip(k, q):
        cp = pltpu.make_async_remote_copy(
            src_ref=prior_ref.at[pl.ds(other + q, quarter)], dst_ref=recv_p.at[pl.ds(q, quarter)],
            send_sem=send_sem.at[k], recv_sem=recv_sem.at[k], device_id=core, device_id_type=MESH)
        cw = pltpu.make_async_remote_copy(
            src_ref=w_ref.at[pl.ds(other + q, quarter)], dst_ref=recv_w.at[pl.ds(q, quarter)],
            send_sem=send_sem.at[2 + k], recv_sem=recv_sem.at[2 + k], device_id=core,
            device_id_type=MESH)
        return [cw, cp]

    def onchip_block(b):
        rows_b = pl.ds(far_q + b * blk, blk)
        cp = pltpu.make_async_remote_copy(
            src_ref=prior_ref.at[pl.ds(other + far_q + b * blk, blk)], dst_ref=recv_p.at[rows_b],
            send_sem=f_send.at[b], recv_sem=f_recv.at[b], device_id=core, device_id_type=MESH)
        cw = pltpu.make_async_remote_copy(
            src_ref=w_ref.at[pl.ds(other + far_q + b * blk, blk)], dst_ref=recv_w.at[rows_b],
            send_sem=f_send.at[nb + b], recv_sem=f_recv.at[nb + b], device_id=core,
            device_id_type=MESH)
        return [cw, cp]

    far_in = [onchip_block(b) for b in range(nb)]
    near_in = onchip(1, my_q)
    for pair in far_in:
        for cp in pair:
            cp.start()
    for cp in near_in:
        cp.start()

    def add(lo, count):
        def body(i, carry):
            r = pl.multiple_of(lo + i * step, step)
            p_me = prior_ref[pl.ds(mine + r, step)]
            p_ot = recv_p[pl.ds(r, step)]
            n_me = p_me * w_ref[pl.ds(mine + r, step)].astype(jnp.float32)
            n_ot = p_ot * recv_w[pl.ds(r, step)].astype(jnp.float32)
            part[0, pl.ds(r, step)] = n_ot + n_me
            part[1, pl.ds(r, step)] = p_ot + p_me
            return carry

        lax.fori_loop(0, count // step, body, 0)

    def second(b, lo):
        return pltpu.make_async_remote_copy(
            src_ref=part.at[:, pl.ds(lo + b * blk, blk)], dst_ref=recv2.at[:, pl.ds(b * blk, blk)],
            send_sem=s2_send.at[b], recv_sem=s2_recv.at[b], device_id=chip, device_id_type=MESH)

    def third(b, q):
        rows_b = pl.ds(mine + q + b * blk, blk)
        return pltpu.make_async_remote_copy(
            src_ref=out_ref.at[rows_b], dst_ref=out_ref.at[rows_b],
            send_sem=s3_send.at[b], recv_sem=s3_recv.at[b], device_id=chip, device_id_type=MESH)

    sent2 = []
    for b in range(nb):
        for cp in far_in[b]:
            cp.wait_recv()
        add(far_q + b * blk, blk)
        cp = second(b, far_q)
        cp.start()
        sent2.append(cp)
    for cp in near_in:
        cp.wait_recv()
    add(my_q, quarter)

    def fourth(k, lo):
        rows_k = pl.ds(lo, blk)
        return pltpu.make_async_remote_copy(
            src_ref=out_ref.at[rows_k], dst_ref=out_ref.at[rows_k],
            send_sem=t_send.at[k], recv_sem=t_recv.at[k], device_id=core, device_id_type=MESH)

    sent3 = []
    sent4 = []
    for b in range(nb):
        second(b, my_q).wait_recv()

        def merge(i, carry):
            r = pl.multiple_of(b * blk + i * step, step)
            n = part[0, pl.ds(my_q + r, step)] + recv2[0, pl.ds(r, step)]
            d = part[1, pl.ds(my_q + r, step)] + recv2[1, pl.ds(r, step)]
            out_ref[pl.ds(mine + my_q + r, step)] = (n / d).astype(out_ref.dtype)
            return carry

        lax.fori_loop(0, blk // step, merge, 0)
        cp = third(b, my_q)
        cp.start()
        sent3.append(cp)
        cp = fourth(b, mine + my_q + b * blk)
        cp.start()
        sent4.append(cp)
    for b in range(nb):
        third(b, far_q).wait_recv()
        cp = fourth(nb + b, mine + far_q + b * blk)
        cp.start()
        sent4.append(cp)
    for b in range(nb):
        fourth(b, other + my_q + b * blk).wait_recv()
        fourth(nb + b, other + far_q + b * blk).wait_recv()
    for cp in sum(far_in, []) + near_in + sent2 + sent3 + sent4:
        cp.wait_send()


def mp_merge(prior, w, cid, blocks=8):
    rows, cols = prior.shape
    vmem = pltpu.MemorySpace.VMEM
    return pl.pallas_call(
        mp_merge_kernel,
        out_shape=jax.ShapeDtypeStruct((rows, cols), jnp.bfloat16),
        in_specs=[pl.BlockSpec(memory_space=vmem)] * 2,
        out_specs=pl.BlockSpec(memory_space=vmem),
        scratch_shapes=[
            pltpu.VMEM((rows // 2, cols), jnp.float32),
            pltpu.VMEM((rows // 2, cols), w.dtype),
            pltpu.VMEM((2, rows // 2, cols), jnp.float32),
            pltpu.VMEM((2, rows // 4, cols), jnp.float32),
            pltpu.SemaphoreType.DMA((5,)),
            pltpu.SemaphoreType.DMA((5,)),
            pltpu.SemaphoreType.DMA((blocks,)),
            pltpu.SemaphoreType.DMA((blocks,)),
            pltpu.SemaphoreType.DMA((blocks,)),
            pltpu.SemaphoreType.DMA((blocks,)),
            pltpu.SemaphoreType.DMA((2 * blocks,)),
            pltpu.SemaphoreType.DMA((2 * blocks,)),
            pltpu.SemaphoreType.DMA((2 * blocks,)),
            pltpu.SemaphoreType.DMA((2 * blocks,)),
        ],
        compiler_params=pltpu.CompilerParams(
            collective_id=cid, has_side_effects=True, vmem_limit_bytes=60 * 1024 * 1024),
        cost_estimate=pl.CostEstimate(flops=rows * cols * 6, bytes_accessed=rows * cols * 12, transcendentals=0),
    )(prior, w)


def ring_copies(axis, me, n, src, slot, sems, base):
    right, left = lax.rem(me + 1, n), lax.rem(me + n - 1, n)
    far = lax.rem(me + 2, n)
    send, recv = sems
    half = src.shape[0] // 2

    def rc(s, d, k, dev):
        return pltpu.make_async_remote_copy(
            src_ref=s, dst_ref=d, send_sem=send.at[base + k], recv_sem=recv.at[base + k],
            device_id={axis: dev}, device_id_type=MESH)

    whole = pl.ds(0, 2 * half)
    lo, hi = pl.ds(0, half), pl.ds(half, half)
    first = [rc(src, slot(me, whole), 0, right), rc(src, slot(me, whole), 1, left)]
    arrive = [rc(src, slot(left, whole), 0, left), rc(src, slot(right, whole), 1, right)]
    relay = [
        rc(slot(right, lo), slot(right, lo), 2, left),
        rc(slot(left, hi), slot(left, hi), 3, right),
    ]
    land = [
        rc(slot(far, lo), slot(far, lo), 2, right),
        rc(slot(far, hi), slot(far, hi), 3, left),
    ]
    return first, arrive, relay, land


def gather_kernel(act_in, grad_in, seq_ref, act_out, grad_out, seq_out, act_ref, grad_ref,
                  send, recv, local, seq_send, seq_recv, p0_send, p0_recv, q0_send, q0_recv):
    nx = 4
    ny = 4
    x = lax.axis_index("x")
    y = lax.axis_index("y")
    zh = lax.axis_index("zh")
    xr, xl = lax.rem(x + 1, nx), lax.rem(x + nx - 1, nx)
    yr, yl = lax.rem(y + 1, ny), lax.rem(y + ny - 1, ny)

    nj = 2 * ny
    j = zh * ny + y
    rw = act_ref.shape[2]
    cw = grad_ref.shape[2]

    def plane(jd):
        return {"zh": jd // ny, "y": lax.rem(jd, ny)}

    barrier = pltpu.get_barrier_semaphore()
    for s in range(1, nj):
        pl.semaphore_signal(barrier, 1, device_id=plane(lax.rem(j + s, nj)), device_id_type=MESH)
    for s in range(1, nx):
        pl.semaphore_signal(barrier, 1, device_id={"x": lax.rem(x + s, nx)}, device_id_type=MESH)
    pl.semaphore_wait(barrier, nj - 1 + nx - 1)

    def act_p0(s, jd, js):
        return pltpu.make_async_remote_copy(
            src_ref=act_in.at[:, pl.ds(pl.multiple_of(jd * rw, 128), rw)], dst_ref=act_ref.at[js],
            send_sem=p0_send.at[s], recv_sem=p0_recv.at[s], device_id=plane(jd),
            device_id_type=MESH)

    def grad_p0(s, xd, xs):
        return pltpu.make_async_remote_copy(
            src_ref=grad_in.at[:, pl.ds(pl.multiple_of(xd * cw, 128), cw)], dst_ref=grad_ref.at[xs],
            send_sem=q0_send.at[s], recv_sem=q0_recv.at[s], device_id={"x": xd},
            device_id_type=MESH)

    p0_out = [act_p0(s, lax.rem(j + s, nj), j) for s in range(1, nj)]
    p0_in = [act_p0(s, j, lax.rem(j + nj - s, nj)) for s in range(1, nj)]
    q0_out = [grad_p0(s, lax.rem(x + s, nx), x) for s in range(1, nx)]
    q0_in = [grad_p0(s, x, lax.rem(x + nx - s, nx)) for s in range(1, nx)]
    own0 = [
        pltpu.make_async_copy(
            act_in.at[:, pl.ds(pl.multiple_of(j * rw, 128), rw)], act_ref.at[j], local.at[3]),
        pltpu.make_async_copy(
            grad_in.at[:, pl.ds(pl.multiple_of(x * cw, 128), cw)], grad_ref.at[x], local.at[4]),
    ]
    for c in own0 + p0_out + q0_out:
        c.start()
    for c in q0_in:
        c.wait_recv()
    own0[1].wait()

    sems = (send, recv)
    a_first, a_arrive, a_relay, a_land = ring_copies(
        "x", x, nx, act_ref, lambda i, p: act_out.at[i, p], sems, 0)
    g_first, g_arrive, g_relay, g_land = ring_copies(
        "y", y, ny, grad_ref, lambda i, p: grad_out.at[p, zh, i], sems, 4)
    p_first, p_arrive, p_relay, p_land = ring_copies(
        "y", y, ny, grad_out.at[:, 1 - zh, y], lambda i, p: grad_out.at[p, 1 - zh, i], sems, 8)
    swap = pltpu.make_async_remote_copy(
        src_ref=grad_ref, dst_ref=grad_out.at[:, zh, y], send_sem=send.at[12],
        recv_sem=recv.at[12], device_id={"zh": 1 - zh}, device_id_type=MESH)
    swap_in = pltpu.make_async_remote_copy(
        src_ref=grad_ref, dst_ref=grad_out.at[:, 1 - zh, y], send_sem=send.at[12],
        recv_sem=recv.at[12], device_id={"zh": 1 - zh}, device_id_type=MESH)

    own = [
        pltpu.make_async_copy(act_ref, act_out.at[x], local.at[0]),
        pltpu.make_async_copy(grad_ref, grad_out.at[:, zh, y], local.at[1]),
        pltpu.make_async_copy(seq_ref, seq_out.at[x], local.at[2]),
    ]

    def sc(s, d, k, dev):
        return pltpu.make_async_remote_copy(
            src_ref=s, dst_ref=d, send_sem=seq_send.at[k], recv_sem=seq_recv.at[k],
            device_id={"x": dev}, device_id_type=MESH)

    seq_first = [sc(seq_ref, seq_out.at[x], 0, xr), sc(seq_ref, seq_out.at[x], 1, xl)]

    swap.start()
    for c in g_first + seq_first + [own[1], own[2]]:
        c.start()
    for c in p0_in:
        c.wait_recv()
    own0[0].wait()
    for c in a_first + [own[0]]:
        c.start()
    swap_in.wait_recv()
    for c in p_first:
        c.start()
    for c in g_arrive:
        c.wait_recv()
    for c in g_relay:
        c.start()
    for c in a_arrive:
        c.wait_recv()
    for c in a_relay:
        c.start()
    for c in p_arrive:
        c.wait_recv()
    for c in p_relay:
        c.start()
    sc(seq_ref, seq_out.at[xl], 0, xl).wait_recv()
    sc(seq_ref, seq_out.at[xr], 1, xr).wait_recv()
    seq_relay = sc(seq_out.at[xr], seq_out.at[xr], 2, xl)
    seq_relay.start()
    for c in a_land + g_land + p_land:
        c.wait_recv()
    sc(seq_out.at[lax.rem(x + 2, nx)], seq_out.at[lax.rem(x + 2, nx)], 2, xr).wait_recv()
    for c in a_first + a_relay + g_first + g_relay + p_first + p_relay + seq_first:
        c.wait_send()
    seq_relay.wait_send()
    swap.wait_send()
    for c in p0_out + q0_out:
        c.wait_send()
    for c in own:
        c.wait()


def gather_all(act, grad, seq, nj, nx, rw, cw):
    tok = act.shape[0]
    any_space = pl.BlockSpec(memory_space=pl.ANY)
    return pl.pallas_call(
        gather_kernel,
        out_shape=(
            jax.ShapeDtypeStruct((nx, nj, tok, rw), act.dtype),
            jax.ShapeDtypeStruct((nx, 2, nj // 2, tok, cw), grad.dtype),
            jax.ShapeDtypeStruct((nx,) + seq.shape, seq.dtype),
            jax.ShapeDtypeStruct((nj, tok, rw), act.dtype),
            jax.ShapeDtypeStruct((nx, tok, cw), grad.dtype),
        ),
        in_specs=[any_space] * 3,
        out_specs=(any_space,) * 5,
        scratch_shapes=[
            pltpu.SemaphoreType.DMA((13,)),
            pltpu.SemaphoreType.DMA((13,)),
            pltpu.SemaphoreType.DMA((5,)),
            pltpu.SemaphoreType.DMA((3,)),
            pltpu.SemaphoreType.DMA((3,)),
            pltpu.SemaphoreType.DMA((nj,)),
            pltpu.SemaphoreType.DMA((nj,)),
            pltpu.SemaphoreType.DMA((nx,)),
            pltpu.SemaphoreType.DMA((nx,)),
        ],
        compiler_params=pltpu.CompilerParams(collective_id=1, has_side_effects=True),
        cost_estimate=pl.CostEstimate(
            flops=0, bytes_accessed=8 * tok * (nj * rw + 2 * nx * cw), transcendentals=0),
    )(act, grad, seq)


def per_device(activations, out_grads, seq_ids, weights):
    nx = lax.axis_size("x")
    nj = lax.axis_size(("zh", "y"))
    tok = activations.shape[1]
    col_width = weights.shape[2]
    row_width = weights.shape[1]
    total = nx * nj * tok
    act_all, grad_all, owners, _, _ = gather_all(
        activations[0], out_grads[0], seq_ids, nj, nx, row_width, col_width)
    act_all = act_all.reshape(total, row_width)
    grad_all = grad_all.reshape(total, col_width)
    first_long = jnp.sum((owners < 1).astype(jnp.int32)) * (total // owners.size) > total // 2

    def part(lo, hi):
        return lax.dot_general(
            act_all[lo:hi], grad_all[lo:hi], (((0,), (0,)), ((), ())),
            preferred_element_type=jnp.float32,
        )

    quarter = total // 4
    head = part(0, quarter)
    mid = part(quarter, 3 * quarter)
    tail = part(3 * quarter, total)
    g0 = jnp.where(first_long, head + mid, head)
    g1 = jnp.where(first_long, tail, mid + tail)
    fisher = g0 * g0 + g1 * g1
    prior = fisher / SEQS + smoothing
    return mp_merge(prior, weights[0], 2)


def solution(mesh):
    assert mesh.shape["mp"] == 4 and mesh.shape["fsdp"] == 32
    fine = jax.sharding.Mesh(
        mesh.devices.reshape(2, 2, 4, 2, 4), ("zl", "c", "x", "zh", "y")
    )
    mp, fs = ("zl", "c"), ("x", "zh", "y")
    placed = (P(mp, fs, None), P(mp, fs, None), P(mp, fs), P(mp, fs, None))
    return jax.shard_map(
        per_device, mesh=fine, in_specs=placed, out_specs=P(fs, None), check_vma=False
    )
```
